128 devices in a mesh: row: 16 (over x, z), seq: 8 (over y, core).
Axes of the slice: x: 4, y: 4, z: 4, core: 2. Of those that a mesh axis runs over, the one named last changes fastest.
Arguments:
- inputs: bfloat16 [64, 1024, 768], P('row', 'seq'), may hold values from -6 to 6
- segment_ids: int32 [64, 1024], P('row', 'seq'), may hold values from 0 to 3, never falling along the last dimension, each value on 1 to 512 neighbouring positions
- out_grad: bfloat16 [64, 1024, 768], P('row', 'seq'), may hold values from -6 to 6
- params: float32 [768, 9344], P(('row', 'seq'))
- vectors: float32 [13, 768], P(None, ('row', 'seq'))
- params_m: float32 [768, 9344], P(('row', 'seq')), may hold values from -0.0022382177 to 0.0022382177
- params_v: float32 [768, 9344], P(('row', 'seq')), may hold values from 1.3915607e-07 to 5.566243e-07
- vectors_m: float32 [13, 768], P(None, ('row', 'seq')), may hold values from -0.0044764355 to 0.0044764355
- vectors_v: float32 [13, 768], P(None, ('row', 'seq')), may hold values from 5.566243e-07 to 2.2264971e-06
Outputs:
- block_out: bfloat16 [64, 1024, 768], P('row', 'seq')
- input_grad: float32 [64, 1024, 768], P('row', 'seq')
- grad_norm: float32 [1], replicated
- params_grad: float32 [768, 9344], P(('row', 'seq'))
- params_new: float32 [768, 9344], P(('row', 'seq'))
- params_m_new: float32 [768, 9344], P(('row', 'seq'))
- params_v_new: float32 [768, 9344], P(('row', 'seq'))
- vectors_grad: float32 [13, 768], P(None, ('row', 'seq'))
- vectors_new: float32 [13, 768], P(None, ('row', 'seq'))
- vectors_m_new: float32 [13, 768], P(None, ('row', 'seq'))
- vectors_v_new: float32 [13, 768], P(None, ('row', 'seq'))
The draws below stay inside these ranges and needn't reach their ends.
Inputs may be any that keep to these rules, and one draw needn't show every extreme that they name: `segment_ids`: in each row the segment ids never fall from one position to the next; a segment holds 1 to 512 positions, and some segment holds exactly 512.
All inputs are finite; a program needn't handle non-finite values.
Results may differ from the reference program's by a relative error of at most 0.012.
The reference program's roundings to bfloat16 on the way count: a program that leaves them out, or rounds other values in their place, can miss the bound.
Values may be sent and summed in bfloat16 or wider, within the bound.
A program may use at most 256 MiB of HBM per device.

```python
import math
import jax
import jax.numpy as jnp
import numpy as np
from jax import lax

D = 768
HEADS = 12
HEAD = 64
FF = 3072
LEN = 1024
ROWS = 64
PCOLS = 9344


def draw_params(key, part):
    columns = 4 * D + 2 * HEAD + 2 * FF
    noise = jax.random.normal(key, (D, columns), jnp.float32)
    column = jnp.arange(columns)
    factor = jnp.where(column < 3 * D, D ** (-0.5), jnp.where(column < 4 * D, 8.0 * D ** (-0.5), jnp.where(column < 4 * D + 2 * HEAD, 0.25, jnp.where(column < 4 * D + 2 * HEAD + FF, D ** (-0.5), FF ** (-0.5)))))
    return noise * factor


def draw_vectors(key, part):
    noise = jax.random.normal(key, (13, D), jnp.float32)
    rowsel = jnp.arange(13)
    gains = ((rowsel == 0) | (rowsel == 2)).astype(jnp.float32)
    return gains[:, None] + 0.2 * noise


def levels(key, dims, shards, low, high):
    loudness, own = 1.0, jax.random.fold_in(key, 6)
    for axis_at, blocks in shards:
        draws = jnp.exp(jax.random.uniform(jax.random.fold_in(own, axis_at), (blocks,), jnp.float32, low / len(shards), high / len(shards)))
        loudness = loudness * jnp.repeat(draws, dims[axis_at] // blocks).reshape([-1 if axis == axis_at else 1 for axis in range(len(dims))])
    return loudness


def split_up(amount, total, reach, lean):
    portions = [(1 << 20) // math.isqrt(standing ** lean) + 1 for standing in range(2, amount + 1)]
    rest, given = total - reach - (amount - 1), [1] * (amount - 1)
    while rest > 0:
        free = [i for i in range(amount - 1) if given[i] < reach]
        whole, left = sum([portions[i] for i in free]), rest
        for i in free:
            more = min(reach - given[i], max(1, left * portions[i] // whole), rest)
            given[i] = given[i] + more
            rest = rest - more
    return np.array([reach] + given)


def uneven_parts(stream_key, count, total, limit, lean):
    if count == 2:
        one = jax.random.randint(stream_key, (), max(1, total - limit), min(limit, total - 1) + 1)
        return jnp.stack([one, total - one])
    tallies = jnp.asarray(split_up(count, total, limit, lean), jnp.int32)
    pairs = (count - 1) // 2
    giver, receiver = tallies[1:1 + 2 * pairs:2], tallies[2:2 + 2 * pairs:2]
    margin = jnp.minimum(giver - 1, limit - receiver)
    moved = jax.random.randint(jax.random.fold_in(stream_key, 1), (pairs,), 0, 1 << 20) % (margin + 1)
    tallies = tallies.at[1:1 + 2 * pairs:2].set(giver - moved).at[2:2 + 2 * pairs:2].set(receiver + moved)
    return tallies[jax.random.permutation(jax.random.fold_in(stream_key, 2), count)]


def scatter_about(own_key, shape, scale, reach, cuts=(), kind=jnp.bfloat16):
    factor_of = levels(own_key, shape, cuts, -0.22, 0.18) if cuts else 1.0
    drawn = jax.random.normal(own_key, shape, jnp.float32) * scale * factor_of
    return jnp.minimum(jnp.maximum(drawn, -reach), reach).astype(kind)


def setup_inputs(seed: int = 0) -> dict:
    splits = jax.random.split(jax.random.key(seed), 10)
    return {
        "inputs": scatter_about(splits[0], (ROWS, LEN, D), 1.0, 6.0, ((0, 16), (1, 8))),
        "segment_ids": jax.vmap(lambda own: jnp.searchsorted(jnp.cumsum(uneven_parts(own, 4, LEN, LEN // 2, 0)), jnp.arange(LEN), side="right"))(jax.random.split(splits[1], ROWS)).reshape((ROWS, LEN)).astype(jnp.int32),
        "out_grad": scatter_about(splits[2], (ROWS, LEN, D), 1.0, 6.0, ((0, 16), (1, 8))),
        "params": draw_params(jax.random.fold_in(splits[9], 71), 0),
        "vectors": draw_vectors(jax.random.fold_in(splits[9], 71), 0),
        "params_m": scatter_about(splits[5], (D, PCOLS), (1.0 / (D * PCOLS + 13 * D) ** 0.5), 0.0022382177, ((0, 128),), jnp.float32),
        "params_v": jnp.clip(jnp.exp(math.log(5.56624286218721e-07) - 1.3862944 * jax.random.uniform(splits[6], (D, PCOLS), jnp.float32) ** levels(splits[6], (D, PCOLS), ((0, 128),), -0.2, 0.2)), 1.3915607155468024e-07, 5.56624286218721e-07),
        "vectors_m": scatter_about(splits[7], (13, D), (2.0 / (D * PCOLS + 13 * D) ** 0.5), 0.0044764355, ((1, 128),), jnp.float32),
        "vectors_v": jnp.clip(jnp.exp(math.log(2.226497144874884e-06) - 1.3862944 * jax.random.uniform(splits[8], (13, D), jnp.float32) ** levels(splits[8], (13, D), ((1, 128),), -0.2, 0.2)), 5.56624286218721e-07, 2.226497144874884e-06),
    }


highest = lax.Precision.HIGHEST
clip_norm = 1.0
beta_one = 0.5
beta_two = 0.5
adam_eps = 1e-08

@jax.custom_vjp
def low(v):
    return lax.optimization_barrier(v.astype(jnp.bfloat16)).astype(jnp.float32)

@jax.custom_vjp
def low_back(v):
    return v

def low_keep(v):
    return (low(v), None)

def low_pass(kept, grad):
    return (grad,)

def back_keep(v):
    return (v, None)

def back_low(kept, grad):
    return (low(grad),)
low.defvjp(low_keep, low_pass)
low_back.defvjp(back_keep, back_low)

def layer_norm(values, gain, shift):
    center = values - lax.optimization_barrier(jnp.mean(values, -1, keepdims=True))
    spread = lax.optimization_barrier(jnp.mean(center * center, -1, keepdims=True))
    return center * lax.rsqrt(spread + 1e-05) * gain + shift

def features(logits):
    return jnp.concatenate([jax.nn.softmax(logits, -1), jax.nn.softmax(-logits, -1)], -1)

def row_layer(tokens, segments, weights, vector_all):
    length = tokens.shape[0]
    col_feat = 4 * D
    col_up = col_feat + 2 * HEAD
    col_down = col_up + FF
    normed = low(layer_norm(tokens, vector_all[0], vector_all[1]))
    project = low(low_back(jnp.dot(normed, weights[:, :3 * D], precision=highest) + vector_all[4:7].reshape(-1)))
    queries = project[:, :D].reshape(length, HEADS, HEAD)
    key_rows = project[:, D:2 * D].reshape(length, HEADS, HEAD)
    value_rows = project[:, 2 * D:3 * D].reshape(length, HEADS, HEAD)
    query_map = weights[:, col_feat:col_feat + HEAD].reshape(HEADS, HEAD, HEAD)
    key_map = weights[:, col_feat + HEAD:col_up].reshape(HEADS, HEAD, HEAD)
    query_feat = features(low_back(jnp.einsum('the,hef->thf', queries, query_map, precision=highest)))
    key_feat = features(low_back(jnp.einsum('the,hef->thf', key_rows, key_map, precision=highest)))
    places = jnp.arange(length)
    allowed = (places[None, :] <= places[:, None]) & (segments[:, None] == segments[None, :])
    scores = jnp.einsum('thf,shf->hts', query_feat, key_feat, precision=highest) * allowed[None].astype(jnp.float32)
    numerator = jnp.einsum('hts,she->the', scores, value_rows, precision=highest)
    denominator = jnp.transpose(lax.optimization_barrier(jnp.sum(scores, -1)))
    mixed_heads = low((numerator / denominator[:, :, None]).reshape(length, D))
    attend = low_back(jnp.dot(mixed_heads, weights[:, 3 * D:4 * D], precision=highest) + vector_all[7])
    middle = tokens + attend
    normed_two = low(layer_norm(middle, vector_all[2], vector_all[3]))
    hidden = low_back(jnp.dot(normed_two, weights[:, col_up:col_down], precision=highest) + vector_all[8:12].reshape(-1))
    active = low(jax.nn.gelu(hidden, approximate=True))
    return middle + jnp.dot(active, jnp.transpose(weights[:, col_down:]), precision=highest) + vector_all[12]

def adamw_step(weight, gradient, moment_one, moment_two, clip_scale, step_rate, decay_rate):
    gradient = gradient * clip_scale
    moment_one = beta_one * moment_one + (1.0 - beta_one) * gradient
    moment_two = beta_two * moment_two + (1.0 - beta_two) * gradient * gradient
    weight = weight - step_rate * (moment_one / (jnp.sqrt(moment_two) + adam_eps) + decay_rate * weight)
    return (gradient, weight, moment_one, moment_two)

def reference(inputs, segment_ids, out_grad, params, vectors, params_m, params_v, vectors_m, vectors_v):

    def forward(tokens, weights, vector_all):
        weights = low(weights)
        vector_all = low(vector_all)
        layer_rows = jax.checkpoint(row_layer)
        return lax.map(lambda row_pair: layer_rows(row_pair[0], row_pair[1], weights, vector_all), (tokens, segment_ids))
    outputs, pullback = jax.vjp(forward, inputs.astype(jnp.float32), params, vectors)
    input_grad, params_full, vectors_full = pullback(out_grad.astype(jnp.float32))
    squares = jnp.sum(params_full * params_full) + jnp.sum(vectors_full * vectors_full)
    grad_norm = jnp.sqrt(squares)
    clip_scale = clip_norm / jnp.maximum(grad_norm, clip_norm)
    params_grad, params_new, params_m_new, params_v_new = adamw_step(params, params_full, params_m, params_v, clip_scale, 0.05, 0.1)
    vectors_grad, vectors_new, vectors_m_new, vectors_v_new = adamw_step(vectors, vectors_full, vectors_m, vectors_v, clip_scale, 0.2, 0.0)
    return (outputs.astype(jnp.bfloat16), input_grad, grad_norm.reshape(1), params_grad, params_new, params_m_new, params_v_new, vectors_grad, vectors_new, vectors_m_new, vectors_v_new)
```

```python
import jax
import jax.numpy as jnp
from jax import lax
from jax.experimental import pallas as pl
from jax.experimental.pallas import tpu as pltpu
from jax.sharding import Mesh
from jax.sharding import PartitionSpec as P


D=768
WC=4864
G1=1792
PIECES=((0,384,0,384),(384,384,768,384),(768,384,1536,384),(1152,384,2304,384),(1536,128,3072,0),
        (1792,1536,3200,1536),(3328,1536,6272,1536))
COLS=(((0,384,896),(896,1280,1792)),((1792,2560,3328),(3328,4096,4864)))
MESH=pl.DeviceIdType.MESH

def ids():
    return lax.axis_index("x"),lax.axis_index("z"),lax.axis_index("y"),lax.axis_index("c")

def slab(xx,zz):
    return pl.multiple_of((lax.rem(xx+8,4)*4+lax.rem(zz+8,4))*48,16)

def seq_peer(s,k):
    t=lax.rem(s+k+8,8)
    return t, {"y":t//2,"c":lax.rem(t,2)}

def greet(sem, x, z, s):
    for k in range(1,8):
        pl.semaphore_signal(sem,inc=1,device_id=seq_peer(s,k)[1],device_id_type=MESH)
    for d in (1,3):
        pl.semaphore_signal(sem,inc=1,device_id={"x":lax.rem(x+d,4)},device_id_type=MESH)
        pl.semaphore_signal(sem,inc=1,device_id={"z":lax.rem(z+d,4)},device_id_type=MESH)

def k1(par,vec,xin,dyin,sgin,w,wo,xrow,dyrow,sg,wire,rcv,s0s,s0r,ags,agr,rss,rsr,wos,wor,sgs,sgr):
    x,z,y,c=ids()
    s=y*2+c
    bar=pltpu.get_barrier_semaphore()
    greet(bar,x,z,s)
    for cc in range(2):
        wire[cc,:,:]=jnp.zeros((8,WC),jnp.bfloat16)
        for d,wd,sr,st in PIECES:
            wire[cc,0:6,d:d+wd]=par[:,sr+st*cc:sr+st*cc+wd].astype(jnp.bfloat16)
        wire[cc,0:6,1664:1792]=vec[...].astype(jnp.bfloat16)
    pl.semaphore_wait(bar,11)
    GC=((0,G1),(G1,WC))
    def st0(g,k,recv):
        t,dev=seq_peer(s,k)
        src,_=seq_peer(s,-k)
        a,b=GC[g]
        slot=src if recv else s
        return pltpu.make_async_remote_copy(wire.at[dev["c"],:,a:b],rcv.at[slot,:,a:b],s0s.at[g,k],s0r.at[g,k],device_id=dev,device_id_type=MESH)
    def res(which,k,recv):
        src_ref,dst_ref=((xin,xrow),(dyin,dyrow))[which]
        j=lax.rem(y+k,4)
        slot=(lax.rem(y-k+4,4)*2+c) if recv else s
        return pltpu.make_async_remote_copy(src_ref.at[j],dst_ref.at[pl.ds(pl.multiple_of(slot*128,128),128)],rss.at[which,k],rsr.at[which,k],device_id={"y":j},device_id_type=MESH)
    def own(which):
        src_ref,dst_ref=((xin,xrow),(dyin,dyrow))[which]
        return pltpu.make_async_copy(src_ref.at[y],dst_ref.at[pl.ds(pl.multiple_of(s*128,128),128)],rss.at[which,0])
    def sib(which,k,recv):
        dst_ref=(xrow,dyrow)[which]
        cc=(1-c) if recv else c
        slot=lax.rem(y-k+4,4)*2+cc
        ref=dst_ref.at[pl.ds(pl.multiple_of(slot*128,128),128)]
        return pltpu.make_async_remote_copy(ref,ref,rss.at[which,4+k],rsr.at[which,4+k],device_id={"c":1-c},device_id_type=MESH)
    def sgc(k,recv):
        t,dev=seq_peer(s,k)
        src,_=seq_peer(s,-k)
        slot=src if recv else s
        return pltpu.make_async_remote_copy(sgin.at[t//2],sg.at[slot],sgs.at[k],sgr.at[k],device_id=dev,device_id_type=MESH)
    for k in range(1,8): st0(0,k,False).start()
    for k in range(1,8): sgc(k,False).start()
    sg[s]=sgin[y]
    own(0).start()
    for k in range(1,4): res(0,k,False).start()
    for k in range(1,8): st0(1,k,False).start()
    own(1).start()
    for k in range(1,4): res(1,k,False).start()
    rcv[s]=wire[c]
    rr=lax.broadcasted_iota(jnp.int32,(48,64),0); cc_=lax.broadcasted_iota(jnp.int32,(48,64),1)
    P=((lax.rem(rr,6)==lax.rem(cc_,8))&(rr//6==cc_//8)).astype(jnp.bfloat16)
    rows0=slab(x,z)
    def assemble(g):
        a,b=GC[g]
        for lo in range(a,b,896 if g==0 else 768):
            hi=lo+(896 if g==0 else 768)
            X=jnp.concatenate([rcv[t,:,lo:hi].astype(jnp.float32) for t in range(8)],axis=0).astype(jnp.bfloat16)
            w[pl.ds(rows0,48),lo:hi]=jnp.dot(P,X,preferred_element_type=jnp.float32).astype(jnp.bfloat16)
    def pos(part,d1,d2):
        return slab(x+d1,z+d2) if part==0 else slab(x+d2,z+d1)
    def cp(g,part,sem,d1,d2,half,phase,dirn):
        lo,mid,hi=COLS[g][part]
        ca,cb={0:(lo,hi),1:(lo,mid),2:(mid,hi)}[half]
        ref=w.at[pl.ds(pos(part,d1,d2),48),ca:cb]
        ax=("x","z")[(part+phase)%2]
        me=(x,z)[(part+phase)%2]
        return pltpu.make_async_remote_copy(ref,ref,ags.at[g,part,sem],agr.at[g,part,sem],device_id={ax:lax.rem(me+dirn+4,4)},device_id_type=MESH)
    D1=(0,-1,1,2)
    def p2send(g,p,q):
        cp(g,p,4+4*q,D1[q],0,0,1,1).start(); cp(g,p,5+4*q,D1[q],0,0,1,-1).start()
    def p2fwd(g,p,q):
        cp(g,p,4+4*q,D1[q],-1,0,1,1).wait_recv(); cp(g,p,6+4*q,D1[q],-1,1,1,1).start()
        cp(g,p,5+4*q,D1[q],1,0,1,-1).wait_recv(); cp(g,p,7+4*q,D1[q],1,2,1,-1).start()
    def ag_a(g):
        for p in range(2):
            cp(g,p,0,0,0,0,0,1).start(); cp(g,p,1,0,0,0,0,-1).start()
        for p in range(2): p2send(g,p,0)
    def ag_b(g):
        for p in range(2):
            cp(g,p,0,-1,0,0,0,1).wait_recv(); cp(g,p,2,-1,0,1,0,1).start()
            cp(g,p,1,1,0,0,0,-1).wait_recv(); cp(g,p,3,1,0,2,0,-1).start()
            p2send(g,p,1); p2send(g,p,2)
    def ag_c(g):
        for p in range(2): p2fwd(g,p,0)
        for p in range(2):
            cp(g,p,2,2,0,1,0,1).wait_recv(); cp(g,p,3,2,0,2,0,-1).wait_recv()
            p2send(g,p,3)
        for p in range(2): p2fwd(g,p,1); p2fwd(g,p,2)
    def ag_d(g):
        for p in range(2): p2fwd(g,p,3)
        for p in range(2):
            for q in range(4):
                cp(g,p,6+4*q,D1[q],2,1,1,1).wait_recv(); cp(g,p,7+4*q,D1[q],2,2,1,-1).wait_recv()
    def ag_sends(g):
        for p in range(2):
            cp(g,p,0,0,0,0,0,1).wait_send(); cp(g,p,1,0,0,0,0,-1).wait_send()
            cp(g,p,2,-1,0,1,0,1).wait_send(); cp(g,p,3,1,0,2,0,-1).wait_send()
            for q in range(4):
                cp(g,p,4+4*q,D1[q],0,0,1,1).wait_send(); cp(g,p,5+4*q,D1[q],0,0,1,-1).wait_send()
                cp(g,p,6+4*q,D1[q],-1,1,1,1).wait_send(); cp(g,p,7+4*q,D1[q],1,2,1,-1).wait_send()
    for k in range(1,8): st0(0,k,True).wait_recv()
    assemble(0)
    ag_a(0)
    for wh in range(2):
        if wh==1:
            for k in range(1,8): st0(1,k,True).wait_recv()
            assemble(1)
            ag_a(1)
            ag_b(0)
        own(wh).wait(); sib(wh,0,False).start()
        for k in range(1,4):
            res(wh,k,True).wait_recv(); sib(wh,k,False).start()
    ag_c(0)
    ag_b(1)
    ag_d(0)
    half=pl.ds(pl.multiple_of(c*384,128),384)
    wo_cp=pltpu.make_async_remote_copy(w.at[:,1152:1536],wo.at[:,half],wos,wor,device_id={"c":1-c},device_id_type=MESH)
    wo_cp.start()
    wo[:,half]=w[:,1152:1536]
    ag_c(1)
    ag_d(1)
    ohalf=pl.ds(pl.multiple_of((1-c)*384,128),384)
    pltpu.make_async_remote_copy(w.at[:,1152:1536],wo.at[:,ohalf],wos,wor,device_id={"c":1-c},device_id_type=MESH).wait_recv()
    wo_cp.wait_send()
    for g in range(2):
        for k in range(1,8): st0(g,k,False).wait_send()
        ag_sends(g)
    for k in range(1,8):
        sgc(k,True).wait_recv(); sgc(k,False).wait_send()
    for wh in range(2):
        for k in range(1,4): res(wh,k,False).wait_send()
        for k in range(4):
            sib(wh,k,True).wait_recv(); sib(wh,k,False).wait_send()

def call_k1(par,vec,xin,dyin,sgin):
    V=pl.BlockSpec(memory_space=pltpu.VMEM)
    bf=jnp.bfloat16
    return pl.pallas_call(k1,
      out_shape=[jax.ShapeDtypeStruct((D,WC),bf),jax.ShapeDtypeStruct((D,D),bf),jax.ShapeDtypeStruct((1024,D),bf),jax.ShapeDtypeStruct((1024,D),bf),jax.ShapeDtypeStruct((8,8,128),jnp.float32)],
      in_specs=[V]*5,out_specs=[V]*5,
      scratch_shapes=[pltpu.VMEM((2,8,WC),bf),pltpu.VMEM((8,8,WC),bf),
        pltpu.SemaphoreType.DMA((2,8)),pltpu.SemaphoreType.DMA((2,8)),
        pltpu.SemaphoreType.DMA((2,2,20)),pltpu.SemaphoreType.DMA((2,2,20)),
        pltpu.SemaphoreType.DMA((2,8)),pltpu.SemaphoreType.DMA((2,8)),
        pltpu.SemaphoreType.DMA,pltpu.SemaphoreType.DMA,pltpu.SemaphoreType.DMA((8,)),pltpu.SemaphoreType.DMA((8,))],
      compiler_params=pltpu.CompilerParams(collective_id=0,has_side_effects=True,vmem_limit_bytes=48*2**20),
      name="gather")(par,vec,xin,dyin,sgin)

def greet_all(sem,x,z,s):
    for k in range(1,8):
        pl.semaphore_signal(sem,inc=1,device_id=seq_peer(s,k)[1],device_id_type=MESH)
    for k in range(1,16):
        t=lax.rem(x*4+z+k,16)
        pl.semaphore_signal(sem,inc=1,device_id={"x":t//4,"z":lax.rem(t,4)},device_id_type=MESH)

D1=(0,-1,1,2)
def k3(gin,bo,ig,par,pm,pv,vec,vm,vv,
       out_o,ig_o,norm_o,pg_o,pn_o,pmn_o,pvn_o,vg_o,vn_o,vmn_o,vvn_o,
       g,r1,r2,ys,yr,tr,n1,n2,
       s1s,s1r,s2s,s2r,yss,ysr,n1s,n1r,n2s,n2r,tks,tkr,igb):
    x,z,y,c=ids()
    s=y*2+c
    bar=pltpu.get_barrier_semaphore()
    greet_all(bar,x,z,s)
    g[...]=gin[...]
    pl.semaphore_wait(bar,22)
    toks=((bo,out_o),(ig,igb))
    def tok(w,k,recv):
        src,dst=toks[w]
        t,dev=seq_peer(s,k)
        q,_=seq_peer(s,-k)
        i=lax.rem(t,4)
        row=(q//2) if recv else y
        return pltpu.make_async_remote_copy(src.at[pl.ds(pl.multiple_of(i*128,128),128)],dst.at[row],tks.at[w,k],tkr.at[w,k],device_id=dev,device_id_type=MESH)
    def tok_start(w):
        for k in range(1,8):
            t,_=seq_peer(s,k)
            @pl.when(t//4==c)
            def _(): tok(w,k,False).start()
        src,dst=toks[w]
        @pl.when(s//4==c)
        def _():
            dst[y]=src[pl.ds(pl.multiple_of(lax.rem(s,4)*128,128),128)]
    def tok_wait(w):
        for k in range(1,8):
            q,_=seq_peer(s,-k)
            @pl.when(lax.rem(q,2)==s//4)
            def _(): tok(w,k,True).wait_recv()
        for k in range(1,8):
            t,_=seq_peer(s,k)
            @pl.when(t//4==c)
            def _(): tok(w,k,False).wait_send()
    def pos(part,d1,d2):
        return slab(x+d1,z+d2) if part==0 else slab(x+d2,z+d1)
    def rng(gp,p,h):
        lo,mid,hi=COLS[gp][p]
        return {0:(lo,hi),1:(lo,mid),2:(mid,hi)}[h]
    def gref(gp,p,d1,d2,h):
        a,b=rng(gp,p,h)
        return g.at[pl.ds(pos(p,d1,d2),48),a:b]
    def dev(p,phase,dirn):
        k=(p+phase)%2
        me=(x,z)[k]
        return {("x","z")[k]:lax.rem(me+dirn+4,4)}
    def c1(gp,p,q,kind,recv=False):
        h=(1,2,0,0)[kind]; slot=(0,0,1,2)[kind]; dirn=(1,-1,1,-1)[kind]
        e=(2,2,1,-1)[kind]
        a,b=rng(gp,p,h)
        return pltpu.make_async_remote_copy(gref(gp,p,D1[q],e,h),r1.at[q,slot,:,a:b],s1s.at[gp,p,q,kind],s1r.at[gp,p,q,kind],device_id=dev(p,1,dirn),device_id_type=MESH)
    def c2(gp,p,kind):
        h=(1,2,0,0)[kind]; slot=(0,0,1,2)[kind]; dirn=(1,-1,1,-1)[kind]
        d=(2,2,1,-1)[kind]
        a,b=rng(gp,p,h)
        return pltpu.make_async_remote_copy(gref(gp,p,d,0,h),r2.at[slot,:,a:b],s2s.at[gp,p,kind],s2r.at[gp,p,kind],device_id=dev(p,0,dirn),device_id_type=MESH)
    f32=jnp.float32
    def acc(dst,*srcs):
        t=dst[...].astype(f32)
        for r in srcs: t=t+r[...].astype(f32)
        dst[...]=t.astype(jnp.bfloat16)
    def r1_start(gp,p,q):
        c1(gp,p,q,0).start(); c1(gp,p,q,1).start()
    def r1_mid(gp,p,q):
        for kind,e in ((0,1),(1,-1)):
            c1(gp,p,q,kind).wait_recv()
            h=(1,2)[kind]; a,b=rng(gp,p,h)
            acc(gref(gp,p,D1[q],e,h),r1.at[q,0,:,a:b])
            c1(gp,p,q,2+kind).start()
    def r1_end(gp,p,q):
        a,b=rng(gp,p,0)
        c1(gp,p,q,2).wait_recv(); c1(gp,p,q,3).wait_recv()
        acc(gref(gp,p,D1[q],0,0),r1.at[q,1,:,a:b],r1.at[q,2,:,a:b])
    def r2_start(gp,p):
        c2(gp,p,0).start(); c2(gp,p,1).start()
    def r2_mid(gp,p):
        for kind,d in ((0,1),(1,-1)):
            c2(gp,p,kind).wait_recv()
            h=(1,2)[kind]; a,b=rng(gp,p,h)
            acc(gref(gp,p,d,0,h),r2.at[0,:,a:b])
            c2(gp,p,2+kind).start()
    def r2_end(gp,p):
        a,b=rng(gp,p,0)
        c2(gp,p,2).wait_recv(); c2(gp,p,3).wait_recv()
        acc(gref(gp,p,0,0,0),r2.at[1,:,a:b],r2.at[2,:,a:b])
    GC=((0,G1),(G1,WC))
    rr=lax.broadcasted_iota(jnp.int32,(64,48),0); cc_=lax.broadcasted_iota(jnp.int32,(64,48),1)
    PT=((lax.rem(cc_,6)==lax.rem(rr,8))&(cc_//6==rr//8)).astype(jnp.bfloat16)
    def ycp(gp,k,recv):
        t,dv=seq_peer(s,k); q,_=seq_peer(s,-k)
        a,b=GC[gp]
        slot=q if recv else s
        return pltpu.make_async_remote_copy(ys.at[t,:,a:b],yr.at[slot,:,a:b],yss.at[gp,k],ysr.at[gp,k],device_id=dv,device_id_type=MESH)
    def y_start(gp):
        a,b=GC[gp]
        st=896 if gp==0 else 768
        for lo in range(a,b,st):
            hi=lo+st
            R=g[pl.ds(slab(x,z),48),lo:hi]
            Y=jnp.dot(PT,R,preferred_element_type=f32).astype(jnp.bfloat16)
            for t in range(8): ys[t,:,lo:hi]=Y[8*t:8*t+8]
        for k in range(1,8): ycp(gp,k,False).start()
        yr[s,:,a:b]=ys[s,:,a:b]
    def y_wait(gp):
        for k in range(1,8): ycp(gp,k,True).wait_recv()
    tok_start(0)
    for gp in (1,0):
        for q in (3,1,2,0):
            for p in range(2): r1_start(gp,p,q)
    tok_start(1)
    for gp in (1,0):
        for q in (3,1,2,0):
            for p in range(2): r1_mid(gp,p,q)
        for p in range(2): r1_end(gp,p,3); r2_start(gp,p)
        for p in range(2): r1_end(gp,p,1); r1_end(gp,p,2); r2_mid(gp,p)
        for p in range(2): r1_end(gp,p,0)
        for p in range(2): r2_end(gp,p)
        y_start(gp)
    total=jnp.zeros((1,1),f32)
    for gp in (1,0):
        y_wait(gp)
        for d,wd,sr,st in PIECES:
            if (d>=G1)!=(gp==1): continue
            for cc in range(2 if st else 1):
                if st: v=sum(yr[2*j+cc,0:6,d:d+wd].astype(f32) for j in range(4))
                else: v=sum(yr[j,0:6,d:d+wd].astype(f32) for j in range(8))
                pg_o[:,sr+st*cc:sr+st*cc+wd]=v
                total=total+jnp.sum(jnp.sum(v*v,axis=1,keepdims=True),axis=0,keepdims=True)
    V=sum(yr[j,:,1664:1792].astype(f32) for j in range(8))
    total=total+jnp.sum(jnp.sum(V[0:6]*V[0:6],axis=1,keepdims=True),axis=0,keepdims=True)
    tr[...]=jnp.zeros((128,128),f32)
    tr[0:8,:]=V
    VT=jnp.transpose(tr[...])[0:13,0:6]
    mine=jnp.broadcast_to(total,(8,128))
    n1[s]=mine
    def nc1(k,recv):
        t,dv=seq_peer(s,k); q,_=seq_peer(s,-k)
        slot=q if recv else s
        return pltpu.make_async_remote_copy(n1.at[s],n1.at[slot],n1s.at[k],n1r.at[k],device_id=dv,device_id_type=MESH)
    for k in range(1,8): nc1(k,False).start()
    for k in range(1,8): nc1(k,True).wait_recv()
    pln=x*4+z
    n2[pln]=sum(n1[j] for j in range(8))
    def nc2(k,recv):
        t=lax.rem(pln+k,16); q=lax.rem(pln-k+16,16)
        slot=q if recv else pln
        return pltpu.make_async_remote_copy(n2.at[pln],n2.at[slot],n2s.at[k],n2r.at[k],device_id={"x":t//4,"z":lax.rem(t,4)},device_id_type=MESH)
    for k in range(1,16): nc2(k,False).start()
    tok_wait(0); tok_wait(1)
    ig_o[...]=igb[...].astype(f32)
    for k in range(1,16): nc2(k,True).wait_recv()
    sq=sum(n2[j] for j in range(16))
    nrm=jnp.sqrt(sq)[0:1,0:1]
    norm_o[...]=nrm
    cl=1.0/jnp.maximum(nrm,1.0)
    def adam(w,gr,m,v,rate,decay):
        gr=gr*cl
        m=0.5*m+0.5*gr
        v=0.5*v+0.5*gr*gr
        return gr, w-rate*(m/(jnp.sqrt(v)+1e-8)+decay*w), m, v
    for lo in range(0,9344,1168*8//8):
        break
    for lo in range(0,73,8):
        a,b=lo*128,min(lo+8,73)*128
        gr,w,m,v=adam(par[:,a:b],pg_o[:,a:b],pm[:,a:b],pv[:,a:b],0.05,0.1)
        pg_o[:,a:b]=gr; pn_o[:,a:b]=w; pmn_o[:,a:b]=m; pvn_o[:,a:b]=v
    gr,w,m,v=adam(vec[...],VT,vm[...],vv[...],0.2,0.0)
    vg_o[...]=gr; vn_o[...]=w; vmn_o[...]=m; vvn_o[...]=v
    for gp in range(2):
        for p in range(2):
            for kind in range(4):
                c2(gp,p,kind).wait_send()
                for q in range(4): c1(gp,p,q,kind).wait_send()
        for k in range(1,8): ycp(gp,k,False).wait_send()
    for k in range(1,8): nc1(k,False).wait_send()
    for k in range(1,16): nc2(k,False).wait_send()

def call_k3(*args):
    V=pl.BlockSpec(memory_space=pltpu.VMEM)
    bf=jnp.bfloat16; f32=jnp.float32
    S=jax.ShapeDtypeStruct; DM=pltpu.SemaphoreType.DMA
    pp=S((6,9344),f32); vv=S((13,6),f32)
    return pl.pallas_call(k3,
      out_shape=[S((4,128,768),bf),S((4,128,768),f32),S((1,1),f32),pp,pp,pp,pp,vv,vv,vv,vv],
      in_specs=[V]*9,out_specs=[V]*11,
      scratch_shapes=[pltpu.VMEM((768,WC),bf),pltpu.VMEM((4,3,48,WC),bf),pltpu.VMEM((3,48,WC),bf),pltpu.VMEM((8,8,WC),bf),pltpu.VMEM((8,8,WC),bf),
        pltpu.VMEM((128,128),f32),pltpu.VMEM((8,8,128),f32),pltpu.VMEM((16,8,128),f32),
        DM((2,2,4,4)),DM((2,2,4,4)),DM((2,2,4)),DM((2,2,4)),DM((2,8)),DM((2,8)),DM((8,)),DM((8,)),DM((16,)),DM((16,)),DM((2,8)),DM((2,8)),
        pltpu.VMEM((4,128,768),bf)],
      compiler_params=pltpu.CompilerParams(collective_id=1,has_side_effects=True,vmem_limit_bytes=56*2**20),
      name="scatter")(*args)
f32=jnp.float32; bf=jnp.bfloat16
T=1024; D=768; HD=384; FH=1536; WC=4864
NEG=-3.0e38

def dot(a,b): return lax.dot_general(a,b,(((1,),(0,)),((),())),preferred_element_type=f32)
def dnt(a,b): return lax.dot_general(a,b,(((1,),(1,)),((),())),preferred_element_type=f32)
def dtn(a,b): return lax.dot_general(a,b,(((0,),(0,)),((),())),preferred_element_type=f32)
def al(v,m=128): return pl.multiple_of(v,m)
def low_lanes(shape): return lax.broadcasted_iota(jnp.int32,shape,len(shape)-1)<64
def roll64(v): return pltpu.roll(v,64,1)
def rows(i,n=256): return pl.ds(al(i*n),n)

def norm_stats(v):
    mu=jnp.mean(v,axis=-1,keepdims=True)
    cen=v-mu
    r=lax.rsqrt(jnp.mean(cen*cen,axis=-1,keepdims=True)+1e-5)
    return cen,r

def setup_masks(sg,segc,mask,maskt):
    for b in range(8):
        segc[b*128:b*128+128,:]=jnp.transpose(jnp.broadcast_to(sg[b,0:1,:],(128,128)))
    r=lax.broadcasted_iota(jnp.int32,(256,256),0); q=lax.broadcasted_iota(jnp.int32,(256,256),1)
    for i in range(4):
        row=jnp.concatenate([sg[2*i,0:1,:],sg[2*i+1,0:1,:]],axis=1)
        col=segc[i*256:i*256+256,:]
        eq=jnp.concatenate([col,col],axis=1)==row
        mask[i]=(eq&(q<=r)).astype(f32)
        maskt[i]=(eq&(r<=q)).astype(f32)

def feature_maps(w,c,p):
    F=w[pl.ds(al(c*384+p*128),128),1536:1664].astype(f32)
    R=roll64(F)
    top=lax.broadcasted_iota(jnp.int32,(128,128),0)<64
    m0=low_lanes((128,128))
    z=jnp.zeros_like(F)
    bq=jnp.where(top&m0,F,jnp.where(top|m0,z,R))
    bk=jnp.where(top&m0,R,jnp.where(top|m0,z,F))
    return bq.astype(bf),bk.astype(bf)

def seg_ones():
    a=lax.broadcasted_iota(jnp.int32,(128,128),0)<64
    return (a==low_lanes((128,128))).astype(bf)

def feats(z,m0,ones):
    mx=jnp.where(m0,jnp.max(jnp.where(m0,z,NEG),-1,keepdims=True),jnp.max(jnp.where(m0,NEG,z),-1,keepdims=True))
    mn=jnp.where(m0,jnp.min(jnp.where(m0,z,-NEG),-1,keepdims=True),jnp.min(jnp.where(m0,-NEG,z),-1,keepdims=True))
    ep=jnp.exp(z-mx).astype(bf); en=jnp.exp(mn-z).astype(bf)
    fp=ep.astype(f32)/dot(ep,ones); fn=roll64(en.astype(f32)/dot(en,ones))
    return jnp.where(m0,fp,fn).astype(bf),jnp.where(m0,fn,fp).astype(bf)

def same_seg(segc,i):
    sc=segc[i*256:i*256+256,:]
    last=segc[i*256+255:i*256+256,:]
    km=(sc==last).astype(f32)
    if i==0: return None,km,None
    prev=segc[i*256-1:i*256,:]
    return (sc==prev).astype(f32),km,(last==prev).astype(f32)

def phase_a(c,x,sg,w,vec,h1,qkv,qf,kf,att,invd,st,segc,mask,maskt,attl):
    vec[...]=jnp.transpose(w[:,1664:1792].astype(f32))[0:16]
    setup_masks(sg,segc,mask,maskt)
    g1=vec[0:1,:]; b1=vec[1:2,:]
    @pl.loop(0,4)
    def _(i):
        cen,r=norm_stats(x[rows(i),:].astype(f32))
        h1[rows(i),:]=(cen*r*g1+b1).astype(bf)
    half=pl.ds(al(c*384),384)
    bias=jnp.concatenate([vec[4:5,half],vec[5:6,half],vec[6:7,half]],axis=1)
    @pl.loop(0,4)
    def _(i):
        hb=h1[rows(i),:]
        for n in range(3):
            qkv[rows(i),n*384:n*384+384]=(dot(hb,w[:,n*384:n*384+384])+bias[:,n*384:n*384+384]).astype(bf)
    ones=seg_ones()
    m0=low_lanes((256,128))
    @pl.loop(0,3)
    def _(p):
        lanes=pl.ds(al(p*128),128)
        bq,bk=feature_maps(w,c,p)
        state=[None,None]
        for i in range(4):
            rs=slice(i*256,i*256+256)
            qe,qo=feats(dot(qkv[rs,lanes],bq),m0,ones)
            ke,ko=feats(dot(qkv[rs,pl.ds(al(384+p*128),128)],bk),m0,ones)
            v=qkv[rs,pl.ds(al(768+p*128),128)]
            qm,km,same=same_seg(segc,i)
            outs=[]
            for h,(qq,kk) in enumerate(((qe,ke),(qo,ko))):
                vx=jnp.where(m0==(h==0),v,jnp.ones_like(v))
                qf[2*p+h,rs,:]=qq; kf[2*p+h,rs,:]=kk
                a=(dnt(qq,kk)*mask[i]).astype(bf)
                o=dot(a,vx)
                if i>0:
                    sb=state[h].astype(bf)
                    st[2*p+h,i-1]=sb
                    o=o+dot(qq,sb)*qm
                if i<3:
                    sn=dtn((kk.astype(f32)*km).astype(bf),vx)
                    state[h]=sn if i==0 else sn+same*state[h]
                outs.append(o)
            num=jnp.where(m0,outs[0],outs[1]); den=roll64(jnp.where(m0,outs[1],outs[0]))
            inv=1.0/den
            av=num*inv
            invd[rs,lanes]=inv
            att[rs,lanes]=av
            attl[rs,lanes]=av.astype(bf)

def phase_b(c,x,dy,attf,w,wo,vec,x2,h2,h2t,dyt,attt,act,du,g,gb,outp,dh2p):
    g2=vec[2:3,:]; b2=vec[3:4,:]; bo=vec[7:8,:]
    @pl.loop(0,4)
    def _(i):
        v=x[rows(i),:].astype(f32)+dot(attf[rows(i),:],wo[...])+bo
        x2[rows(i),:]=v
        cen,r=norm_stats(v)
        h=(cen*r*g2+b2).astype(bf)
        h2[rows(i),:]=h
        h2t[:,rows(i)]=jnp.transpose(h)
        dyt[:,rows(i)]=jnp.transpose(dy[rows(i),:])
        attt[:,rows(i)]=jnp.transpose(attf[rows(i),:])
    k0=0.7978845608028654; k1=0.044715
    CH=256
    gb[...]=jnp.zeros_like(gb)
    @pl.loop(0,FH//CH)
    def _(j):
        cu=pl.ds(al(1792+j*CH),CH); cd=pl.ds(al(3328+j*CH),CH); cj=pl.ds(al(j*CH),CH)
        off=c*FH+j*CH
        bu=vec[pl.ds(8+off//D,1),pl.ds(al(lax.rem(off,D)),CH)]
        @pl.loop(0,4)
        def _(i):
            u=dot(h2[rows(i),:],w[:,cu])+bu
            u2=u*u
            t=jnp.tanh(k0*(u+k1*u2*u))
            act[rows(i),cj]=(0.5*u*(1.0+t)).astype(bf)
            da=dot(dy[rows(i),:],w[:,cd])
            gp=0.5*(1.0+t)+0.5*u*(1.0-t*t)*(k0*(1.0+(3*k1)*u2))
            d=(gp*da).astype(bf)
            du[rows(i),cj]=d
            gb[0:1,cj]=gb[0:1,cj]+jnp.sum(d.astype(f32),axis=0,keepdims=True)
        for m in range(3):
            ms=slice(m*256,m*256+256)
            g[ms,cd]=dot(dyt[ms,:],act[:,cj]).astype(bf)
            g[ms,cu]=dot(h2t[ms,:],du[:,cj]).astype(bf)
    for n in range(3):
        ns=slice(n*256,n*256+256)
        @pl.loop(0,4)
        def _(i):
            outp[rows(i),ns]=dnt(act[rows(i),:],w[ns,3328:4864]).astype(bf)
            dh2p[rows(i),ns]=dnt(du[rows(i),:],w[ns,1792:3328]).astype(bf)

def phase_c(c,dy,dh2p,dh2o,x2,vec,w,wo,attt,h1,qkv,qf,kf,att,invd,st,segc,mask,maskt,dx2,dob,datt,h1t,dproj,g,vg,dh1p,gb):
    g2=vec[2:3,:]
    vg[...]=jnp.zeros_like(vg)
    one=(c==0).astype(f32)
    @pl.loop(0,4)
    def _(i):
        cen,r=norm_stats(x2[rows(i),:])
        xh=cen*r
        dh=dh2p[rows(i),:].astype(f32)+dh2o[rows(i),:].astype(f32)
        dyv=dy[rows(i),:].astype(f32)
        dx=dh*g2
        dx=r*(dx-jnp.mean(dx,-1,keepdims=True)-xh*jnp.mean(dx*xh,-1,keepdims=True))+dyv
        dx2[rows(i),:]=dx
        do=dx.astype(bf)
        dob[rows(i),:]=do
        sm=lambda v: jnp.sum(v,axis=0,keepdims=True)*one
        vg[2:3,:]+=sm(dh*xh); vg[3:4,:]+=sm(dh); vg[7:8,:]+=sm(do.astype(f32)); vg[12:13,:]+=sm(dyv)
        datt[rows(i),:]=dnt(do,wo[pl.ds(al(c*384),384),:])
        h1t[:,rows(i)]=jnp.transpose(h1[rows(i),:])
    for m in range(3):
        ms=slice(m*256,m*256+256)
        g[ms,1152:1536]=dot(attt[ms,:],dob[:,pl.ds(al(c*384),384)]).astype(bf)
    g[:,1536:1664]=jnp.zeros((768,128),bf)
    ones=seg_ones()
    m0=low_lanes((256,128))
    @pl.loop(0,3)
    def _(p):
        lanes=pl.ds(al(p*128),128)
        kl=pl.ds(al(384+p*128),128); vl=pl.ds(al(768+p*128),128)
        bq,bk=feature_maps(w,c,p)
        dst=[None,None]
        gq=jnp.zeros((128,128),f32); gk=jnp.zeros((128,128),f32)
        for i in (3,2,1,0):
            rs=slice(i*256,i*256+256)
            dv_=datt[rs,lanes]; inv=invd[rs,lanes]
            dn=dv_*inv
            dd=roll64(-(dn*att[rs,lanes]))
            v=qkv[rs,vl]
            qm,km,same=same_seg(segc,i)
            dq=[];dk=[];dvv=[]
            for h in range(2):
                mh=m0==(h==0)
                vx=jnp.where(mh,v,jnp.ones_like(v))
                dx=jnp.where(mh,dn,dd).astype(bf)
                qq=qf[2*p+h,rs,:]; kk=kf[2*p+h,rs,:]
                at=(dnt(kk,qq)*maskt[i]).astype(bf)
                da=(dnt(dx,vx)*mask[i]).astype(bf)
                dat=(dnt(vx,dx)*maskt[i]).astype(bf)
                gqf=dot(da,kk); gkf=dot(dat,qq); gv=dot(at,dx)
                if i<3:
                    ds=dst[h].astype(bf)
                    gkf=gkf+dnt(vx,ds)*km
                    gv=gv+dot(kk,ds)*km
                if i>0:
                    gqf=gqf+dnt(dx,st[2*p+h,i-1])*qm
                    dn_=dtn((qq.astype(f32)*qm).astype(bf),dx)
                    dst[h]=dn_ if i==3 else dn_+same*dst[h]
                dq.append(gqf);dk.append(gkf);dvv.append(gv)
            def soft(fe,fo,de,do_):
                fe=fe.astype(f32); fo=fo.astype(f32)
                fp=jnp.where(m0,fe,fo); fr=jnp.where(m0,fo,fe)
                tp=fp*jnp.where(m0,de,do_); tr=fr*jnp.where(m0,do_,de)
                sp=dot(tp.astype(bf),ones)+dot((tp-tp.astype(bf).astype(f32)).astype(bf),ones)
                sr=dot(tr.astype(bf),ones)+dot((tr-tr.astype(bf).astype(f32)).astype(bf),ones)
                return ((tp-fp*sp)-roll64(tr-fr*sr)).astype(bf)
            zq=soft(qf[2*p,rs,:],qf[2*p+1,rs,:],dq[0],dq[1])
            zk=soft(kf[2*p,rs,:],kf[2*p+1,rs,:],dk[0],dk[1])
            gq=gq+dtn(qkv[rs,lanes],zq); gk=gk+dtn(qkv[rs,kl],zk)
            dproj[rs,lanes]=dnt(zq,bq).astype(bf)
            dproj[rs,kl]=dnt(zk,bk).astype(bf)
            dproj[rs,vl]=jnp.where(m0,dvv[0],dvv[1]).astype(bf)
        top=lax.broadcasted_iota(jnp.int32,(128,128),0)<64
        ml=low_lanes((128,128))
        g[pl.ds(al(c*384+p*128),128),1536:1664]=jnp.where(top,jnp.where(ml,gq,roll64(gk)),jnp.where(ml,roll64(gq),gk)).astype(bf)
    for n in range(3):
        ns=slice(n*384,n*384+384)
        for m in range(3):
            ms=slice(m*256,m*256+256)
            g[ms,ns]=dot(h1t[ms,:],dproj[:,ns]).astype(bf)
        vg[4+n:5+n,pl.ds(al(c*384),384)]=jnp.sum(dproj[:,ns].astype(f32),axis=0,keepdims=True)
    for k in range(2):
        vg[pl.ds(8+2*c+k,1),:]=gb[0:1,k*768:k*768+768]
    for n in range(3):
        ns=slice(n*256,n*256+256)
        @pl.loop(0,4)
        def _(i):
            dh1p[rows(i),ns]=dnt(dproj[rows(i),:],w[ns,0:1152]).astype(bf)

def phase_d(c,x,x2,dx2,vec,outp,outo,dh1p,dh1o,vg,g,bo,ig):
    g1=vec[0:1,:]; bd=vec[12:13,:]
    @pl.loop(0,2)
    def _(i):
        rs=pl.ds(al(c*512+i*256),256)
        bo[rows(i),:]=(x2[rs,:]+outp[rs,:].astype(f32)+outo[rows(i),:].astype(f32)+bd).astype(bf)
        cen,r=norm_stats(x[rs,:].astype(f32))
        xh=cen*r
        dh=dh1p[rs,:].astype(f32)+dh1o[rows(i),:].astype(f32)
        dx=dh*g1
        dx=r*(dx-jnp.mean(dx,-1,keepdims=True)-xh*jnp.mean(dx*xh,-1,keepdims=True))
        ig[rows(i),:]=(dx+dx2[rs,:]).astype(bf)
        vg[0:1,:]+=jnp.sum(dh*xh,axis=0,keepdims=True); vg[1:2,:]+=jnp.sum(dh,axis=0,keepdims=True)
    z=jnp.concatenate([vg[...],jnp.zeros((112,768),f32)],axis=0)
    g[:,1664:1792]=jnp.transpose(z).astype(bf)

def compute(x,dy,sg,w,wo,interpret=False):
    V=pl.BlockSpec(memory_space=pltpu.VMEM)
    S=jax.ShapeDtypeStruct; M=pltpu.VMEM
    c_=lambda: lax.axis_index("c")
    def call(fn,name,ins,outs,alias=None,limit=58):
        kw={}
        if interpret: kw["interpret"]=interpret
        return pl.pallas_call(fn,out_shape=outs,in_specs=[V]*len(ins),out_specs=[V]*len(outs),
            compiler_params=pltpu.CompilerParams(vmem_limit_bytes=limit*2**20),name=name,input_output_aliases=alias or {},**kw)(*ins)
    pc=c_().reshape(1).astype(jnp.int32)
    SM=pl.BlockSpec(memory_space=pltpu.SMEM)
    def callc(fn,name,ins,outs,limit=58,scr=()):
        kw={}
        if interpret: kw["interpret"]=interpret
        return pl.pallas_call(lambda cr,*r: fn(cr[0],*r),out_shape=outs,in_specs=[SM]+[V]*len(ins),out_specs=[V]*len(outs),scratch_shapes=list(scr),
            compiler_params=pltpu.CompilerParams(vmem_limit_bytes=limit*2**20),name=name,**kw)(pc,*ins)
    def pa(c,x,sg,w,vec,h1,qkv,qf,kf,att,invd,st,segc,mask,maskt,attl):
        phase_a(c,x,sg,w,vec,h1,qkv,qf,kf,att,invd,st,segc,mask,maskt,attl)
    ft=S((6,T,128),bf)
    vec,h1,qkv,qf,kf,att,invd,st,segc,mask,maskt,attl=callc(pa,"phase_a",(x,sg,w),
        [S((16,D),f32),S((T,D),bf),S((T,3*HD),bf),ft,ft,S((T,HD),f32),S((T,HD),f32),S((6,3,128,128),bf),S((T,128),f32),S((4,256,256),f32),S((4,256,256),f32),S((T,HD),bf)])
    perm=[(0,1),(1,0)]
    swap=lambda v: lax.ppermute(v,"c",perm)
    other=swap(attl)
    c=c_()
    attf=jnp.where(c==0,jnp.concatenate([attl,other],1),jnp.concatenate([other,attl],1))
    def pb(c,x,dy,attf,w,wo,vec,x2,h2,attt,outp,dh2p,gu,gb,h2t,dyt,act,du,g):
        phase_b(c,x,dy,attf,w,wo,vec,x2,h2,h2t,dyt,attt,act,du,g,gb,outp,dh2p)
        gu[...]=g[:,1792:4864]
    x2,h2,attt,outp,dh2p,gu,gb=callc(pb,"phase_b",(x,dy,attf,w,wo,vec),
        [S((T,D),f32),S((T,D),bf),S((D,T),bf),S((T,D),bf),S((T,D),bf),S((D,3072),bf),S((8,FH),f32)],
        scr=[M((D,T),bf),M((D,T),bf),M((T,FH),bf),M((T,FH),bf),M((D,WC),bf)])
    dh2o=swap(dh2p)
    oc=lax.dynamic_slice_in_dim(outp,(1-c)*512,512,0)
    outo=swap(oc)
    def pc_(c,dy,dh2p,dh2o,x2,vec,w,wo,attt,h1,qkv,qf,kf,att,invd,st,segc,mask,maskt,gb,dx2,g,vg,dh1p,dob,datt,h1t,dproj):
        phase_c(c,dy,dh2p,dh2o,x2,vec,w,wo,attt,h1,qkv,qf,kf,att,invd,st,segc,mask,maskt,dx2,dob,datt,h1t,dproj,g,vg,dh1p,gb)
    dx2,ga,vg,dh1p=callc(pc_,"phase_c",(dy,dh2p,dh2o,x2,vec,w,wo,attt,h1,qkv,qf,kf,att,invd,st,segc,mask,maskt,gb),
        [S((T,D),f32),S((D,1664),bf),S((16,D),f32),S((T,D),bf)],scr=[M((T,D),bf),M((T,HD),f32),M((D,T),bf),M((T,3*HD),bf)])
    dh1o=swap(lax.dynamic_slice_in_dim(dh1p,(1-c)*512,512,0))
    def pd(c,x,x2,dx2,vec,outp,outo,dh1p,dh1o,vg,bo,ig,gv,vgs,gs):
        vgs[...]=vg[...]
        phase_d(c,x,x2,dx2,vec,outp,outo,dh1p,dh1o,vgs,gs,bo,ig)
        gv[...]=gs[:,1664:1792]
    bo,ig,gv=callc(pd,"phase_d",(x,x2,dx2,vec,outp,outo,dh1p,dh1o,vg),[S((512,D),bf),S((512,D),bf),S((D,128),bf)],scr=[M((16,D),f32),M((D,WC),bf)])
    g=jnp.concatenate([ga,gv,gu],axis=1)
    return g,bo,ig

def body(inputs,segment_ids,out_grad,params,vectors,params_m,params_v,vectors_m,vectors_v):
    vt=jnp.pad(vectors.T,((0,0),(0,115)))
    sgin=jnp.broadcast_to(segment_ids.astype(jnp.float32)[:,None,:],(4,8,128))
    w,wo,xrow,dyrow,sg=call_k1(params,vt,inputs,out_grad,sgin)
    g,bo,ig=compute(xrow,dyrow,sg,w,wo)
    o=call_k3(g,bo,ig,params,params_m,params_v,vectors,vectors_m,vectors_v)
    return (o[0],o[1],o[2].reshape(1))+tuple(o[3:])

def solution(mesh):
    torus=Mesh(mesh.devices.reshape(4,4,4,2),("x","z","y","c"))
    row=("x","z"); seq=("y","c"); every=("x","z","y","c")
    tok=P(row,seq,None); mat=P(every,None); vec=P(None,every)
    return jax.shard_map(body,mesh=torus,in_specs=(tok,P(row,seq),tok,mat,vec,mat,mat,vec,vec),
        out_specs=(tok,tok,P(),mat,mat,mat,mat,vec,vec,vec,vec),check_vma=False)
```

```python
import jax
import jax.numpy as jnp
from jax import lax
from jax.experimental import pallas as pl
from jax.experimental.pallas import tpu as pltpu
from jax.sharding import Mesh
from jax.sharding import PartitionSpec as P

f32 = jnp.float32
bf = jnp.bfloat16
MESH = pl.DeviceIdType.MESH
T, D, HD, FH = 1024, 768, 384, 1536
G1 = 1792
WC = 4864
PIECES = (
    (0, 384, 0, 384),
    (384, 384, 768, 384),
    (768, 384, 1536, 384),
    (1152, 384, 2304, 384),
    (1536, 128, 3072, 0),
    (1792, 1536, 3200, 1536),
    (3328, 1536, 6272, 1536),
)
GATHER = (((0, 384, 896), (896, 1280, 1792)), ((1792, 2560, 3328), (3328, 4096, 4864)))
REDUCE = (((0, 384, 768), (768, 1152, 1664)), ((1792, 2560, 3328), (3328, 4096, 4864)))
FAR = (0, -1, 1, 2)
BIG = 3.0e38


def dot(a, b):
    return lax.dot_general(a, b, (((1,), (0,)), ((), ())), preferred_element_type=f32)


def dot_nt(a, b):
    return lax.dot_general(a, b, (((1,), (1,)), ((), ())), preferred_element_type=f32)


def dot_tn(a, b):
    return lax.dot_general(a, b, (((0,), (0,)), ((), ())), preferred_element_type=f32)


def at(v, m=128):
    return pl.multiple_of(v, m)


def rows(i, n=256):
    return pl.ds(at(i * n), n)


def low_lanes(shape):
    return lax.broadcasted_iota(jnp.int32, shape, len(shape) - 1) < 64


def roll64(v):
    return pltpu.roll(v, 64, 1)


def slab(xx, zz):
    return at((lax.rem(xx + 8, 4) * 4 + lax.rem(zz + 8, 4)) * 48, 16)


def norm_stats(v):
    mu = jnp.mean(v, axis=-1, keepdims=True)
    cen = v - mu
    return cen, lax.rsqrt(jnp.mean(cen * cen, axis=-1, keepdims=True) + 1e-5)


def seg_ones():
    a = lax.broadcasted_iota(jnp.int32, (128, 128), 0) < 64
    return (a == low_lanes((128, 128))).astype(bf)


def feats(z, m0, ones):
    mx = jnp.where(m0, jnp.max(jnp.where(m0, z, -BIG), -1, keepdims=True), jnp.max(jnp.where(m0, -BIG, z), -1, keepdims=True))
    mn = jnp.where(m0, jnp.min(jnp.where(m0, z, BIG), -1, keepdims=True), jnp.min(jnp.where(m0, BIG, z), -1, keepdims=True))
    ep = jnp.exp(z - mx).astype(bf)
    en = jnp.exp(mn - z).astype(bf)
    fp = ep.astype(f32) / dot(ep, ones)
    fn = roll64(en.astype(f32) / dot(en, ones))
    return jnp.where(m0, fp, fn).astype(bf), jnp.where(m0, fn, fp).astype(bf)


def soft_back(fe, fo, de, do, m0, ones):
    fe = fe.astype(f32)
    fo = fo.astype(f32)
    fp = jnp.where(m0, fe, fo)
    fr = jnp.where(m0, fo, fe)
    tp = fp * jnp.where(m0, de, do)
    tr = fr * jnp.where(m0, do, de)

    def total(t):
        hi = t.astype(bf)
        return dot(hi, ones) + dot((t - hi.astype(f32)).astype(bf), ones)

    return ((tp - fp * total(tp)) - roll64(tr - fr * total(tr))).astype(bf)


def same_doc(segc, i):
    sc = segc[i * 256 : i * 256 + 256, :]
    last = segc[i * 256 + 255 : i * 256 + 256, :]
    km = (sc == last).astype(f32)
    if i == 0:
        return None, km, None
    prev = segc[i * 256 - 1 : i * 256, :]
    return (sc == prev).astype(f32), km, (last == prev).astype(f32)


def layer(
    par, vt, xin, dyin, sgin,
    out_o, ig_o, pg_o, vs_o, norm_o,
    w, wo, xr, dyr, sg, wire, rcv, vec, h1, h1t, qkv, qf, kf, invd, st, segc, mask, maskt, attf,
    x2, h2, h2t, dyt, act, du, outp, outo, dh2p, dh2o, dh1o, g, r1, r2, yr, n1, n2, vg, gb, vsrc, vrc,
    s0s, s0r, ags, agr, rss, rsr, sgs, sgr, exs, exr, s1s, s1r, s2s, s2r, yss, ysr,
    n1s, n1r, n2s, n2r, tks, tkr, vxs, vxr, los,
):
    x, z, y, c = (lax.axis_index(a) for a in ("x", "z", "y", "c"))
    s = y * 2 + c
    pln = x * 4 + z
    own = at(c * 384)

    def rcopy(src, dst, ss, rs, dev):
        return pltpu.make_async_remote_copy(src, dst, ss, rs, device_id=dev, device_id_type=MESH)

    def seq_peer(k):
        t = lax.rem(s + k + 8, 8)
        return t, {"y": t // 2, "c": lax.rem(t, 2)}

    def plane_peer(k):
        t = lax.rem(pln + k + 16, 16)
        return t, {"x": t // 4, "z": lax.rem(t, 4)}

    other = {"c": 1 - c}

    bar = pltpu.get_barrier_semaphore()
    for k in range(1, 8):
        pl.semaphore_signal(bar, inc=1, device_id=seq_peer(k)[1], device_id_type=MESH)
    for k in range(1, 16):
        pl.semaphore_signal(bar, inc=1, device_id=plane_peer(k)[1], device_id_type=MESH)
    for cc in range(2):
        wire[cc, :, :] = jnp.zeros((8, WC), bf)
        for d, wd, sr, sp in PIECES:
            wire[cc, 0:6, d : d + wd] = par[:, sr + sp * cc : sr + sp * cc + wd].astype(bf)
        wire[cc, 0:6, 1664:1792] = vt[...].astype(bf)
    pl.semaphore_wait(bar, 22)
    cols_of = ((0, G1), (G1, WC))

    def st0(gp, k, recv=False):
        t, dev = seq_peer(k)
        a, b = cols_of[gp]
        slot = seq_peer(-k)[0] if recv else s
        return rcopy(wire.at[dev["c"], :, a:b], rcv.at[slot, :, a:b], s0s.at[gp, k], s0r.at[gp, k], dev)

    def sgc(k, recv=False):
        t, dev = seq_peer(k)
        slot = seq_peer(-k)[0] if recv else s
        return rcopy(sgin.at[t // 2], sg.at[slot], sgs.at[k], sgr.at[k], dev)

    pairs = ((xin, xr), (dyin, dyr))

    def res(wh, k, recv=False):
        src, dst = pairs[wh]
        j = lax.rem(y + k, 4)
        slot = (lax.rem(y - k + 4, 4) * 2 + c) if recv else s
        return rcopy(src.at[j], dst.at[rows(slot, 128)], rss.at[wh, k], rsr.at[wh, k], {"y": j})

    def keep(wh):
        src, dst = pairs[wh]
        return pltpu.make_async_copy(src.at[y], dst.at[rows(s, 128)], los.at[wh])

    def sib(wh, k, recv=False):
        slot = lax.rem(y - k + 4, 4) * 2 + ((1 - c) if recv else c)
        ref = pairs[wh][1].at[rows(slot, 128)]
        return rcopy(ref, ref, rss.at[wh, 4 + k], rsr.at[wh, 4 + k], other)

    def res_start(wh):
        keep(wh).start()
        for k in range(1, 4):
            res(wh, k).start()

    def res_pass(wh):
        keep(wh).wait()
        sib(wh, 0).start()
        for k in range(1, 4):
            res(wh, k, True).wait_recv()
            sib(wh, k).start()

    def res_end(wh):
        for k in range(4):
            sib(wh, k, True).wait_recv()

    def pos(p, d1, d2):
        return slab(x + d1, z + d2) if p == 0 else slab(x + d2, z + d1)

    def along(p, phase, way):
        k = (p + phase) % 2
        return {("x", "z")[k]: lax.rem((x, z)[k] + way + 4, 4)}

    def cut(table, gp, p, h):
        lo, mid, hi = table[gp][p]
        return ((lo, hi), (lo, mid), (mid, hi))[h]

    def ag(gp, p, sem, d1, d2, h, phase, way):
        a, b = cut(GATHER, gp, p, h)
        ref = w.at[pl.ds(pos(p, d1, d2), 48), a:b]
        return rcopy(ref, ref, ags.at[gp, p, sem], agr.at[gp, p, sem], along(p, phase, way))

    def p2send(gp, p, q):
        ag(gp, p, 4 + 4 * q, FAR[q], 0, 0, 1, 1).start()
        ag(gp, p, 5 + 4 * q, FAR[q], 0, 0, 1, -1).start()

    def p2fwd(gp, p, q):
        ag(gp, p, 4 + 4 * q, FAR[q], -1, 0, 1, 1).wait_recv()
        ag(gp, p, 6 + 4 * q, FAR[q], -1, 1, 1, 1).start()
        ag(gp, p, 5 + 4 * q, FAR[q], 1, 0, 1, -1).wait_recv()
        ag(gp, p, 7 + 4 * q, FAR[q], 1, 2, 1, -1).start()

    def ag_a(gp):
        for p in range(2):
            ag(gp, p, 0, 0, 0, 0, 0, 1).start()
            ag(gp, p, 1, 0, 0, 0, 0, -1).start()
        for p in range(2):
            p2send(gp, p, 0)

    def ag_b(gp):
        for p in range(2):
            ag(gp, p, 0, -1, 0, 0, 0, 1).wait_recv()
            ag(gp, p, 2, -1, 0, 1, 0, 1).start()
            ag(gp, p, 1, 1, 0, 0, 0, -1).wait_recv()
            ag(gp, p, 3, 1, 0, 2, 0, -1).start()
            p2send(gp, p, 1)
            p2send(gp, p, 2)

    def ag_c(gp):
        for p in range(2):
            p2fwd(gp, p, 0)
        for p in range(2):
            ag(gp, p, 2, 2, 0, 1, 0, 1).wait_recv()
            ag(gp, p, 3, 2, 0, 2, 0, -1).wait_recv()
            p2send(gp, p, 3)

    def ag_d(gp):
        for q in (1, 2, 3):
            for p in range(2):
                p2fwd(gp, p, q)

    def ag_e(gp):
        for p in range(2):
            for q in range(4):
                ag(gp, p, 6 + 4 * q, FAR[q], 2, 1, 1, 1).wait_recv()
                ag(gp, p, 7 + 4 * q, FAR[q], 2, 2, 1, -1).wait_recv()

    def ag_sends(gp):
        for p in range(2):
            ag(gp, p, 0, 0, 0, 0, 0, 1).wait_send()
            ag(gp, p, 1, 0, 0, 0, 0, -1).wait_send()
            ag(gp, p, 2, -1, 0, 1, 0, 1).wait_send()
            ag(gp, p, 3, 1, 0, 2, 0, -1).wait_send()
            for q in range(4):
                ag(gp, p, 4 + 4 * q, FAR[q], 0, 0, 1, 1).wait_send()
                ag(gp, p, 5 + 4 * q, FAR[q], 0, 0, 1, -1).wait_send()
                ag(gp, p, 6 + 4 * q, FAR[q], -1, 1, 1, 1).wait_send()
                ag(gp, p, 7 + 4 * q, FAR[q], 1, 2, 1, -1).wait_send()

    rr = lax.broadcasted_iota(jnp.int32, (48, 64), 0)
    rc = lax.broadcasted_iota(jnp.int32, (48, 64), 1)
    spread = ((lax.rem(rr, 6) == lax.rem(rc, 8)) & (rr // 6 == rc // 8)).astype(bf)

    def assemble(gp):
        for k in range(1, 8):
            st0(gp, k, True).wait_recv()
        a, b = cols_of[gp]
        n = 896 if gp == 0 else 768
        for lo in range(a, b, n):
            raw = jnp.concatenate([rcv[t, :, lo : lo + n].astype(f32) for t in range(8)], axis=0).astype(bf)
            w[pl.ds(slab(x, z), 48), lo : lo + n] = dot(spread, raw).astype(bf)

    for k in range(1, 8):
        st0(0, k).start()
    for k in range(1, 8):
        sgc(k).start()
    res_start(0)
    for k in range(1, 8):
        st0(1, k).start()
    sg[s] = sgin[y]
    rcv[s] = wire[c]
    assemble(0)
    ag_a(0)
    res_start(1)
    res_pass(0)
    assemble(1)
    ag_b(0)
    for k in range(1, 8):
        sgc(k, True).wait_recv()
    for b in range(8):
        segc[b * 128 : b * 128 + 128, :] = jnp.transpose(jnp.broadcast_to(sg[b, 0:1, :], (128, 128)))
    mr = lax.broadcasted_iota(jnp.int32, (256, 256), 0)
    mc = lax.broadcasted_iota(jnp.int32, (256, 256), 1)
    for i in range(4):
        row = jnp.concatenate([sg[2 * i, 0:1, :], sg[2 * i + 1, 0:1, :]], axis=1)
        col = segc[i * 256 : i * 256 + 256, :]
        eq = jnp.concatenate([col, col], axis=1) == row
        mask[i] = (eq & (mc <= mr)).astype(f32)
        maskt[i] = (eq & (mr <= mc)).astype(f32)
    ag_c(0)
    res_end(0)
    ag_d(0)
    ag_a(1)
    ag_e(0)

    def ex(i, src, dst):
        return rcopy(src, dst, exs.at[i], exr.at[i], other)

    mine = pl.ds(own, 384)
    ex(0, w.at[:, 1152:1536], wo.at[:, mine]).start()
    wo[:, mine] = w[:, 1152:1536]

    vec[...] = jnp.transpose(w[:, 1664:1792].astype(f32))[0:16]

    @pl.loop(0, 4)
    def _(i):
        cen, r = norm_stats(xr[rows(i), :].astype(f32))
        h = (cen * r * vec[0:1, :] + vec[1:2, :]).astype(bf)
        h1[rows(i), :] = h
        h1t[:, rows(i)] = jnp.transpose(h)

    res_pass(1)
    bias = jnp.concatenate([vec[4:5, mine], vec[5:6, mine], vec[6:7, mine]], axis=1)

    @pl.loop(0, 4)
    def _(i):
        hb = h1[rows(i), :]
        for n in range(3):
            e = slice(n * 384, n * 384 + 384)
            qkv[rows(i), e] = (dot(hb, w[:, e]) + bias[:, e]).astype(bf)

    ag_b(1)
    ones = seg_ones()
    m0 = low_lanes((256, 128))

    def feature_maps(p):
        F = w[pl.ds(at(c * 384 + p * 128), 128), 1536:1664].astype(f32)
        R = roll64(F)
        top = lax.broadcasted_iota(jnp.int32, (128, 128), 0) < 64
        ml = low_lanes((128, 128))
        zz = jnp.zeros_like(F)
        bq = jnp.where(top & ml, F, jnp.where(top | ml, zz, R))
        bk = jnp.where(top & ml, R, jnp.where(top | ml, zz, F))
        return bq.astype(bf), bk.astype(bf)

    def att_part(p):
        return attf.at[:, pl.ds(at(own + p * 128), 128)]

    @pl.loop(0, 3)
    def _(p):
        lanes = pl.ds(at(p * 128), 128)
        bq, bk = feature_maps(p)
        state = [None, None]
        for i in range(4):
            rs = slice(i * 256, i * 256 + 256)
            qe, qo = feats(dot(qkv[rs, lanes], bq), m0, ones)
            ke, ko = feats(dot(qkv[rs, pl.ds(at(384 + p * 128), 128)], bk), m0, ones)
            v = qkv[rs, pl.ds(at(768 + p * 128), 128)]
            qm, km, same = same_doc(segc, i)
            outs = []
            for h, (qq, kk) in enumerate(((qe, ke), (qo, ko))):
                vx = jnp.where(m0 == (h == 0), v, jnp.ones_like(v))
                qf[2 * p + h, rs, :] = qq
                kf[2 * p + h, rs, :] = kk
                o = dot((dot_nt(qq, kk) * mask[i]).astype(bf), vx)
                if i > 0:
                    sb = state[h].astype(bf)
                    st[2 * p + h, i - 1] = sb
                    o = o + dot(qq, sb) * qm
                if i < 3:
                    sn = dot_tn((kk.astype(f32) * km).astype(bf), vx)
                    state[h] = sn if i == 0 else sn + same * state[h]
                outs.append(o)
            num = jnp.where(m0, outs[0], outs[1])
            inv = 1.0 / roll64(jnp.where(m0, outs[1], outs[0]))
            invd[rs, lanes] = inv
            attf[rs, pl.ds(at(own + p * 128), 128)] = (num * inv).astype(bf)
        ex(1 + p, att_part(p), att_part(p)).start()

        @pl.when(p == 0)
        def _():
            ag_c(1)

        @pl.when(p == 1)
        def _():
            ag_d(1)

    ag_e(1)
    res_end(1)
    ex(0, w.at[:, 1152:1536], wo.at[:, pl.ds(at((1 - c) * 384), 384)]).wait_recv()
    for p in range(3):
        part = attf.at[:, pl.ds(at((1 - c) * 384 + p * 128), 128)]
        ex(1 + p, part, part).wait_recv()

    @pl.loop(0, 4)
    def _(i):
        v = xr[rows(i), :].astype(f32) + dot(attf[rows(i), :], wo[...]) + vec[7:8, :]
        x2[rows(i), :] = v
        cen, r = norm_stats(v)
        h = (cen * r * vec[2:3, :] + vec[3:4, :]).astype(bf)
        h2[rows(i), :] = h
        h2t[:, rows(i)] = jnp.transpose(h)
        dyt[:, rows(i)] = jnp.transpose(dyr[rows(i), :])

    k0 = 0.7978845608028654
    k1 = 0.044715
    gb[...] = jnp.zeros_like(gb)

    @pl.loop(0, FH // 256)
    def _(j):
        cu = pl.ds(at(1792 + j * 256), 256)
        cd = pl.ds(at(3328 + j * 256), 256)
        gu = pl.ds(at(j * 256), 256)
        gd = pl.ds(at(1536 + j * 256), 256)
        off = c * FH + j * 256
        bu = vec[pl.ds(8 + off // D, 1), pl.ds(at(lax.rem(off, D)), 256)]

        @pl.loop(0, 4)
        def _(i):
            u = dot(h2[rows(i), :], w[:, cu]) + bu
            u2 = u * u
            t = jnp.tanh(k0 * (u + k1 * u2 * u))
            act[rows(i), gu] = (0.5 * u * (1.0 + t)).astype(bf)
            da = dot(dyr[rows(i), :], w[:, cd])
            gp = 0.5 * (1.0 + t) + 0.5 * u * (1.0 - t * t) * (k0 * (1.0 + (3 * k1) * u2))
            d = (gp * da).astype(bf)
            du[rows(i), gu] = d
            gb[0:1, gu] = gb[0:1, gu] + jnp.sum(d.astype(f32), axis=0, keepdims=True)

        for m in range(3):
            ms = slice(m * 256, m * 256 + 256)
            g[ms, gd] = dot(dyt[ms, :], act[:, gu]).astype(bf)
            g[ms, gu] = dot(h2t[ms, :], du[:, gu]).astype(bf)

    def gref(gp, p, d1, d2, h):
        a, b = cut(REDUCE, gp, p, h)
        r = pl.ds(pos(p, d1, d2), 48)
        return w.at[r, a + G1 : b + G1] if gp == 0 else g.at[r, a - G1 : b - G1]

    def land(gp, p, slot, h):
        a, b = cut(REDUCE, gp, p, h)
        r = slice(slot * 48, slot * 48 + 48)
        if gp == 0:
            base = cut(REDUCE, 0, p, 0)[0]
            return (du, h2t)[p].at[r, a - base : b - base]
        return (r1.at[r, a - G1 : b - G1] if slot < 12 else r2.at[slice((slot - 12) * 48, (slot - 12) * 48 + 48), a - G1 : b - G1])

    HALF = (1, 2, 0, 0)
    SLOT = (0, 0, 1, 2)
    HOP = (2, 2, 1, -1)

    def c1(gp, p, q, kind):
        h = HALF[kind]
        return rcopy(gref(gp, p, FAR[q], HOP[kind], h), land(gp, p, q * 3 + SLOT[kind], h), s1s.at[gp, p, q, kind], s1r.at[gp, p, q, kind], along(p, 1, (1, -1)[kind % 2]))

    def c2(gp, p, kind):
        h = HALF[kind]
        return rcopy(gref(gp, p, HOP[kind], 0, h), land(gp, p, 12 + SLOT[kind], h), s2s.at[gp, p, kind], s2r.at[gp, p, kind], along(p, 0, (1, -1)[kind % 2]))

    def acc(dst, *srcs):
        t = dst[...].astype(f32)
        for r in srcs:
            t = t + r[...].astype(f32)
        dst[...] = t.astype(bf)

    def r1_start(gp, q):
        for p in range(2):
            c1(gp, p, q, 0).start()
            c1(gp, p, q, 1).start()

    def r1_mid(gp, q):
        for p in range(2):
            for kind in range(2):
                c1(gp, p, q, kind).wait_recv()
                acc(gref(gp, p, FAR[q], (1, -1)[kind], 1 + kind), land(gp, p, q * 3, 1 + kind))
                c1(gp, p, q, 2 + kind).start()

    def r1_end(gp, q):
        for p in range(2):
            c1(gp, p, q, 2).wait_recv()
            c1(gp, p, q, 3).wait_recv()
            acc(gref(gp, p, FAR[q], 0, 0), land(gp, p, q * 3 + 1, 0), land(gp, p, q * 3 + 2, 0))

    def r2_start(gp):
        for p in range(2):
            c2(gp, p, 0).start()
            c2(gp, p, 1).start()

    def r2_mid(gp):
        for p in range(2):
            for kind in range(2):
                c2(gp, p, kind).wait_recv()
                acc(gref(gp, p, (1, -1)[kind], 0, 1 + kind), land(gp, p, 12, 1 + kind))
                c2(gp, p, 2 + kind).start()

    def r2_end(gp):
        for p in range(2):
            c2(gp, p, 2).wait_recv()
            c2(gp, p, 3).wait_recv()
            acc(gref(gp, p, 0, 0, 0), land(gp, p, 13, 0), land(gp, p, 14, 0))

    tr = lax.broadcasted_iota(jnp.int32, (64, 48), 0)
    tc = lax.broadcasted_iota(jnp.int32, (64, 48), 1)
    split = ((lax.rem(tc, 6) == lax.rem(tr, 8)) & (tc // 6 == tr // 8)).astype(bf)

    def ycp(gp, k, recv=False):
        t, dev = seq_peer(k)
        a, b = cols_of[gp]
        slot = seq_peer(-k)[0] if recv else s
        return rcopy(rcv.at[t, :, a:b], yr.at[slot, :, a:b], yss.at[gp, k], ysr.at[gp, k], dev)

    def y_start(gp):
        mine_ = pl.ds(slab(x, z), 48)
        for p in range(2):
            lo, _, hi = REDUCE[gp][p]
            part = w[mine_, lo + G1 : hi + G1] if gp == 0 else g[mine_, lo - G1 : hi - G1]
            out = dot(split, part).astype(bf)
            for t in range(8):
                rcv[t, :, lo:hi] = out[8 * t : 8 * t + 8]
        if gp == 0:
            tot = vsrc[mine_, :]
            for k in range(1, 16):
                tot = tot + vrc[plane_peer(-k)[0]]
            hi_ = tot.astype(bf)
            out = dot(split, hi_).astype(bf)
            for t in range(8):
                rcv[t, :, 1664:1792] = out[8 * t : 8 * t + 8]
        for k in range(1, 8):
            ycp(gp, k).start()
        a, b = cols_of[gp]
        yr[s, :, a:b] = rcv[s, :, a:b]

    for q in (3, 1, 2, 0):
        r1_start(1, q)

    half = at(c * 512)
    away = at((1 - c) * 512)

    @pl.loop(0, 4)
    def _(i):
        for n in range(3):
            ns = slice(n * 256, n * 256 + 256)
            outp[rows(i), ns] = dot_nt(act[rows(i), :], w[ns, 3328:4864]).astype(bf)

    ex(4, outp.at[pl.ds(away, 512)], outo).start()
    for n in range(3):
        ns = slice(n * 256, n * 256 + 256)

        @pl.loop(0, 4)
        def _(i):
            dh2p[rows(i), ns] = dot_nt(du[rows(i), :], w[ns, 1792:3328]).astype(bf)

        ex(5 + n, dh2p.at[:, ns], dh2o.at[:, ns]).start()
    ex(4, outp.at[pl.ds(away, 512)], outo).wait_recv()

    @pl.loop(0, 2)
    def _(i):
        rs = pl.ds(at(half + i * 256), 256)
        outp[rs, :] = (x2[rs, :] + outp[rs, :].astype(f32) + outo[rows(i), :].astype(f32) + vec[12:13, :]).astype(bf)

    toks = ((outp, out_o), (dh2p, ig_o))

    def tok(wh, k, recv=False):
        src, dst = toks[wh]
        t, dev = seq_peer(k)
        row = (seq_peer(-k)[0] // 2) if recv else y
        return rcopy(src.at[pl.ds(at(half + lax.rem(t, 4) * 128), 128)], dst.at[row], tks.at[wh, k], tkr.at[wh, k], dev)

    def tok_start(wh):
        for k in range(1, 8):

            @pl.when(seq_peer(k)[0] // 4 == c)
            def _():
                tok(wh, k).start()

        src, dst = toks[wh]

        @pl.when(s // 4 == c)
        def _():
            dst[y] = src[pl.ds(at(half + lax.rem(s, 4) * 128), 128), :]

    def tok_wait(wh):
        for k in range(1, 8):

            @pl.when(lax.rem(seq_peer(-k)[0], 2) == s // 4)
            def _():
                tok(wh, k, True).wait_recv()

        for k in range(1, 8):

            @pl.when(seq_peer(k)[0] // 4 == c)
            def _():
                tok(wh, k).wait_send()

    tok_start(0)

    vg[...] = jnp.zeros_like(vg)
    one = (c == 0).astype(f32)
    attt = dyt

    @pl.loop(0, 4)
    def _(i):
        attt[:, rows(i)] = jnp.transpose(attf[rows(i), :])

    for n in range(3):
        ns = slice(n * 256, n * 256 + 256)
        ex(5 + n, dh2p.at[:, ns], dh2o.at[:, ns]).wait_recv()

    @pl.loop(0, 4)
    def _(i):
        cen, r = norm_stats(x2[rows(i), :])
        xh = cen * r
        dh = dh2p[rows(i), :].astype(f32) + dh2o[rows(i), :].astype(f32)
        dyv = dyr[rows(i), :].astype(f32)
        dx = dh * vec[2:3, :]
        dx = r * (dx - jnp.mean(dx, -1, keepdims=True) - xh * jnp.mean(dx * xh, -1, keepdims=True)) + dyv
        x2[rows(i), :] = dx
        do = dx.astype(bf)
        h1[rows(i), :] = do

        def sm(v):
            return jnp.sum(v, axis=0, keepdims=True) * one

        vg[2:3, :] += sm(dh * xh)
        vg[3:4, :] += sm(dh)
        vg[7:8, :] += sm(do.astype(f32))
        vg[12:13, :] += sm(dyv)
        invd[rows(i), :] = dot_nt(do, wo[mine, :]) * invd[rows(i), :]

    for q in (3, 1):
        r1_mid(1, q)
    ag_sends(1)
    for m in range(3):
        ms = slice(m * 256, m * 256 + 256)
        w[ms, G1 + 1152 : G1 + 1536] = dot(attt[ms, :], h1[:, mine]).astype(bf)
    w[:, G1 + 1536 : G1 + 1664] = jnp.zeros((768, 128), bf)
    for q in (2, 0):
        r1_mid(1, q)

    dproj = act

    @pl.loop(0, 3)
    def _(p):
        lanes = pl.ds(at(p * 128), 128)
        kl = pl.ds(at(384 + p * 128), 128)
        vl = pl.ds(at(768 + p * 128), 128)
        bq, bk = feature_maps(p)
        dst = [None, None]
        gq = jnp.zeros((128, 128), f32)
        gk = jnp.zeros((128, 128), f32)
        for i in (3, 2, 1, 0):
            rs = slice(i * 256, i * 256 + 256)
            dn = invd[rs, lanes]
            dd = roll64(-(dn * attf[rs, pl.ds(at(own + p * 128), 128)].astype(f32)))
            v = qkv[rs, vl]
            qm, km, same = same_doc(segc, i)
            dq, dk, dv = [], [], []
            for h in range(2):
                mh = m0 == (h == 0)
                vx = jnp.where(mh, v, jnp.ones_like(v))
                dx = jnp.where(mh, dn, dd).astype(bf)
                qq = qf[2 * p + h, rs, :]
                kk = kf[2 * p + h, rs, :]
                a_t = (dot_nt(kk, qq) * maskt[i]).astype(bf)
                da = (dot_nt(dx, vx) * mask[i]).astype(bf)
                da_t = (dot_nt(vx, dx) * maskt[i]).astype(bf)
                gqf = dot(da, kk)
                gkf = dot(da_t, qq)
                gv = dot(a_t, dx)
                if i < 3:
                    ds = dst[h].astype(bf)
                    gkf = gkf + dot_nt(vx, ds) * km
                    gv = gv + dot(kk, ds) * km
                if i > 0:
                    gqf = gqf + dot_nt(dx, st[2 * p + h, i - 1]) * qm
                    new = dot_tn((qq.astype(f32) * qm).astype(bf), dx)
                    dst[h] = new if i == 3 else new + same * dst[h]
                dq.append(gqf)
                dk.append(gkf)
                dv.append(gv)
            zq = soft_back(qf[2 * p, rs, :], qf[2 * p + 1, rs, :], dq[0], dq[1], m0, ones)
            zk = soft_back(kf[2 * p, rs, :], kf[2 * p + 1, rs, :], dk[0], dk[1], m0, ones)
            gq = gq + dot_tn(qkv[rs, lanes], zq)
            gk = gk + dot_tn(qkv[rs, kl], zk)
            dproj[rs, lanes] = dot_nt(zq, bq).astype(bf)
            dproj[rs, kl] = dot_nt(zk, bk).astype(bf)
            dproj[rs, vl] = jnp.where(m0, dv[0], dv[1]).astype(bf)
        top = lax.broadcasted_iota(jnp.int32, (128, 128), 0) < 64
        ml = low_lanes((128, 128))
        w[pl.ds(at(own + p * 128), 128), G1 + 1536 : G1 + 1664] = jnp.where(
            top, jnp.where(ml, gq, roll64(gk)), jnp.where(ml, roll64(gq), gk)
        ).astype(bf)

        @pl.when(p == 0)
        def _():
            r1_end(1, 3)
            r2_start(1)

        @pl.when(p == 1)
        def _():
            r1_end(1, 1)
            r1_end(1, 2)
            r2_mid(1)

    for n in range(3):
        ns = slice(n * 384, n * 384 + 384)
        for m in range(3):
            ms = slice(m * 256, m * 256 + 256)
            w[ms, G1 + n * 384 : G1 + n * 384 + 384] = dot(h1t[ms, :], dproj[:, ns]).astype(bf)
        vg[4 + n : 5 + n, mine] = jnp.sum(dproj[:, ns].astype(f32), axis=0, keepdims=True)
    for k in range(2):
        vg[pl.ds(8 + 2 * c + k, 1), :] = gb[0:1, k * 768 : k * 768 + 768]
    for q in (3, 1, 2, 0):
        r1_start(0, q)
    for i in (5, 6, 7):
        ex(i, dh2p.at[:, 0:256], dh2o.at[:, 0:256]).wait_send()
    for n in range(3):
        ns = slice(n * 256, n * 256 + 256)

        @pl.loop(0, 4)
        def _(i):
            dh2p[rows(i), ns] = dot_nt(dproj[rows(i), 0:1152], w[ns, 0:1152]).astype(bf)

        ex(8 + n, dh2p.at[pl.ds(away, 512), ns], dh1o.at[:, ns]).start()
    r1_end(1, 0)
    r2_end(1)
    y_start(1)
    for q in (3, 1):
        r1_mid(0, q)
    for n in range(3):
        ns = slice(n * 256, n * 256 + 256)
        ex(8 + n, dh2p.at[pl.ds(away, 512), ns], dh1o.at[:, ns]).wait_recv()

    @pl.loop(0, 2)
    def _(i):
        rs = pl.ds(at(half + i * 256), 256)
        cen, r = norm_stats(xr[rs, :].astype(f32))
        xh = cen * r
        dh = dh2p[rs, :].astype(f32) + dh1o[rows(i), :].astype(f32)
        dx = dh * vec[0:1, :]
        dx = r * (dx - jnp.mean(dx, -1, keepdims=True) - xh * jnp.mean(dx * xh, -1, keepdims=True))
        dh2p[rs, :] = (dx + x2[rs, :]).astype(bf)
        vg[0:1, :] += jnp.sum(dh * xh, axis=0, keepdims=True)
        vg[1:2, :] += jnp.sum(dh, axis=0, keepdims=True)

    vsrc[...] = jnp.transpose(jnp.concatenate([vg[...], jnp.zeros((112, 768), f32)], axis=0))

    def vx_(k, recv=False):
        t, dev = plane_peer(k)
        slot = plane_peer(-k)[0] if recv else pln
        return rcopy(vsrc.at[pl.ds(at(t * 48, 16), 48)], vrc.at[slot], vxs.at[k], vxr.at[k], dev)

    for k in range(1, 16):
        vx_(k).start()
    for q in (2, 0):
        r1_mid(0, q)
    tok_start(1)
    r1_end(0, 3)
    r2_start(0)
    r1_end(0, 1)
    r1_end(0, 2)
    r2_mid(0)
    r1_end(0, 0)
    for k in range(1, 16):
        vx_(k, True).wait_recv()

    def sums(gp):
        for k in range(1, 8):
            ycp(gp, k, True).wait_recv()
        tot = jnp.zeros((1, 1), f32)
        for d, wd, sr, sp in PIECES:
            if (d >= G1) != (gp == 1):
                continue
            for cc in range(2 if sp else 1):
                srcs = [2 * j + cc for j in range(4)] if sp else range(8)
                v = sum(yr[j, 0:6, d : d + wd].astype(f32) for j in srcs)
                pg_o[:, sr + sp * cc : sr + sp * cc + wd] = v
                tot = tot + jnp.sum(jnp.sum(v * v, axis=1, keepdims=True), axis=0, keepdims=True)
        return tot

    total = sums(1)
    r2_end(0)
    y_start(0)
    total = total + sums(0)
    V = sum(yr[j, :, 1664:1792].astype(f32) for j in range(8))
    vs_o[...] = V
    total = total + jnp.sum(jnp.sum(V[0:6] * V[0:6], axis=1, keepdims=True), axis=0, keepdims=True)
    n1[s] = jnp.broadcast_to(total, (8, 128))

    def nc1(k, recv=False):
        slot = seq_peer(-k)[0] if recv else s
        return rcopy(n1.at[s], n1.at[slot], n1s.at[k], n1r.at[k], seq_peer(k)[1])

    def nc2(k, recv=False):
        slot = plane_peer(-k)[0] if recv else pln
        return rcopy(n2.at[pln], n2.at[slot], n2s.at[k], n2r.at[k], plane_peer(k)[1])

    for k in range(1, 8):
        nc1(k).start()
    for k in range(1, 8):
        nc1(k, True).wait_recv()
    n2[pln] = sum(n1[j] for j in range(8))
    for k in range(1, 16):
        nc2(k).start()
    ag_sends(0)
    for gp in range(2):
        for k in range(1, 8):
            st0(gp, k).wait_send()
            ycp(gp, k).wait_send()
        for p in range(2):
            for kind in range(4):
                c2(gp, p, kind).wait_send()
                for q in range(4):
                    c1(gp, p, q, kind).wait_send()
    for wh in range(2):
        for k in range(1, 4):
            res(wh, k).wait_send()
        for k in range(4):
            sib(wh, k).wait_send()
        tok_wait(wh)
    for k in range(1, 8):
        sgc(k).wait_send()
        nc1(k).wait_send()
    ex(0, w.at[:, 1152:1536], wo.at[:, mine]).wait_send()
    for p in range(3):
        ex(1 + p, att_part(p), att_part(p)).wait_send()
    ex(4, outp.at[pl.ds(away, 512)], outo).wait_send()
    for n in range(3):
        ns = slice(n * 256, n * 256 + 256)
        ex(8 + n, dh2p.at[pl.ds(away, 512), ns], dh1o.at[:, ns]).wait_send()
    for k in range(1, 16):
        vx_(k).wait_send()
        nc2(k, True).wait_recv()
        nc2(k).wait_send()
    norm_o[...] = jnp.sqrt(sum(n2[j] for j in range(16)))


def run_layer(par, vt, xin, dyin, sgin):
    V = pl.BlockSpec(memory_space=pltpu.VMEM)
    H = pl.BlockSpec(memory_space=pl.ANY)
    M = pltpu.VMEM
    DM = pltpu.SemaphoreType.DMA
    S = jax.ShapeDtypeStruct
    tok = (T, D)
    return pl.pallas_call(
        layer,
        out_shape=[S((4, 128, D), bf), S((4, 128, D), bf), S((6, 9344), f32), S((8, 128), f32), S((8, 128), f32)],
        in_specs=[V, V, H, H, V],
        out_specs=[V] * 5,
        scratch_shapes=[
            M((D, WC), bf), M((D, D), bf), M(tok, bf), M(tok, bf), M((8, 8, 128), f32), M((2, 8, WC), bf), M((8, 8, WC), bf),
            M((16, D), f32), M(tok, bf), M((D, T), bf), M((T, 3 * HD), bf), M((6, T, 128), bf), M((6, T, 128), bf),
            M((T, HD), f32), M((6, 3, 128, 128), bf), M((T, 128), f32), M((4, 256, 256), f32), M((4, 256, 256), f32), M(tok, bf),
            M(tok, f32), M(tok, bf), M((D, T), bf), M((D, T), bf), M((T, FH), bf), M((T, FH), bf), M(tok, bf), M((512, D), bf),
            M(tok, bf), M(tok, bf), M((512, D), bf), M((D, 2 * FH), bf), M((576, 2 * FH), bf), M((144, 2 * FH), bf),
            M((8, 8, WC), bf), M((8, 8, 128), f32), M((16, 8, 128), f32), M((16, D), f32), M((8, FH), f32),
            M((D, 128), f32), M((16, 48, 128), f32),
            DM((2, 8)), DM((2, 8)), DM((2, 2, 20)), DM((2, 2, 20)), DM((2, 8)), DM((2, 8)), DM((8,)), DM((8,)),
            DM((11,)), DM((11,)), DM((2, 2, 4, 4)), DM((2, 2, 4, 4)), DM((2, 2, 4)), DM((2, 2, 4)), DM((2, 8)), DM((2, 8)),
            DM((8,)), DM((8,)), DM((16,)), DM((16,)), DM((2, 8)), DM((2, 8)), DM((16,)), DM((16,)), DM((2,)),
        ],
        compiler_params=pltpu.CompilerParams(collective_id=0, has_side_effects=True, vmem_limit_bytes=64 * 2**20 - 2**17),
        name="layer",
    )(par, vt, xin, dyin, sgin)


def adamw(weight, grad, m, v, scale, rate, decay):
    grad = grad * scale
    m = 0.5 * m + 0.5 * grad
    v = 0.5 * v + 0.5 * grad * grad
    return grad, weight - rate * (m / (jnp.sqrt(v) + 1e-8) + decay * weight), m, v


def body(inputs, segment_ids, out_grad, params, vectors, params_m, params_v, vectors_m, vectors_v):
    vt = jnp.pad(vectors.T, ((0, 0), (0, 115)))
    sgin = jnp.broadcast_to(segment_ids.astype(f32)[:, None, :], (4, 8, 128))
    out, ig, pg, vs, norm = run_layer(params, vt, inputs, out_grad, sgin)
    scale = 1.0 / jnp.maximum(norm[0, 0], 1.0)
    p = adamw(params, pg, params_m, params_v, scale, 0.05, 0.1)
    q = adamw(vectors, vs[0:6, 0:13].T, vectors_m, vectors_v, scale, 0.2, 0.0)
    return (out, ig.astype(f32), norm[0, 0:1]) + p + q


def solution(mesh):
    torus = Mesh(mesh.devices.reshape(4, 4, 4, 2), ("x", "z", "y", "c"))
    row, seq, every = ("x", "z"), ("y", "c"), ("x", "z", "y", "c")
    tok, mat, vec = P(row, seq, None), P(every, None), P(None, every)
    return jax.shard_map(
        body,
        mesh=torus,
        in_specs=(tok, P(row, seq), tok, mat, vec, mat, mat, vec, vec),
        out_specs=(tok, tok, P(), mat, mat, mat, mat, vec, vec, vec, vec),
        check_vma=False,
    )
```

```python
import jax
import jax.numpy as jnp
from jax import lax
from jax.experimental import pallas as pl
from jax.experimental.pallas import tpu as pltpu
from jax.sharding import Mesh
from jax.sharding import PartitionSpec as P

f32 = jnp.float32
bf = jnp.bfloat16
MESH = pl.DeviceIdType.MESH
T, D, HD, FH = 1024, 768, 384, 1536
WC = 4864
GC = 1664
PIECES = (
    (0, 128, 0, 384), (128, 128, 768, 384), (256, 128, 1536, 384), (384, 128, 3072, 0),
    (640, 128, 128, 384), (768, 128, 896, 384), (896, 128, 1664, 384),
    (1024, 128, 256, 384), (1152, 128, 1024, 384), (1280, 128, 1792, 384), (1408, 384, 2304, 384),
    (1792, 768, 3200, 1536), (2560, 768, 6272, 1536), (3328, 768, 3968, 1536), (4096, 768, 7040, 1536),
)
VAT = 512
WOAT = 1408
FAT = 384
STAGE = ((0, 640), (640, 1792), (1792, 4864))
GATHER = (
    ((0, 128, 256), (256, 384, 640)),
    ((640, 896, 1152), (1152, 1408, 1792)),
    ((1792, 2176, 2560), (2560, 2944, 3328)),
    ((3328, 3712, 4096), (4096, 4480, 4864)),
)
GPIECES = (
    (0, 384, 2304, 384), (384, 128, 0, 384), (512, 128, 768, 384), (640, 128, 1536, 384),
    (768, 128, 128, 384), (896, 128, 896, 384), (1024, 128, 1664, 384),
    (1152, 128, 256, 384), (1280, 128, 1024, 384), (1408, 128, 1792, 384), (1536, 128, 3072, 0),
    (1792, 768, 3200, 1536), (2560, 768, 6272, 1536), (3328, 768, 3968, 1536), (4096, 768, 7040, 1536),
)
REDUCE = (((1792, 2176, 2560), (2560, 2944, 3328)), ((3328, 3712, 4096), (4096, 4480, 4864)))
DIRECT = (((0, 384), (384, 768)), ((768, 896), (896, 1152)), ((1152, 1408), (1408, 1664)))
YCOLS = ((1792, 4864), (0, 1152), (1152, 1792))
FAR = (0, -1, 1, 2)
BIG = 3.0e38


def dot(a, b):
    return lax.dot_general(a, b, (((1,), (0,)), ((), ())), preferred_element_type=f32)


def dot_nt(a, b):
    return lax.dot_general(a, b, (((1,), (1,)), ((), ())), preferred_element_type=f32)


def dot_tn(a, b):
    return lax.dot_general(a, b, (((0,), (0,)), ((), ())), preferred_element_type=f32)


def at(v, m=128):
    return pl.multiple_of(v, m)


def rows(i, n=256):
    return pl.ds(at(i * n), n)


def low_lanes(shape):
    return lax.broadcasted_iota(jnp.int32, shape, len(shape) - 1) < 64


def roll64(v):
    return pltpu.roll(v, 64, 1)


def slab(xx, zz):
    return at((lax.rem(xx + 8, 4) * 4 + lax.rem(zz + 8, 4)) * 48, 16)


def norm_stats(v):
    mu = jnp.mean(v, axis=-1, keepdims=True)
    cen = v - mu
    return cen, lax.rsqrt(jnp.mean(cen * cen, axis=-1, keepdims=True) + 1e-5)


def seg_ones():
    a = lax.broadcasted_iota(jnp.int32, (128, 128), 0) < 64
    return (a == low_lanes((128, 128))).astype(bf)


def feats(z, m0, ones):
    mx = jnp.where(m0, jnp.max(jnp.where(m0, z, -BIG), -1, keepdims=True), jnp.max(jnp.where(m0, -BIG, z), -1, keepdims=True))
    mn = jnp.where(m0, jnp.min(jnp.where(m0, z, BIG), -1, keepdims=True), jnp.min(jnp.where(m0, BIG, z), -1, keepdims=True))
    ep = jnp.exp(z - mx).astype(bf)
    en = jnp.exp(mn - z).astype(bf)
    fp = ep.astype(f32) / dot(ep, ones)
    fn = roll64(en.astype(f32) / dot(en, ones))
    return jnp.where(m0, fp, fn).astype(bf), jnp.where(m0, fn, fp).astype(bf)


def soft_back(fe, fo, de, do, m0, ones):
    fe = fe.astype(f32)
    fo = fo.astype(f32)
    fp = jnp.where(m0, fe, fo)
    fr = jnp.where(m0, fo, fe)
    tp = fp * jnp.where(m0, de, do)
    tr = fr * jnp.where(m0, do, de)

    def total(t):
        hi = t.astype(bf)
        return dot(hi, ones) + dot((t - hi.astype(f32)).astype(bf), ones)

    return ((tp - fp * total(tp)) - roll64(tr - fr * total(tr))).astype(bf)


def same_doc(segc, i):
    sc = segc[i * 256 : i * 256 + 256, :]
    last = segc[i * 256 + 255 : i * 256 + 256, :]
    km = (sc == last).astype(f32)
    if i == 0:
        return None, km, None
    prev = segc[i * 256 - 1 : i * 256, :]
    return (sc == prev).astype(f32), km, (last == prev).astype(f32)


def layer(
    par, vt, xin, dyin, sgin,
    out_o, ig_o, pg_o, vs_o, norm_o,
    w, wo, xr, dyr, sg, sgb, wire, rcv, vec, h1, h1t, qkv, qf, kf, invd, st, segc, mask, maskt, attf,
    x2, h2, h2t, dyt, act, du, outo, dh2o, dh1o, g, r1, r2, gq, d1, d2, gf, yr, n1, n2, vg, gb, vsrc, v1, v2,
    ss, s0r, sgr, rsr, sbr, agr, t1r, t2r, d1r, d2r, ysr, vxr, n1r, n2r, exs, exr, tks, tkr, los,
):
    x, z, y, c = (lax.axis_index(a) for a in ("x", "z", "y", "c"))
    s = y * 2 + c
    pln = x * 4 + z
    own = at(c * 384)

    def rcopy(src, dst, ss, rs, dev):
        return pltpu.make_async_remote_copy(src, dst, ss, rs, device_id=dev, device_id_type=MESH)

    def take(ref, sem):
        rcopy(ref, ref, sem, sem, other).wait_recv()

    def sent(ref, i):
        rcopy(ref, ref, ss.at[i], ss.at[i], other).wait_send()

    def seq_peer(k):
        t = lax.rem(s + k + 8, 8)
        return t, {"y": t // 2, "c": lax.rem(t, 2)}

    def axis_peer(a, k):
        return {("x", "z")[a]: lax.rem((x, z)[a] + k + 4, 4)}

    other = {"c": 1 - c}

    bar = pltpu.get_barrier_semaphore()
    for k in range(1, 8):
        pl.semaphore_signal(bar, inc=1, device_id=seq_peer(k)[1], device_id_type=MESH)
    for a in range(2):
        for k in range(1, 4):
            pl.semaphore_signal(bar, inc=1, device_id=axis_peer(a, k), device_id_type=MESH)
    for cc in range(2):
        wire[cc, :, :] = jnp.zeros((8, WC), bf)
        for d, wd, sr, sp in PIECES:
            wire[cc, 0:6, d : d + wd] = par[:, sr + sp * cc : sr + sp * cc + wd].astype(bf)
        wire[cc, 0:6, VAT : VAT + 13] = vt[...].astype(bf)
    for j in range(4):
        sgb[j] = jnp.broadcast_to(sgin[j : j + 1, :].astype(f32), (8, 128))
    pl.semaphore_wait(bar, 13)

    def st0(gp, k):
        t, dev = seq_peer(k)
        a, b = STAGE[gp]
        return rcopy(wire.at[dev["c"], :, a:b], rcv.at[s, :, a:b], ss.at[0], s0r.at[gp], dev)

    def sgc(k):
        t, dev = seq_peer(k)
        return rcopy(sgb.at[t // 2], sg.at[s], ss.at[1], sgr.at[0], dev)

    pairs = ((xin, xr), (dyin, dyr))

    def res(wh, k):
        src, dst = pairs[wh]
        j = lax.rem(y + k, 4)
        return rcopy(src.at[j], dst.at[rows(s, 128)], ss.at[2], rsr.at[wh], {"y": j})

    def keep(wh):
        src, dst = pairs[wh]
        return pltpu.make_async_copy(src.at[y], dst.at[rows(s, 128)], los.at[wh])

    def sib(wh, k):
        ref = pairs[wh][1].at[rows(lax.rem(y - k + 4, 4) * 2 + c, 128)]
        return rcopy(ref, ref, ss.at[3], sbr.at[wh], other)

    def res_start(wh):
        keep(wh).start()
        for k in (2, 1, 3):
            res(wh, k).start()

    def res_pass(wh):
        keep(wh).wait()
        sib(wh, 0).start()
        take(pairs[wh][1].at[0:384], rsr.at[wh])
        for k in range(1, 4):
            sib(wh, k).start()

    def res_end(wh):
        take(pairs[wh][1].at[0:512], sbr.at[wh])

    def pos(p, d1, d2):
        return slab(x + d1, z + d2) if p == 0 else slab(x + d2, z + d1)

    def along(p, phase, way):
        return axis_peer((p + phase) % 2, way)

    def cut(table, gp, p, h):
        lo, mid, hi = table[gp][p]
        return ((lo, hi), (lo, mid), (mid, hi))[h]

    def ag(gp, p, sem, d1, d2, h, phase, way):
        a, b = cut(GATHER, gp, p, h)
        ref = w.at[pl.ds(pos(p, d1, d2), 48), a:b]
        return rcopy(ref, ref, ss.at[4], agr.at[gp, sem], along(p, phase, way))

    def ag_take(gp, sem):
        take(w.at[0 : (96, 48)[sem % 2], GATHER[gp][0][0] : GATHER[gp][1][2]], agr.at[gp, sem])

    def p2send(gp, q):
        for p in range(2):
            ag(gp, p, 2 + 2 * q, FAR[q], 0, 0, 1, 1).start()
            ag(gp, p, 2 + 2 * q, FAR[q], 0, 0, 1, -1).start()

    def ag_d(gp, q):
        ag_take(gp, 2 + 2 * q)
        for p in range(2):
            ag(gp, p, 3 + 2 * q, FAR[q], -1, 1, 1, 1).start()
            ag(gp, p, 3 + 2 * q, FAR[q], 1, 2, 1, -1).start()

    def ag_a(gp):
        for p in range(2):
            ag(gp, p, 0, 0, 0, 0, 0, 1).start()
            ag(gp, p, 0, 0, 0, 0, 0, -1).start()
        p2send(gp, 0)

    def ag_b(gp):
        ag_take(gp, 0)
        for p in range(2):
            ag(gp, p, 1, -1, 0, 1, 0, 1).start()
            ag(gp, p, 1, 1, 0, 2, 0, -1).start()
        p2send(gp, 1)
        p2send(gp, 2)

    def ag_c(gp):
        ag_take(gp, 1)
        p2send(gp, 3)
        ag_d(gp, 0)

    def ag_e(gp):
        for q in range(4):
            ag_take(gp, 3 + 2 * q)

    rr = lax.broadcasted_iota(jnp.int32, (48, 64), 0)
    rc = lax.broadcasted_iota(jnp.int32, (48, 64), 1)
    spread = ((lax.rem(rr, 6) == lax.rem(rc, 8)) & (rr // 6 == rc // 8)).astype(bf)

    def assemble(gp):
        a, b = STAGE[gp]
        take(rcv.at[0:7, :, a:b], s0r.at[gp])
        n = (640, 1152, 768)[gp]
        for lo in range(a, b, n):
            raw = jnp.concatenate([rcv[t, :, lo : lo + n].astype(f32) for t in range(8)], axis=0).astype(bf)
            w[pl.ds(slab(x, z), 48), lo : lo + n] = dot(spread, raw).astype(bf)

    for k in range(1, 8):
        st0(0, k).start()
    for k in range(1, 8):
        st0(1, k).start()
    for k in range(1, 8):
        sgc(k).start()
    res_start(0)
    for k in range(1, 8):
        st0(2, k).start()
    sg[s] = sgb[y]
    rcv[s] = wire[c]
    assemble(0)
    ag_a(0)
    assemble(1)
    ag_a(1)
    ag_b(0)
    take(sg.at[0:7], sgr.at[0])
    for b in range(8):
        segc[b * 128 : b * 128 + 128, :] = jnp.transpose(jnp.broadcast_to(sg[b, 0:1, :], (128, 128)))
    mr = lax.broadcasted_iota(jnp.int32, (256, 256), 0)
    mc = lax.broadcasted_iota(jnp.int32, (256, 256), 1)
    for i in range(4):
        row = jnp.concatenate([sg[2 * i, 0:1, :], sg[2 * i + 1, 0:1, :]], axis=1)
        col = segc[i * 256 : i * 256 + 256, :]
        eq = jnp.concatenate([col, col], axis=1) == row
        mask[i] = jnp.where(eq & (mc <= mr), 1.0, 0.0).astype(bf)
        maskt[i] = jnp.where(eq & (mr <= mc), 1.0, 0.0).astype(bf)
    ag_c(0)
    for q in (1, 2):
        ag_d(0, q)
    res_pass(0)
    ag_b(1)
    ag_d(0, 3)
    res_end(0)
    res_start(1)

    @pl.loop(0, 4)
    def _(i):
        cen, r = norm_stats(xr[rows(i), :].astype(f32))
        x2[rows(i), :] = cen * r

    ag_c(1)
    assemble(2)
    ag_a(2)
    ag_a(3)
    ag_e(0)

    def ex(i, src, dst):
        return rcopy(src, dst, exs.at[i], exr.at[i], other)

    mine = pl.ds(own, 384)

    vec[...] = jnp.transpose(w[:, VAT : VAT + 128].astype(f32))[0:16]

    @pl.loop(0, 4)
    def _(i):
        h = (x2[rows(i), :] * vec[0:1, :] + vec[1:2, :]).astype(bf)
        h1[rows(i), :] = h
        h1t[:, rows(i)] = jnp.transpose(x2[rows(i), :].astype(bf))

    ones = seg_ones()
    m0 = low_lanes((256, 128))

    def feature_maps(p):
        F = w[pl.ds(at(own + p * 128), 128), FAT : FAT + 128].astype(f32)
        R = roll64(F)
        top = lax.broadcasted_iota(jnp.int32, (128, 128), 0) < 64
        ml = low_lanes((128, 128))
        zz = jnp.zeros_like(F)
        bq = jnp.where(top & ml, F, jnp.where(top | ml, zz, R))
        bk = jnp.where(top & ml, R, jnp.where(top | ml, zz, F))
        return bq.astype(bf), bk.astype(bf)

    def pump(table, p, i):
        for (pp, ii), todo in table.items():
            if ii == i:

                @pl.when(p == pp)
                def _():
                    for t in todo:
                        t[0](*t[1:])

    def wo_start():
        ex(0, w.at[:, WOAT : WOAT + 384], wo.at[:, mine]).start()
        wo[:, mine] = w[:, WOAT : WOAT + 384]

    forward = {
        (0, 0): ((ag_d, 1, 1), (ag_d, 1, 2), (ag_b, 2)),
        (0, 1): ((ag_d, 1, 3),),
        (0, 2): ((ag_b, 3),),
        (0, 3): ((ag_e, 1), (wo_start,)),
        (1, 0): ((ag_c, 2),),
        (1, 1): ((ag_c, 3),),
        (1, 2): ((ag_d, 2, 1), (ag_d, 2, 2)),
        (1, 3): ((ag_d, 3, 1), (res_pass, 1)),
        (2, 0): ((ag_d, 2, 3), (ag_d, 3, 2)),
        (2, 2): ((ag_d, 3, 3),),
    }

    def att_part(p):
        return attf.at[:, pl.ds(at(own + p * 128), 128)]

    @pl.loop(0, 3)
    def _(p):
        lanes = pl.ds(at(p * 128), 128)
        bq, bk = feature_maps(p)
        base = at(p * 384 + 256 * jnp.minimum(p, 1))
        part = pl.ds(at(own + p * 128), 128)
        bias = jnp.concatenate([vec[4:5, part], vec[5:6, part], vec[6:7, part]], axis=1)
        state = [None, None]
        for i in range(4):
            rs = slice(i * 256, i * 256 + 256)
            pr = (dot(h1[rs, :], w[:, pl.ds(base, 384)]) + bias).astype(bf)
            qkv[rs, pl.ds(at(p * 384), 384)] = pr
            qe, qo = feats(dot(pr[:, 0:128], bq), m0, ones)
            ke, ko = feats(dot(pr[:, 128:256], bk), m0, ones)
            v = pr[:, 256:384]
            qm, km, same = same_doc(segc, i)
            outs = []
            for h, (qq, kk) in enumerate(((qe, ke), (qo, ko))):
                vx = jnp.where(m0 == (h == 0), v, jnp.ones_like(v))
                qf[2 * p + h, rs, :] = qq
                kf[2 * p + h, rs, :] = kk
                o = dot((dot_nt(qq, kk) * mask[i].astype(f32)).astype(bf), vx)
                if i > 0:
                    sb = state[h].astype(bf)
                    st[2 * p + h, i - 1] = sb
                    o = o + dot(qq, sb) * qm
                if i < 3:
                    sn = dot_tn((kk.astype(f32) * km).astype(bf), vx)
                    state[h] = sn if i == 0 else sn + same * state[h]
                outs.append(o)
            num = jnp.where(m0, outs[0], outs[1])
            inv = 1.0 / roll64(jnp.where(m0, outs[1], outs[0]))
            invd[rs, lanes] = inv
            attf[rs, part] = (num * inv).astype(bf)
            if i == 3:
                ex(1 + p, att_part(p), att_part(p)).start()
            pump(forward, p, i)

    ag_e(2)
    res_end(1)
    ex(0, w.at[:, WOAT : WOAT + 384], wo.at[:, pl.ds(at((1 - c) * 384), 384)]).wait_recv()
    for p in range(3):
        part = attf.at[:, pl.ds(at((1 - c) * 384 + p * 128), 128)]
        ex(1 + p, part, part).wait_recv()

    @pl.loop(0, 4)
    def _(i):
        v = xr[rows(i), :].astype(f32) + dot(attf[rows(i), :], wo[...]) + vec[7:8, :]
        x2[rows(i), :] = v
        cen, r = norm_stats(v)
        h = (cen * r * vec[2:3, :] + vec[3:4, :]).astype(bf)
        h2[rows(i), :] = h
        h2t[:, rows(i)] = jnp.transpose(h)
        dyt[:, rows(i)] = jnp.transpose(dyr[rows(i), :])

    k0 = 0.7978845608028654
    k1 = 0.044715

    def mlp(j):
        far = at(1792 + (j // 3) * 768 + j * 256)
        cu = pl.ds(far, 256)
        cd = pl.ds(at(far + 768), 256)
        gu = pl.ds(at(far - 1792), 256)
        gd = pl.ds(at(far - 1024), 256)
        cj = pl.ds(at(j * 256), 256)
        off = c * FH + j * 256
        bu = vec[pl.ds(8 + off // D, 1), pl.ds(at(lax.rem(off, D)), 256)]

        @pl.loop(0, 4)
        def _(i):
            u = dot(h2[rows(i), :], w[:, cu]) + bu
            u2 = u * u
            t = jnp.tanh(k0 * (u + k1 * u2 * u))
            act[rows(i), cj] = (0.5 * u * (1.0 + t)).astype(bf)
            da = dot(dyr[rows(i), :], w[:, cd])
            gp = 0.5 * (1.0 + t) + 0.5 * u * (1.0 - t * t) * (k0 * (1.0 + (3 * k1) * u2))
            d = (gp * da).astype(bf)
            du[rows(i), cj] = d
            gb[0:1, cj] = gb[0:1, cj] + jnp.sum(d.astype(f32), axis=0, keepdims=True)

        for m in range(3):
            ms = slice(m * 256, m * 256 + 256)
            g[ms, gd] = dot(dyt[ms, :], act[:, cj]).astype(bf)
            g[ms, gu] = dot(h2t[ms, :], du[:, cj]).astype(bf)

    def gref(gp, p, d1, d2, h):
        a, b = cut(REDUCE, gp, p, h)
        r = pl.ds(pos(p, d1, d2), 48)
        return g.at[r, a - 1792 : b - 1792]

    def land(gp, p, slot, h):
        a, b = cut(REDUCE, gp, p, h)
        r = slice(slot % 12 * 48, slot % 12 * 48 + 48)
        return (r1 if slot < 12 else r2).at[r, a - 1792 : b - 1792]

    HALF = (1, 2, 0, 0)
    SLOT = (0, 0, 1, 2)
    HOP = (2, 2, 1, -1)

    def c1(gp, p, q, kind):
        h = HALF[kind]
        return rcopy(gref(gp, p, FAR[q], HOP[kind], h), land(gp, p, q * 3 + SLOT[kind], h), ss.at[5], t1r.at[gp, q, kind // 2], along(p, 1, (1, -1)[kind % 2]))

    def c2(gp, p, kind):
        h = HALF[kind]
        return rcopy(gref(gp, p, HOP[kind], 0, h), land(gp, p, 12 + SLOT[kind], h), ss.at[5], t2r.at[gp, kind // 2], along(p, 0, (1, -1)[kind % 2]))

    def tree_take(gp, n, sem):
        take(r1.at[0:n, REDUCE[gp][0][0] - 1792 : REDUCE[gp][1][2] - 1792], sem)

    def acc(dst, *srcs):
        t = dst[...].astype(f32)
        for r in srcs:
            t = t + r[...].astype(f32)
        dst[...] = t.astype(bf)

    def r1_start(gp, q):
        for p in range(2):
            c1(gp, p, q, 0).start()
            c1(gp, p, q, 1).start()

    def r1_mid(gp, q):
        tree_take(gp, 48, t1r.at[gp, q, 0])
        for p in range(2):
            for kind in range(2):
                acc(gref(gp, p, FAR[q], (1, -1)[kind], 1 + kind), land(gp, p, q * 3, 1 + kind))
                c1(gp, p, q, 2 + kind).start()

    def r1_end(gp, q):
        tree_take(gp, 96, t1r.at[gp, q, 1])
        for p in range(2):
            acc(gref(gp, p, FAR[q], 0, 0), land(gp, p, q * 3 + 1, 0), land(gp, p, q * 3 + 2, 0))

    def r2_start(gp):
        for p in range(2):
            c2(gp, p, 0).start()
            c2(gp, p, 1).start()

    def r2_mid(gp):
        tree_take(gp, 48, t2r.at[gp, 0])
        for p in range(2):
            for kind in range(2):
                acc(gref(gp, p, (1, -1)[kind], 0, 1 + kind), land(gp, p, 12, 1 + kind))
                c2(gp, p, 2 + kind).start()

    def r2_end(gp):
        tree_take(gp, 96, t2r.at[gp, 1])
        for p in range(2):
            acc(gref(gp, p, 0, 0, 0), land(gp, p, 13, 0), land(gp, p, 14, 0))

    tr = lax.broadcasted_iota(jnp.int32, (64, 48), 0)
    tc = lax.broadcasted_iota(jnp.int32, (64, 48), 1)
    split = ((lax.rem(tc, 6) == lax.rem(tr, 8)) & (tc // 6 == tr // 8)).astype(bf)

    def dcp(gp, p, phase, e):
        a, b = DIRECT[gp][p]
        first = p == 0
        if phase == 0:
            t = lax.rem((z if first else x) + e, 4)
            src = gq.at[:, t, :, a:b] if first else gq.at[t, :, :, a:b]
            return rcopy(src, d1.at[e - 1, :, :, a:b], ss.at[6], d1r.at[gp], axis_peer(1 if first else 0, e))
        t = lax.rem((x if first else z) + e, 4)
        src = gq.at[t, z, :, a:b] if first else gq.at[x, t, :, a:b]
        return rcopy(src, d2.at[e - 1, :, a:b], ss.at[6], d2r.at[gp], axis_peer(0 if first else 1, e))

    def d_start(gp):
        for e in (2, 1, 3):
            for p in range(2):
                dcp(gp, p, 0, e).start()

    def d_mid(gp):
        take(d1.at[:, :, :, DIRECT[gp][0][0] : DIRECT[gp][1][1]], d1r.at[gp])
        for p in range(2):
            a, b = DIRECT[gp][p]
            for k in range(4):
                dst = gq.at[k, z, :, a:b] if p == 0 else gq.at[x, k, :, a:b]
                acc(dst, *[d1.at[e, k, :, a:b] for e in range(3)])
            for e in (2, 1, 3):
                dcp(gp, p, 1, e).start()

    def d_end(gp):
        take(d2.at[:, :, DIRECT[gp][0][0] : DIRECT[gp][1][1]], d2r.at[gp])
        for p in range(2):
            a, b = DIRECT[gp][p]
            acc(gq.at[x, z, :, a:b], *[d2.at[e, :, a:b] for e in range(3)])

    def ycp(gp, k):
        t, dev = seq_peer(k)
        a, b = YCOLS[gp]
        return rcopy(rcv.at[t, :, a:b], yr.at[s, :, a:b], ss.at[7], ysr.at[gp], dev)

    def deal(a, b, part):
        out = dot(split, part).astype(bf)
        for t in range(8):
            rcv[t, :, a:b] = out[8 * t : 8 * t + 8]

    def y_start(gp):
        a, b = YCOLS[gp]
        if gp == 0:
            for lo in range(0, 3072, 768):
                deal(1792 + lo, 2560 + lo, g[pl.ds(slab(x, z), 48), lo : lo + 768])
        elif gp == 1:
            deal(0, 1152, gq[x, z, :, 0:1152])
        else:
            deal(1152, 1664, gq[x, z, :, 1152:1664])
            deal(1664, 1792, (vsrc[pl.ds(slab(x, z), 48), :] + (v2[0] + v2[1] + v2[2])).astype(bf))
        for k in range(1, 8):
            ycp(gp, k).start()
        yr[s, :, a:b] = rcv[s, :, a:b]

    gb[...] = jnp.zeros_like(gb)
    pl.loop(0, 3)(mlp)
    for q in (3, 1, 2, 0):
        r1_start(0, q)
    ag_e(3)
    pl.loop(3, 6)(mlp)
    for q in (3, 1, 2, 0):
        r1_start(1, q)
    for q in (3, 1, 2, 0):
        r1_mid(0, q)

    outp, dh2p, dh1p = h2, h1, du.at[:, 0:768]
    half = at(c * 512)
    away = at((1 - c) * 512)

    @pl.loop(0, 4)
    def _(i):
        for n in range(3):
            ns = slice(n * 256, n * 256 + 256)
            outp[rows(i), ns] = (dot_nt(act[rows(i), 0:768], w[ns, 2560:3328]) + dot_nt(act[rows(i), 768:1536], w[ns, 4096:4864])).astype(bf)

    ex(4, outp.at[pl.ds(away, 512)], outo).start()
    for n in range(3):
        ns = slice(n * 256, n * 256 + 256)

        @pl.loop(0, 4)
        def _(i):
            dh2p[rows(i), ns] = (dot_nt(du[rows(i), 0:768], w[ns, 1792:2560]) + dot_nt(du[rows(i), 768:1536], w[ns, 3328:4096])).astype(bf)

        ex(5 + n, dh2p.at[:, ns], dh2o.at[:, ns]).start()
    ex(4, outp.at[pl.ds(away, 512)], outo).wait_recv()

    @pl.loop(0, 2)
    def _(i):
        rs = pl.ds(at(half + i * 256), 256)
        outp[rs, :] = (x2[rs, :] + outp[rs, :].astype(f32) + outo[rows(i), :].astype(f32) + vec[12:13, :]).astype(bf)

    toks = ((outp, out_o), (dh1p, ig_o))

    def tok(wh, k, recv=False):
        src, dst = toks[wh]
        t, dev = seq_peer(k)
        row = (seq_peer(-k)[0] // 2) if recv else y
        return rcopy(src.at[pl.ds(at(half + lax.rem(t, 4) * 128), 128)], dst.at[row], tks.at[wh, k], tkr.at[wh, k], dev)

    def tok_start(wh):
        for k in range(1, 8):

            @pl.when(seq_peer(k)[0] // 4 == c)
            def _():
                tok(wh, k).start()

        src, dst = toks[wh]

        @pl.when(s // 4 == c)
        def _():
            dst[y] = src[pl.ds(at(half + lax.rem(s, 4) * 128), 128), :]

    def tok_wait(wh):
        for k in range(1, 8):

            @pl.when(lax.rem(seq_peer(-k)[0], 2) == s // 4)
            def _():
                tok(wh, k, True).wait_recv()

        for k in range(1, 8):

            @pl.when(seq_peer(k)[0] // 4 == c)
            def _():
                tok(wh, k).wait_send()

    tok_start(0)

    vg[...] = jnp.zeros_like(vg)
    one = (c == 0).astype(f32)
    attt = dyt

    @pl.loop(0, 4)
    def _(i):
        attt[:, rows(i)] = jnp.transpose(attf[rows(i), :])

    for n in range(3):
        ns = slice(n * 256, n * 256 + 256)
        ex(5 + n, dh2p.at[:, ns], dh2o.at[:, ns]).wait_recv()
        ex(5 + n, dh2p.at[:, ns], dh2o.at[:, ns]).wait_send()

    @pl.loop(0, 4)
    def _(i):
        cen, r = norm_stats(x2[rows(i), :])
        xh = cen * r
        dh = dh2p[rows(i), :].astype(f32) + dh2o[rows(i), :].astype(f32)
        dyv = dyr[rows(i), :].astype(f32)
        dx = dh * vec[2:3, :]
        dx = r * (dx - jnp.mean(dx, -1, keepdims=True) - xh * jnp.mean(dx * xh, -1, keepdims=True)) + dyv
        x2[rows(i), :] = dx
        do = dx.astype(bf)
        h1[rows(i), :] = do

        def sm(v):
            return jnp.sum(v, axis=0, keepdims=True) * one

        vg[2:3, :] += sm(dh * xh)
        vg[3:4, :] += sm(dh)
        vg[7:8, :] += sm(do.astype(f32))
        vg[12:13, :] += sm(dyv)
        invd[rows(i), :] = dot_nt(do, wo[mine, :]) * invd[rows(i), :]

    for q in (3, 1):
        r1_mid(1, q)
    for m in range(4):
        gq[m, :, :, 0:384] = dot(attt[m * 192 : m * 192 + 192, :], h1[:, mine]).astype(bf).reshape(4, 48, 384)
    gf[...] = jnp.zeros_like(gf)
    vsrc[...] = jnp.zeros_like(vsrc)
    lane = lax.broadcasted_iota(jnp.int32, (192, 128), 1)
    for q in (2, 0):
        r1_mid(1, q)

    dproj = act

    def ends(gp):
        r1_end(gp, 1)
        r1_end(gp, 2)

    backward = {
        (0, 3): ((r1_end, 0, 3), (r2_start, 0)),
        (0, 2): ((ends, 0),),
        (0, 1): ((r2_mid, 0),),
        (0, 0): ((r1_end, 1, 3), (r2_start, 1)),
        (0, -1): ((d_start, 0), (r1_end, 0, 0)),
        (1, 3): ((ends, 1),),
        (1, 2): ((r2_mid, 1), (r2_end, 0)),
        (1, 1): ((r1_end, 1, 0),),
        (1, 0): ((d_mid, 0),),
        (1, -1): ((d_start, 1),),
        (2, 3): ((r2_end, 1),),
        (2, 2): ((y_start, 0),),
        (2, 1): ((d_end, 0),),
        (2, 0): ((d_mid, 1),),
    }

    @pl.loop(0, 3)
    def _(p):
        lanes = pl.ds(at(p * 128), 128)
        ql = pl.ds(at(p * 384), 128)
        kl = pl.ds(at(p * 384 + 128), 128)
        vl = pl.ds(at(p * 384 + 256), 128)
        bq, bk = feature_maps(p)
        dst = [None, None]
        fq = jnp.zeros((128, 128), f32)
        fk = jnp.zeros((128, 128), f32)
        for i in (3, 2, 1, 0):
            rs = slice(i * 256, i * 256 + 256)
            dn = invd[rs, lanes]
            dd = roll64(-(dn * attf[rs, pl.ds(at(own + p * 128), 128)].astype(f32)))
            v = qkv[rs, vl]
            qm, km, same = same_doc(segc, i)
            dq, dk, dv = [], [], []
            for h in range(2):
                mh = m0 == (h == 0)
                vx = jnp.where(mh, v, jnp.ones_like(v))
                dx = jnp.where(mh, dn, dd).astype(bf)
                qq = qf[2 * p + h, rs, :]
                kk = kf[2 * p + h, rs, :]
                a_t = (dot_nt(kk, qq) * maskt[i].astype(f32)).astype(bf)
                da = (dot_nt(dx, vx) * mask[i].astype(f32)).astype(bf)
                da_t = (dot_nt(vx, dx) * maskt[i].astype(f32)).astype(bf)
                gqf = dot(da, kk)
                gkf = dot(da_t, qq)
                gv = dot(a_t, dx)
                if i < 3:
                    ds = dst[h].astype(bf)
                    gkf = gkf + dot_nt(vx, ds) * km
                    gv = gv + dot(kk, ds) * km
                if i > 0:
                    gqf = gqf + dot_nt(dx, st[2 * p + h, i - 1]) * qm
                    new = dot_tn((qq.astype(f32) * qm).astype(bf), dx)
                    dst[h] = new if i == 3 else new + same * dst[h]
                dq.append(gqf)
                dk.append(gkf)
                dv.append(gv)
            zq = soft_back(qf[2 * p, rs, :], qf[2 * p + 1, rs, :], dq[0], dq[1], m0, ones)
            zk = soft_back(kf[2 * p, rs, :], kf[2 * p + 1, rs, :], dk[0], dk[1], m0, ones)
            fq = fq + dot_tn(qkv[rs, ql], zq)
            fk = fk + dot_tn(qkv[rs, kl], zk)
            dproj[rs, ql] = dot_nt(zq, bq).astype(bf)
            dproj[rs, kl] = dot_nt(zk, bk).astype(bf)
            dproj[rs, vl] = jnp.where(m0, dv[0], dv[1]).astype(bf)
            pump(backward, p, i)
        top = lax.broadcasted_iota(jnp.int32, (128, 128), 0) < 64
        ml = low_lanes((128, 128))
        gf[pl.ds(at(own + p * 128), 128), :] = jnp.where(
            top, jnp.where(ml, fq, roll64(fk)), jnp.where(ml, roll64(fq), fk)
        ).astype(bf)
        trio = pl.ds(at(p * 384), 384)
        sums3 = jnp.sum(dproj[:, trio].astype(f32), axis=0, keepdims=True)
        base = at(p * 384 + 256 * jnp.minimum(p, 1))
        for m in range(4):
            ms = slice(m * 192, m * 192 + 192)
            t = dot(h1t[ms, :], dproj[:, trio])
            wt = w[ms, pl.ds(base, 384)].astype(f32)
            gain = w[ms, VAT : VAT + 128].astype(f32)
            gq[m, :, :, pl.ds(at(384 + p * 384), 384)] = (t * gain[:, 0:1] + sums3 * gain[:, 1:2]).astype(bf).reshape(4, 48, 384)
            gg = jnp.sum(wt * t, axis=1, keepdims=True)
            gs = jnp.sum(wt * sums3, axis=1, keepdims=True)
            vsrc[ms, :] += jnp.where(lane == 0, gg, jnp.where(lane == 1, gs, 0.0))
        for n in range(3):
            vg[4 + n : 5 + n, pl.ds(at(own + p * 128), 128)] = sums3[:, n * 128 : n * 128 + 128]
        pump(backward, p, -1)

    for m in range(4):
        gq[m, :, :, 1536:1664] = gf[m * 192 : m * 192 + 192, :].reshape(4, 48, 128)
    d_start(2)
    for k in range(2):
        vg[pl.ds(8 + 2 * c + k, 1), :] = gb[0:1, k * 768 : k * 768 + 768]
    vsrc[...] += jnp.transpose(jnp.concatenate([vg[...], jnp.zeros((112, 768), f32)], axis=0))

    def vx_(a, e):
        t = lax.rem((x, z)[a] + e, 4)
        n = (192, 48)[a]
        src = vsrc.at[pl.ds(at(t * 192 if a == 0 else x * 192 + t * 48, 16), n)]
        return rcopy(src, (v1, v2)[a].at[e - 1], ss.at[8], vxr.at[a], axis_peer(a, e))

    for e in (2, 1, 3):
        vx_(0, e).start()

    def dh1_rows(n, r0):
        ns = slice(n * 256, n * 256 + 256)

        @pl.loop(0, 2)
        def _(i):
            rs = pl.ds(at(r0 + i * 256), 256)
            t = dot_nt(dproj[rs, 0:384], w[ns, 0:384]) + dot_nt(dproj[rs, 384:1152], w[ns, 640:1408])
            dh1p[rs, ns] = t.astype(bf)

    for n in range(3):
        ns = slice(n * 256, n * 256 + 256)
        dh1_rows(n, away)
        ex(8 + n, dh1p.at[pl.ds(away, 512), ns], dh1o.at[:, ns]).start()
    d_end(1)
    y_start(1)
    take(v1, vxr.at[0])
    mid = pl.ds(at(x * 192, 16), 192)
    vsrc[mid, :] = vsrc[mid, :] + (v1[0] + v1[1] + v1[2])
    for e in (2, 1, 3):
        vx_(1, e).start()
    d_mid(2)
    for n in range(3):
        dh1_rows(n, half)
    for n in range(3):
        ns = slice(n * 256, n * 256 + 256)
        ex(8 + n, dh1p.at[pl.ds(away, 512), ns], dh1o.at[:, ns]).wait_recv()

    @pl.loop(0, 2)
    def _(i):
        rs = pl.ds(at(half + i * 256), 256)
        cen, r = norm_stats(xr[rs, :].astype(f32))
        xh = cen * r
        dh = dh1p[rs, :].astype(f32) + dh1o[rows(i), :].astype(f32)
        dx = dh * vec[0:1, :]
        dx = r * (dx - jnp.mean(dx, -1, keepdims=True) - xh * jnp.mean(dx * xh, -1, keepdims=True))
        dh1p[rs, :] = (dx + x2[rs, :]).astype(bf)

    take(v2, vxr.at[1])
    d_end(2)
    y_start(2)
    tok_start(1)

    def sums(gp):
        take(yr.at[0:7, :, YCOLS[gp][0] : YCOLS[gp][1]], ysr.at[gp])
        tot = jnp.zeros((1, 1), f32)
        for d, wd, sr, sp in GPIECES:
            if not YCOLS[gp][0] <= d < YCOLS[gp][1]:
                continue
            for cc in range(2 if sp else 1):
                srcs = [2 * j + cc for j in range(4)] if sp else range(8)
                v = sum(yr[j, 0:6, d : d + wd].astype(f32) for j in srcs)
                pg_o[:, sr + sp * cc : sr + sp * cc + wd] = v
                tot = tot + jnp.sum(jnp.sum(v * v, axis=1, keepdims=True), axis=0, keepdims=True)
        return tot

    total = sums(0) + sums(1)
    total = total + sums(2)
    V = sum(yr[j, :, 1664:1792].astype(f32) for j in range(8))
    vs_o[...] = V[0:6, 0:13]
    total = total + jnp.sum(jnp.sum(V[0:6] * V[0:6], axis=1, keepdims=True), axis=0, keepdims=True)
    n1[s] = jnp.broadcast_to(total, (8, 128))

    def nc1(k):
        return rcopy(n1.at[s], n1.at[s], ss.at[9], n1r.at[0], seq_peer(k)[1])

    def nc2(a, e):
        return rcopy(n2.at[a, 0], n2.at[a, e], ss.at[10], n2r.at[a], axis_peer(a, e))

    for k in range(1, 8):
        nc1(k).start()
    take(n1.at[0:7], n1r.at[0])
    n2[0, 0] = sum(n1[j] for j in range(8))
    for e in (2, 1, 3):
        nc2(0, e).start()
    take(n2.at[0, 0:3], n2r.at[0])
    n2[1, 0] = (n2[0, 0] + n2[0, 2]) + (n2[0, 1] + n2[0, 3])
    for e in (2, 1, 3):
        nc2(1, e).start()
    sent(rcv.at[0:7], 0)
    sent(sg.at[0:7], 1)
    sent(xr.at[0:768], 2)
    sent(xr, 3)
    sent(w.at[0:720], 4)
    sent(g.at[0:720], 5)
    sent(w.at[0:720, 0:GC], 6)
    sent(rcv.at[0:7], 7)
    sent(vsrc.at[0:720], 8)
    sent(n1.at[0:7], 9)
    for wh in range(2):
        tok_wait(wh)
    ex(0, w.at[:, WOAT : WOAT + 384], wo.at[:, mine]).wait_send()
    for p in range(3):
        ex(1 + p, att_part(p), att_part(p)).wait_send()
    ex(4, outp.at[pl.ds(away, 512)], outo).wait_send()
    for n in range(3):
        ns = slice(n * 256, n * 256 + 256)
        ex(8 + n, dh1p.at[pl.ds(away, 512), ns], dh1o.at[:, ns]).wait_send()
    take(n2.at[1, 0:3], n2r.at[1])
    sent(n2.at[:, 0:3], 10)
    norm_o[...] = jnp.sqrt((n2[1, 0] + n2[1, 2]) + (n2[1, 1] + n2[1, 3]))[0:1, 0:1]


def run_layer(par, vt, xin, dyin, sgin):
    V = pl.BlockSpec(memory_space=pltpu.VMEM)
    H = pl.BlockSpec(memory_space=pl.ANY)
    M = pltpu.VMEM
    DM = pltpu.SemaphoreType.DMA
    S = jax.ShapeDtypeStruct
    tok = (T, D)
    return pl.pallas_call(
        layer,
        out_shape=[S((4, 128, D), bf), S((4, 128, D), bf), S((6, 9344), f32), S((6, 13), f32), S((1, 1), f32)],
        in_specs=[V, V, H, H, V],
        out_specs=[V] * 5,
        scratch_shapes=[
            M((D, WC), bf), M((D, D), bf), M(tok, bf), M(tok, bf), M((8, 8, 128), f32), M((4, 8, 128), f32), M((2, 8, WC), bf), M((8, 8, WC), bf),
            M((16, D), f32), M(tok, bf), M((D, T), bf), M((T, 3 * HD), bf), M((6, T, 128), bf), M((6, T, 128), bf),
            M((T, HD), f32), M((6, 3, 128, 128), bf), M((T, 128), f32), M((4, 256, 256), bf), M((4, 256, 256), bf), M(tok, bf),
            M(tok, f32), M(tok, bf), M((D, T), bf), M((D, T), bf), M((T, FH), bf), M((T, FH), bf), M((512, D), bf),
            M(tok, bf), M((512, D), bf), M((D, 2 * FH), bf), M((576, 2 * FH), bf), M((144, 2 * FH), bf),
            M((4, 4, 48, GC), bf), M((3, 4, 48, GC), bf), M((3, 48, GC), bf), M((D, 128), bf),
            M((8, 8, WC), bf), M((8, 8, 128), f32), M((2, 4, 8, 128), f32), M((16, D), f32), M((8, FH), f32),
            M((D, 128), f32), M((3, 192, 128), f32), M((3, 48, 128), f32),
            DM((11,)), DM((3,)), DM((1,)), DM((2,)), DM((2,)), DM((4, 10)), DM((2, 4, 2)), DM((2, 2)), DM((3,)), DM((3,)), DM((3,)), DM((2,)),
            DM((1,)), DM((2,)), DM((11,)), DM((11,)), DM((2, 8)), DM((2, 8)), DM((2,)),
        ],
        compiler_params=pltpu.CompilerParams(collective_id=0, has_side_effects=True, vmem_limit_bytes=64 * 2**20 - 2**17),
        name="layer",
    )(par, vt, xin, dyin, sgin)


def adamw(weight, grad, m, v, scale, rate, decay):
    grad = grad * scale
    m = 0.5 * m + 0.5 * grad
    v = 0.5 * v + 0.5 * grad * grad
    return grad, weight - rate * (m / (jnp.sqrt(v) + 1e-8) + decay * weight), m, v


def body(inputs, segment_ids, out_grad, params, vectors, params_m, params_v, vectors_m, vectors_v):
    out, ig, pg, vs, norm = run_layer(params, vectors.T, inputs, out_grad, segment_ids)
    scale = 1.0 / jnp.maximum(norm[0, 0], 1.0)
    p = adamw(params, pg, params_m, params_v, scale, 0.05, 0.1)
    q = adamw(vectors.T, vs, vectors_m.T, vectors_v.T, scale, 0.2, 0.0)
    return (out, ig.astype(f32), norm.reshape(1)) + p + tuple(t.T for t in q)


def solution(mesh):
    torus = Mesh(mesh.devices.reshape(4, 4, 4, 2), ("x", "z", "y", "c"))
    row, seq, every = ("x", "z"), ("y", "c"), ("x", "z", "y", "c")
    tok, mat, vec = P(row, seq, None), P(every, None), P(None, every)
    return jax.shard_map(
        body,
        mesh=torus,
        in_specs=(tok, P(row, seq), tok, mat, vec, mat, mat, vec, vec),
        out_specs=(tok, tok, P(), mat, mat, mat, mat, vec, vec, vec, vec),
        check_vma=False,
    )
```

```python
import jax
import jax.numpy as jnp
from jax import lax
from jax.experimental import pallas as pl
from jax.experimental.pallas import tpu as pltpu
from jax.sharding import Mesh
from jax.sharding import PartitionSpec as P

f32 = jnp.float32
bf = jnp.bfloat16
MESH = pl.DeviceIdType.MESH
T, D, HD, FH = 1024, 768, 384, 1536
WC = 4864
GC = 1664
PIECES = (
    (0, 128, 0, 384), (128, 128, 768, 384), (256, 128, 1536, 384), (384, 128, 3072, 0),
    (640, 128, 128, 384), (768, 128, 896, 384), (896, 128, 1664, 384),
    (1024, 128, 256, 384), (1152, 128, 1024, 384), (1280, 128, 1792, 384), (1408, 384, 2304, 384),
    (1792, 768, 3200, 1536), (2560, 768, 6272, 1536), (3328, 768, 3968, 1536), (4096, 768, 7040, 1536),
)
VAT = 512
WOAT = 1408
FAT = 384
STAGE = ((0, 640), (640, 1792), (1792, 4864))
GATHER = ((0, 256, 640), (640, 1152, 1792), (1792, 2560, 3328), (3328, 4096, 4864))
GPIECES = (
    (0, 384, 2304, 384), (384, 128, 0, 384), (512, 128, 768, 384), (640, 128, 1536, 384),
    (768, 128, 128, 384), (896, 128, 896, 384), (1024, 128, 1664, 384),
    (1152, 128, 256, 384), (1280, 128, 1024, 384), (1408, 128, 1792, 384), (1536, 128, 3072, 0),
    (1792, 768, 3200, 1536), (2560, 768, 6272, 1536), (3328, 768, 3968, 1536), (4096, 768, 7040, 1536),
)
REDUCE = ((1792, 2560, 3328), (3328, 4096, 4864))
DIRECT = (((0, 384), (384, 768)), ((768, 896), (896, 1152)), ((1152, 1408), (1408, 1664)))
YCOLS = ((1792, 4864), (0, 1152), (1152, 1792))
FAR = (0, -1, 1, 2)
BIG = 3.0e38


def dot(a, b):
    return lax.dot_general(a, b, (((1,), (0,)), ((), ())), preferred_element_type=f32)


def dot_nt(a, b):
    return lax.dot_general(a, b, (((1,), (1,)), ((), ())), preferred_element_type=f32)


def dot_tn(a, b):
    return lax.dot_general(a, b, (((0,), (0,)), ((), ())), preferred_element_type=f32)


def at(v, m=128):
    return pl.multiple_of(v, m)


def rows(i, n=256):
    return pl.ds(at(i * n), n)


def low_lanes(shape):
    return lax.broadcasted_iota(jnp.int32, shape, len(shape) - 1) < 64


def roll64(v):
    return pltpu.roll(v, 64, 1)


def slab(xx, zz):
    return at((lax.rem(xx + 8, 4) * 4 + lax.rem(zz + 8, 4)) * 48, 16)


def norm_stats(v):
    mu = jnp.mean(v, axis=-1, keepdims=True)
    cen = v - mu
    return cen, lax.rsqrt(jnp.mean(cen * cen, axis=-1, keepdims=True) + 1e-5)


def seg_ones():
    a = lax.broadcasted_iota(jnp.int32, (128, 128), 0) < 64
    return (a == low_lanes((128, 128))).astype(bf)


def feats(z, m0, ones):
    mx = jnp.where(m0, jnp.max(jnp.where(m0, z, -BIG), -1, keepdims=True), jnp.max(jnp.where(m0, -BIG, z), -1, keepdims=True))
    mn = jnp.where(m0, jnp.min(jnp.where(m0, z, BIG), -1, keepdims=True), jnp.min(jnp.where(m0, BIG, z), -1, keepdims=True))
    ep = jnp.exp(z - mx).astype(bf)
    en = jnp.exp(mn - z).astype(bf)
    fp = ep.astype(f32) / dot(ep, ones)
    fn = roll64(en.astype(f32) / dot(en, ones))
    return jnp.where(m0, fp, fn).astype(bf), jnp.where(m0, fn, fp).astype(bf)


def soft_back(fe, fo, de, do, m0, ones):
    fe = fe.astype(f32)
    fo = fo.astype(f32)
    fp = jnp.where(m0, fe, fo)
    fr = jnp.where(m0, fo, fe)
    tp = fp * jnp.where(m0, de, do)
    tr = fr * jnp.where(m0, do, de)

    def total(t):
        hi = t.astype(bf)
        return dot(hi, ones) + dot((t - hi.astype(f32)).astype(bf), ones)

    return ((tp - fp * total(tp)) - roll64(tr - fr * total(tr))).astype(bf)


def same_doc(segc, i):
    sc = segc[i * 256 : i * 256 + 256, :]
    last = segc[i * 256 + 255 : i * 256 + 256, :]
    km = (sc == last).astype(f32)
    if i == 0:
        return None, km, None
    prev = segc[i * 256 - 1 : i * 256, :]
    return (sc == prev).astype(f32), km, (last == prev).astype(f32)


def layer(
    par, vt, xin, dyin, sgin,
    out_o, ig_o, pg_o, vs_o, norm_o,
    w, wo, xr, dyr, sg, sgb, wire, rcv, vec, h1, h1t, qkv, qf, kf, invd, st, segc, mask, maskt, attf,
    x2, h2, h2t, dyt, act, du, outo, dh2o, dh1o, g, r1, r2, gq, d1, d2, gf, yr, n1, n2, vg, gb, vsrc, v1, v2,
    ss, s0r, sgr, rsr, sbr, agr, t1r, t2r, d1r, d2r, ysr, vxr, n1r, n2r, exs, exr, tks, tkr, los,
):
    x, z, y, c = (lax.axis_index(a) for a in ("x", "z", "y", "c"))
    s = y * 2 + c
    pln = x * 4 + z
    own = at(c * 384)

    def rcopy(src, dst, ss, rs, dev):
        return pltpu.make_async_remote_copy(src, dst, ss, rs, device_id=dev, device_id_type=MESH)

    def take(ref, sem):
        rcopy(ref, ref, sem, sem, other).wait_recv()

    def sent(ref, i):
        rcopy(ref, ref, ss.at[i], ss.at[i], other).wait_send()

    def seq_peer(k):
        t = lax.rem(s + k + 8, 8)
        return t, {"y": t // 2, "c": lax.rem(t, 2)}

    def axis_peer(a, k):
        return {("x", "z")[a]: lax.rem((x, z)[a] + k + 4, 4)}

    def plane_peer(k):
        t = lax.rem(pln + k, 16)
        return {"x": t // 4, "z": lax.rem(t, 4)}

    other = {"c": 1 - c}

    bar = pltpu.get_barrier_semaphore()
    for k in range(1, 8):
        pl.semaphore_signal(bar, inc=1, device_id=seq_peer(k)[1], device_id_type=MESH)
    for k in range(1, 16):
        pl.semaphore_signal(bar, inc=1, device_id=plane_peer(k), device_id_type=MESH)
    for cc in range(2):
        wire[cc, :, :] = jnp.zeros((8, WC), bf)
        for d, wd, sr, sp in PIECES:
            wire[cc, 0:6, d : d + wd] = par[:, sr + sp * cc : sr + sp * cc + wd].astype(bf)
        wire[cc, 0:6, VAT : VAT + 13] = vt[...].astype(bf)
    for j in range(4):
        sgb[j] = jnp.broadcast_to(sgin[j : j + 1, :].astype(f32), (8, 128))
    pl.semaphore_wait(bar, 22)

    def st0(gp, k):
        t, dev = seq_peer(k)
        a, b = STAGE[gp]
        return rcopy(wire.at[dev["c"], :, a:b], rcv.at[s, :, a:b], ss.at[0], s0r.at[gp], dev)

    def sgc(k):
        t, dev = seq_peer(k)
        return rcopy(sgb.at[t // 2], sg.at[s], ss.at[1], sgr.at[0], dev)

    pairs = ((xin, xr), (dyin, dyr))

    def res(wh, k):
        src, dst = pairs[wh]
        j = lax.rem(y + k, 4)
        return rcopy(src.at[j], dst.at[rows(s, 128)], ss.at[2], rsr.at[wh], {"y": j})

    def keep(wh):
        src, dst = pairs[wh]
        return pltpu.make_async_copy(src.at[y], dst.at[rows(s, 128)], los.at[wh])

    def sib(wh, k):
        ref = pairs[wh][1].at[rows(lax.rem(y - k + 4, 4) * 2 + c, 128)]
        return rcopy(ref, ref, ss.at[3], sbr.at[wh], other)

    def res_start(wh):
        keep(wh).start()
        for k in (2, 1, 3):
            res(wh, k).start()

    def res_pass(wh):
        keep(wh).wait()
        sib(wh, 0).start()
        take(pairs[wh][1].at[0:384], rsr.at[wh])
        for k in range(1, 4):
            sib(wh, k).start()

    def res_end(wh):
        take(pairs[wh][1].at[0:512], sbr.at[wh])

    def pos(p, d1, d2):
        return slab(x + d1, z + d2) if p == 0 else slab(x + d2, z + d1)

    def along(p, phase, way):
        return axis_peer((p + phase) % 2, way)

    def ag(gp, p, sem, d1, d2, phase, way):
        ref = w.at[pl.ds(pos(p, d1, d2), 48), GATHER[gp][p] : GATHER[gp][p + 1]]
        return rcopy(ref, ref, ss.at[4], agr.at[gp, sem], along(p, phase, way))

    def ag_take(gp, sem):
        take(w.at[0 : (96, 48)[sem % 2], GATHER[gp][0] : GATHER[gp][2]], agr.at[gp, sem])

    def p2send(gp, q):
        for p in range(2):
            ag(gp, p, 2 + 2 * q, FAR[q], 0, 1, 1).start()
            ag(gp, p, 2 + 2 * q, FAR[q], 0, 1, -1).start()

    def ag_d(gp, q):
        ag_take(gp, 2 + 2 * q)
        way = (1, -1, -1, 1)[q]
        for p in range(2):
            ag(gp, p, 3 + 2 * q, FAR[q], -way, 1, way).start()

    def ag_a(gp):
        for p in range(2):
            ag(gp, p, 0, 0, 0, 0, 1).start()
            ag(gp, p, 0, 0, 0, 0, -1).start()
        p2send(gp, 0)

    def ag_b(gp):
        ag_take(gp, 0)
        ag(gp, 0, 1, -1, 0, 0, 1).start()
        ag(gp, 1, 1, 1, 0, 0, -1).start()
        p2send(gp, 1)
        p2send(gp, 2)

    def ag_c(gp):
        ag_take(gp, 1)
        p2send(gp, 3)
        ag_d(gp, 0)

    def ag_e(gp):
        for q in range(4):
            ag_take(gp, 3 + 2 * q)

    rr = lax.broadcasted_iota(jnp.int32, (48, 64), 0)
    rc = lax.broadcasted_iota(jnp.int32, (48, 64), 1)
    spread = ((lax.rem(rr, 6) == lax.rem(rc, 8)) & (rr // 6 == rc // 8)).astype(bf)

    def assemble(gp):
        a, b = STAGE[gp]
        take(rcv.at[0:7, :, a:b], s0r.at[gp])
        n = (640, 1152, 768)[gp]
        for lo in range(a, b, n):
            raw = jnp.concatenate([rcv[t, :, lo : lo + n].astype(f32) for t in range(8)], axis=0).astype(bf)
            w[pl.ds(slab(x, z), 48), lo : lo + n] = dot(spread, raw).astype(bf)

    for k in range(1, 8):
        st0(0, k).start()
    for k in range(1, 8):
        st0(1, k).start()
    for k in range(1, 8):
        sgc(k).start()
    res_start(0)
    for k in range(1, 8):
        st0(2, k).start()
    sg[s] = sgb[y]
    rcv[s] = wire[c]
    assemble(0)
    ag_a(0)
    assemble(1)
    ag_a(1)
    ag_b(0)
    take(sg.at[0:7], sgr.at[0])
    for b in range(8):
        segc[b * 128 : b * 128 + 128, :] = jnp.transpose(jnp.broadcast_to(sg[b, 0:1, :], (128, 128)))
    mr = lax.broadcasted_iota(jnp.int32, (256, 256), 0)
    mc = lax.broadcasted_iota(jnp.int32, (256, 256), 1)
    for i in range(4):
        row = jnp.concatenate([sg[2 * i, 0:1, :], sg[2 * i + 1, 0:1, :]], axis=1)
        col = segc[i * 256 : i * 256 + 256, :]
        eq = jnp.concatenate([col, col], axis=1) == row
        mask[i] = jnp.where(eq & (mc <= mr), 1.0, 0.0).astype(bf)
        maskt[i] = jnp.where(eq & (mr <= mc), 1.0, 0.0).astype(bf)
    ag_c(0)
    for q in (1, 2):
        ag_d(0, q)
    res_pass(0)
    ag_b(1)
    ag_d(0, 3)
    res_end(0)
    res_start(1)

    @pl.loop(0, 4)
    def _(i):
        cen, r = norm_stats(xr[rows(i), :].astype(f32))
        x2[rows(i), :] = cen * r

    ag_c(1)
    assemble(2)
    ag_a(2)
    ag_a(3)
    ag_e(0)

    def ex(i, src, dst):
        return rcopy(src, dst, exs.at[i], exr.at[i], other)

    mine = pl.ds(own, 384)

    vec[...] = jnp.transpose(w[:, VAT : VAT + 128].astype(f32))[0:16]

    @pl.loop(0, 4)
    def _(i):
        h = (x2[rows(i), :] * vec[0:1, :] + vec[1:2, :]).astype(bf)
        h1[rows(i), :] = h
        h1t[:, rows(i)] = jnp.transpose(x2[rows(i), :].astype(bf))

    ones = seg_ones()
    m0 = low_lanes((256, 128))

    def feature_maps(p):
        F = w[pl.ds(at(own + p * 128), 128), FAT : FAT + 128].astype(f32)
        R = roll64(F)
        top = lax.broadcasted_iota(jnp.int32, (128, 128), 0) < 64
        ml = low_lanes((128, 128))
        zz = jnp.zeros_like(F)
        bq = jnp.where(top & ml, F, jnp.where(top | ml, zz, R))
        bk = jnp.where(top & ml, R, jnp.where(top | ml, zz, F))
        return bq.astype(bf), bk.astype(bf)

    def pump(table, p, i):
        for (pp, ii), todo in table.items():
            if ii == i:

                @pl.when(p == pp)
                def _():
                    for t in todo:
                        t[0](*t[1:])

    def wo_start():
        ex(0, w.at[:, WOAT : WOAT + 384], wo.at[:, mine]).start()
        wo[:, mine] = w[:, WOAT : WOAT + 384]

    forward = {
        (0, 0): ((ag_d, 1, 1), (ag_d, 1, 2)),
        (0, 1): ((ag_d, 1, 3), (ag_b, 2)),
        (0, 2): ((ag_b, 3),),
        (0, 3): ((ag_e, 1), (wo_start,)),
        (1, 0): ((ag_c, 2),),
        (1, 1): ((ag_c, 3),),
        (1, 2): ((ag_d, 2, 1), (ag_d, 2, 2)),
        (1, 3): ((ag_d, 3, 1), (res_pass, 1)),
        (2, 0): ((ag_d, 2, 3), (ag_d, 3, 2)),
        (2, 2): ((ag_d, 3, 3),),
    }

    def att_part(p):
        return attf.at[:, pl.ds(at(own + p * 128), 128)]

    @pl.loop(0, 3)
    def _(p):
        lanes = pl.ds(at(p * 128), 128)
        bq, bk = feature_maps(p)
        base = at(p * 384 + 256 * jnp.minimum(p, 1))
        part = pl.ds(at(own + p * 128), 128)
        bias = jnp.concatenate([vec[4:5, part], vec[5:6, part], vec[6:7, part]], axis=1)
        state = [None, None]
        for i in range(4):
            rs = slice(i * 256, i * 256 + 256)
            pr = (dot(h1[rs, :], w[:, pl.ds(base, 384)]) + bias).astype(bf)
            qkv[rs, pl.ds(at(p * 384), 384)] = pr
            qe, qo = feats(dot(pr[:, 0:128], bq), m0, ones)
            ke, ko = feats(dot(pr[:, 128:256], bk), m0, ones)
            v = pr[:, 256:384]
            qm, km, same = same_doc(segc, i)
            outs = []
            for h, (qq, kk) in enumerate(((qe, ke), (qo, ko))):
                vx = jnp.where(m0 == (h == 0), v, jnp.ones_like(v))
                qf[2 * p + h, rs, :] = qq
                kf[2 * p + h, rs, :] = kk
                o = dot((dot_nt(qq, kk) * mask[i].astype(f32)).astype(bf), vx)
                if i > 0:
                    sb = state[h].astype(bf)
                    st[2 * p + h, i - 1] = sb
                    o = o + dot(qq, sb) * qm
                if i < 3:
                    sn = dot_tn((kk.astype(f32) * km).astype(bf), vx)
                    state[h] = sn if i == 0 else sn + same * state[h]
                outs.append(o)
            num = jnp.where(m0, outs[0], outs[1])
            inv = 1.0 / roll64(jnp.where(m0, outs[1], outs[0]))
            invd[rs, lanes] = inv
            attf[rs, part] = (num * inv).astype(bf)
            if i == 3:
                ex(1 + p, att_part(p), att_part(p)).start()
            pump(forward, p, i)

    res_end(1)
    ex(0, w.at[:, WOAT : WOAT + 384], wo.at[:, pl.ds(at((1 - c) * 384), 384)]).wait_recv()
    for p in range(3):
        part = attf.at[:, pl.ds(at((1 - c) * 384 + p * 128), 128)]
        ex(1 + p, part, part).wait_recv()

    @pl.loop(0, 4)
    def _(i):
        v = xr[rows(i), :].astype(f32) + dot(attf[rows(i), :], wo[...]) + vec[7:8, :]
        x2[rows(i), :] = v
        cen, r = norm_stats(v)
        h = (cen * r * vec[2:3, :] + vec[3:4, :]).astype(bf)
        h2[rows(i), :] = h
        h2t[:, rows(i)] = jnp.transpose(h)
        dyt[:, rows(i)] = jnp.transpose(dyr[rows(i), :])

    k0 = 0.7978845608028654
    k1 = 0.044715

    def mlp(j):
        far = at(1792 + (j // 3) * 768 + j * 256)
        cu = pl.ds(far, 256)
        cd = pl.ds(at(far + 768), 256)
        gu = pl.ds(at(far - 1792), 256)
        gd = pl.ds(at(far - 1024), 256)
        cj = pl.ds(at(j * 256), 256)
        off = c * FH + j * 256
        bu = vec[pl.ds(8 + off // D, 1), pl.ds(at(lax.rem(off, D)), 256)]

        @pl.loop(0, 4, unroll=4)
        def _(i):
            u = dot(h2[rows(i), :], w[:, cu]) + bu
            u2 = u * u
            t = jnp.tanh(k0 * (u + k1 * u2 * u))
            act[rows(i), cj] = (0.5 * u * (1.0 + t)).astype(bf)
            da = dot(dyr[rows(i), :], w[:, cd])
            gp = 0.5 * (1.0 + t) + 0.5 * u * (1.0 - t * t) * (k0 * (1.0 + (3 * k1) * u2))
            d = (gp * da).astype(bf)
            du[rows(i), cj] = d
            gb[0:1, cj] = gb[0:1, cj] + jnp.sum(d.astype(f32), axis=0, keepdims=True)

        for m in range(3):
            ms = slice(m * 256, m * 256 + 256)
            g[ms, gd] = dot(dyt[ms, :], act[:, cj]).astype(bf)
            g[ms, gu] = dot(h2t[ms, :], du[:, cj]).astype(bf)

    def gref(gp, p, d1, d2):
        return g.at[pl.ds(pos(p, d1, d2), 48), REDUCE[gp][p] - 1792 : REDUCE[gp][p + 1] - 1792]

    def land(gp, p, slot):
        r = slice(slot % 12 * 48, slot % 12 * 48 + 48)
        return (r1 if slot < 12 else r2).at[r, REDUCE[gp][p] - 1792 : REDUCE[gp][p + 1] - 1792]

    def tree_take(n, sem):
        take(r1.at[0:n, 0:1536], sem)

    def c1(gp, p, q, kind):
        way = (1, -1, -1, 1)[q]
        e = (2, way, -way)[kind]
        return rcopy(gref(gp, p, FAR[q], e), land(gp, p, q * 3 + kind), ss.at[5], t1r.at[gp, q, (kind + 1) // 2], along(p, 1, -way if kind == 2 else way))

    def c2(gp, p, kind):
        way = (1, -1)[p]
        e = (2, way, -way)[kind]
        return rcopy(gref(gp, p, e, 0), land(gp, p, 12 + kind), ss.at[5], t2r.at[gp, (kind + 1) // 2], along(p, 0, -way if kind == 2 else way))

    def acc(dst, *srcs):
        t = dst[...].astype(f32)
        for r in srcs:
            t = t + r[...].astype(f32)
        dst[...] = t.astype(bf)

    def r1_start(gp):
        for q in (3, 1, 2, 0):
            for p in range(2):
                c1(gp, p, q, 0).start()
                c1(gp, p, q, 2).start()

    def r1_mid(gp, q):
        tree_take(48, t1r.at[gp, q, 0])
        for p in range(2):
            acc(gref(gp, p, FAR[q], (1, -1, -1, 1)[q]), land(gp, p, q * 3))
            c1(gp, p, q, 1).start()

    def r1_end(gp, q):
        tree_take(96, t1r.at[gp, q, 1])
        for p in range(2):
            acc(gref(gp, p, FAR[q], 0), land(gp, p, q * 3 + 1), land(gp, p, q * 3 + 2))

    def r2_start(gp):
        for q in (3, 1, 2):
            r1_end(gp, q)
        for p in range(2):
            c2(gp, p, 0).start()
            c2(gp, p, 2).start()

    def r2_mid(gp):
        tree_take(48, t2r.at[gp, 0])
        for p in range(2):
            acc(gref(gp, p, (1, -1)[p], 0), land(gp, p, 12))
            c2(gp, p, 1).start()

    def r2_end(gp):
        tree_take(96, t2r.at[gp, 1])
        for p in range(2):
            acc(gref(gp, p, 0, 0), land(gp, p, 13), land(gp, p, 14))

    tr = lax.broadcasted_iota(jnp.int32, (64, 48), 0)
    tc = lax.broadcasted_iota(jnp.int32, (64, 48), 1)
    split = ((lax.rem(tc, 6) == lax.rem(tr, 8)) & (tc // 6 == tr // 8)).astype(bf)

    def dcp(gp, p, phase, e):
        a, b = DIRECT[gp][p]
        first = p == 0
        if phase == 0:
            t = lax.rem((z if first else x) + e, 4)
            src = gq.at[:, t, :, a:b] if first else gq.at[t, :, :, a:b]
            return rcopy(src, d1.at[e - 1, :, :, a:b], ss.at[6], d1r.at[gp], axis_peer(1 if first else 0, e))
        t = lax.rem((x if first else z) + e, 4)
        src = gq.at[t, z, :, a:b] if first else gq.at[x, t, :, a:b]
        return rcopy(src, d2.at[e - 1, :, a:b], ss.at[6], d2r.at[gp], axis_peer(0 if first else 1, e))

    def d_start(gp):
        for e in (2, 1, 3):
            for p in range(2):
                dcp(gp, p, 0, e).start()

    def d_mid(gp):
        take(d1.at[:, :, :, DIRECT[gp][0][0] : DIRECT[gp][1][1]], d1r.at[gp])
        for p in range(2):
            a, b = DIRECT[gp][p]
            for k in range(4):
                dst = gq.at[k, z, :, a:b] if p == 0 else gq.at[x, k, :, a:b]
                acc(dst, *[d1.at[e, k, :, a:b] for e in range(3)])
            for e in (2, 1, 3):
                dcp(gp, p, 1, e).start()

    def d_end(gp):
        take(d2.at[:, :, DIRECT[gp][0][0] : DIRECT[gp][1][1]], d2r.at[gp])
        for p in range(2):
            a, b = DIRECT[gp][p]
            acc(gq.at[x, z, :, a:b], *[d2.at[e, :, a:b] for e in range(3)])

    def ycp(gp, k):
        t, dev = seq_peer(k)
        a, b = YCOLS[gp]
        return rcopy(rcv.at[t, :, a:b], yr.at[s, :, a:b], ss.at[7], ysr.at[gp], dev)

    def deal(a, b, part):
        out = dot(split, part).astype(bf)
        for t in range(8):
            rcv[t, :, a:b] = out[8 * t : 8 * t + 8]

    def y_start(gp):
        a, b = YCOLS[gp]
        if gp == 0:
            for lo in range(0, 3072, 768):
                deal(1792 + lo, 2560 + lo, g[pl.ds(slab(x, z), 48), lo : lo + 768])
        elif gp == 1:
            deal(0, 1152, gq[x, z, :, 0:1152])
        else:
            deal(1152, 1664, gq[x, z, :, 1152:1664])
            deal(1664, 1792, (vsrc[pl.ds(slab(x, z), 48), :] + (v2[0] + v2[1] + v2[2])).astype(bf))
        for k in range(1, 8):
            ycp(gp, k).start()
        yr[s, :, a:b] = rcv[s, :, a:b]

    gb[...] = jnp.zeros_like(gb)
    ag_e(2)
    pl.loop(0, 3)(mlp)
    r1_start(0)
    ag_e(3)
    pl.loop(3, 6)(mlp)
    for q in (3, 1, 2, 0):
        r1_mid(0, q)
    r1_start(1)

    outp, dh2p, dh1p = h2, h1, du.at[:, 0:768]
    half = at(c * 512)
    away = at((1 - c) * 512)

    @pl.loop(0, 4)
    def _(i):
        for n in range(3):
            ns = slice(n * 256, n * 256 + 256)
            outp[rows(i), ns] = (dot_nt(act[rows(i), 0:768], w[ns, 2560:3328]) + dot_nt(act[rows(i), 768:1536], w[ns, 4096:4864])).astype(bf)

    ex(4, outp.at[pl.ds(away, 512)], outo).start()
    r2_start(0)
    for n in range(3):
        ns = slice(n * 256, n * 256 + 256)

        @pl.loop(0, 4)
        def _(i):
            dh2p[rows(i), ns] = (dot_nt(du[rows(i), 0:768], w[ns, 1792:2560]) + dot_nt(du[rows(i), 768:1536], w[ns, 3328:4096])).astype(bf)

        ex(5 + n, dh2p.at[:, ns], dh2o.at[:, ns]).start()
    r2_mid(0)
    r1_end(0, 0)
    for q in (3, 1):
        r1_mid(1, q)
    ex(4, outp.at[pl.ds(away, 512)], outo).wait_recv()

    @pl.loop(0, 2)
    def _(i):
        rs = pl.ds(at(half + i * 256), 256)
        outp[rs, :] = (x2[rs, :] + outp[rs, :].astype(f32) + outo[rows(i), :].astype(f32) + vec[12:13, :]).astype(bf)

    toks = ((outp, out_o), (dh1p, ig_o))

    def tok(wh, k, recv=False):
        src, dst = toks[wh]
        t, dev = seq_peer(k)
        row = (seq_peer(-k)[0] // 2) if recv else y
        return rcopy(src.at[pl.ds(at(half + lax.rem(t, 4) * 128), 128)], dst.at[row], tks.at[wh, k], tkr.at[wh, k], dev)

    def tok_keep(wh):
        src, dst = toks[wh]
        return pltpu.make_async_copy(src.at[pl.ds(at(half + lax.rem(s, 4) * 128), 128)], dst.at[y], los.at[2 + wh])

    def tok_start(wh):
        for k in range(1, 8):

            @pl.when(seq_peer(k)[0] // 4 == c)
            def _():
                tok(wh, k).start()

        @pl.when(s // 4 == c)
        def _():
            tok_keep(wh).start()

    def tok_wait(wh):
        @pl.when(s // 4 == c)
        def _():
            tok_keep(wh).wait()

        for k in range(1, 8):

            @pl.when(lax.rem(seq_peer(-k)[0], 2) == s // 4)
            def _():
                tok(wh, k, True).wait_recv()

        for k in range(1, 8):

            @pl.when(seq_peer(k)[0] // 4 == c)
            def _():
                tok(wh, k).wait_send()

    tok_start(0)

    vg[...] = jnp.zeros_like(vg)
    one = (c == 0).astype(f32)
    attt = dyt

    @pl.loop(0, 4)
    def _(i):
        attt[:, rows(i)] = jnp.transpose(attf[rows(i), :])

    for n in range(3):
        ns = slice(n * 256, n * 256 + 256)
        ex(5 + n, dh2p.at[:, ns], dh2o.at[:, ns]).wait_recv()
        ex(5 + n, dh2p.at[:, ns], dh2o.at[:, ns]).wait_send()

    @pl.loop(0, 4)
    def _(i):
        cen, r = norm_stats(x2[rows(i), :])
        xh = cen * r
        dh = dh2p[rows(i), :].astype(f32) + dh2o[rows(i), :].astype(f32)
        dyv = dyr[rows(i), :].astype(f32)
        dx = dh * vec[2:3, :]
        dx = r * (dx - jnp.mean(dx, -1, keepdims=True) - xh * jnp.mean(dx * xh, -1, keepdims=True)) + dyv
        x2[rows(i), :] = dx
        do = dx.astype(bf)
        h1[rows(i), :] = do

        def sm(v):
            return jnp.sum(v, axis=0, keepdims=True) * one

        vg[2:3, :] += sm(dh * xh)
        vg[3:4, :] += sm(dh)
        vg[7:8, :] += sm(do.astype(f32))
        vg[12:13, :] += sm(dyv)
        invd[rows(i), :] = dot_nt(do, wo[mine, :]) * invd[rows(i), :]

    for q in (2, 0):
        r1_mid(1, q)
    for m in range(4):
        gq[m, :, :, 0:384] = dot(attt[m * 192 : m * 192 + 192, :], h1[:, mine]).astype(bf).reshape(4, 48, 384)
    gf[...] = jnp.zeros_like(gf)
    vsrc[...] = jnp.zeros_like(vsrc)
    lane = lax.broadcasted_iota(jnp.int32, (192, 128), 1)
    dproj = act

    backward = {
        (0, 3): ((r2_start, 1),),
        (0, 2): ((r2_end, 0),),
        (0, 1): ((r2_mid, 1),),
        (0, 0): ((r1_end, 1, 0),),
        (0, -1): ((d_start, 0),),
        (1, 3): ((r2_end, 1),),
        (1, 2): ((y_start, 0),),
        (1, 0): ((d_mid, 0),),
        (1, -1): ((d_start, 1),),
        (2, 3): ((d_end, 0),),
        (2, 2): ((d_mid, 1),),
        (2, 0): ((d_end, 1), (y_start, 1)),
    }

    @pl.loop(0, 3)
    def _(p):
        lanes = pl.ds(at(p * 128), 128)
        ql = pl.ds(at(p * 384), 128)
        kl = pl.ds(at(p * 384 + 128), 128)
        vl = pl.ds(at(p * 384 + 256), 128)
        bq, bk = feature_maps(p)
        dst = [None, None]
        fq = jnp.zeros((128, 128), f32)
        fk = jnp.zeros((128, 128), f32)
        for i in (3, 2, 1, 0):
            rs = slice(i * 256, i * 256 + 256)
            dn = invd[rs, lanes]
            dd = roll64(-(dn * attf[rs, pl.ds(at(own + p * 128), 128)].astype(f32)))
            v = qkv[rs, vl]
            qm, km, same = same_doc(segc, i)
            dq, dk, dv = [], [], []
            for h in range(2):
                mh = m0 == (h == 0)
                vx = jnp.where(mh, v, jnp.ones_like(v))
                dx = jnp.where(mh, dn, dd).astype(bf)
                qq = qf[2 * p + h, rs, :]
                kk = kf[2 * p + h, rs, :]
                a_t = (dot_nt(kk, qq) * maskt[i].astype(f32)).astype(bf)
                da = (dot_nt(dx, vx) * mask[i].astype(f32)).astype(bf)
                da_t = (dot_nt(vx, dx) * maskt[i].astype(f32)).astype(bf)
                gqf = dot(da, kk)
                gkf = dot(da_t, qq)
                gv = dot(a_t, dx)
                if i < 3:
                    ds = dst[h].astype(bf)
                    gkf = gkf + dot_nt(vx, ds) * km
                    gv = gv + dot(kk, ds) * km
                if i > 0:
                    gqf = gqf + dot_nt(dx, st[2 * p + h, i - 1]) * qm
                    new = dot_tn((qq.astype(f32) * qm).astype(bf), dx)
                    dst[h] = new if i == 3 else new + same * dst[h]
                dq.append(gqf)
                dk.append(gkf)
                dv.append(gv)
            zq = soft_back(qf[2 * p, rs, :], qf[2 * p + 1, rs, :], dq[0], dq[1], m0, ones)
            zk = soft_back(kf[2 * p, rs, :], kf[2 * p + 1, rs, :], dk[0], dk[1], m0, ones)
            fq = fq + dot_tn(qkv[rs, ql], zq)
            fk = fk + dot_tn(qkv[rs, kl], zk)
            dproj[rs, ql] = dot_nt(zq, bq).astype(bf)
            dproj[rs, kl] = dot_nt(zk, bk).astype(bf)
            dproj[rs, vl] = jnp.where(m0, dv[0], dv[1]).astype(bf)
            pump(backward, p, i)
        top = lax.broadcasted_iota(jnp.int32, (128, 128), 0) < 64
        ml = low_lanes((128, 128))
        gf[pl.ds(at(own + p * 128), 128), :] = jnp.where(
            top, jnp.where(ml, fq, roll64(fk)), jnp.where(ml, roll64(fq), fk)
        ).astype(bf)
        trio = pl.ds(at(p * 384), 384)
        sums3 = jnp.sum(dproj[:, trio].astype(f32), axis=0, keepdims=True)
        base = at(p * 384 + 256 * jnp.minimum(p, 1))
        for m in range(4):
            ms = slice(m * 192, m * 192 + 192)
            t = dot(h1t[ms, :], dproj[:, trio])
            wt = w[ms, pl.ds(base, 384)].astype(f32)
            gain = w[ms, VAT : VAT + 128].astype(f32)
            gq[m, :, :, pl.ds(at(384 + p * 384), 384)] = (t * gain[:, 0:1] + sums3 * gain[:, 1:2]).astype(bf).reshape(4, 48, 384)
            gg = jnp.sum(wt * t, axis=1, keepdims=True)
            gs = jnp.sum(wt * sums3, axis=1, keepdims=True)
            vsrc[ms, :] += jnp.where(lane == 0, gg, jnp.where(lane == 1, gs, 0.0))
        for n in range(3):
            vg[4 + n : 5 + n, pl.ds(at(own + p * 128), 128)] = sums3[:, n * 128 : n * 128 + 128]
        pump(backward, p, -1)

    for m in range(4):
        gq[m, :, :, 1536:1664] = gf[m * 192 : m * 192 + 192, :].reshape(4, 48, 128)
    d_start(2)
    for k in range(2):
        vg[pl.ds(8 + 2 * c + k, 1), :] = gb[0:1, k * 768 : k * 768 + 768]
    vsrc[...] += jnp.transpose(jnp.concatenate([vg[...], jnp.zeros((112, 768), f32)], axis=0))

    def vx_(a, e):
        t = lax.rem((x, z)[a] + e, 4)
        n = (192, 48)[a]
        src = vsrc.at[pl.ds(at(t * 192 if a == 0 else x * 192 + t * 48, 16), n)]
        return rcopy(src, (v1, v2)[a].at[e - 1], ss.at[8], vxr.at[a], axis_peer(a, e))

    for e in (2, 1, 3):
        vx_(0, e).start()

    def dh1_rows(n, r0):
        ns = slice(n * 256, n * 256 + 256)

        @pl.loop(0, 2)
        def _(i):
            rs = pl.ds(at(r0 + i * 256), 256)
            t = dot_nt(dproj[rs, 0:384], w[ns, 0:384]) + dot_nt(dproj[rs, 384:1152], w[ns, 640:1408])
            dh1p[rs, ns] = t.astype(bf)

    for n in range(3):
        ns = slice(n * 256, n * 256 + 256)
        dh1_rows(n, away)
        ex(8 + n, dh1p.at[pl.ds(away, 512), ns], dh1o.at[:, ns]).start()
    take(v1, vxr.at[0])
    mid = pl.ds(at(x * 192, 16), 192)
    vsrc[mid, :] = vsrc[mid, :] + (v1[0] + v1[1] + v1[2])
    for e in (2, 1, 3):
        vx_(1, e).start()
    d_mid(2)
    for n in range(3):
        dh1_rows(n, half)
    for n in range(3):
        ns = slice(n * 256, n * 256 + 256)
        ex(8 + n, dh1p.at[pl.ds(away, 512), ns], dh1o.at[:, ns]).wait_recv()

    @pl.loop(0, 2, unroll=2)
    def _(i):
        rs = pl.ds(at(half + i * 256), 256)
        cen, r = norm_stats(xr[rs, :].astype(f32))
        xh = cen * r
        dh = dh1p[rs, :].astype(f32) + dh1o[rows(i), :].astype(f32)
        dx = dh * vec[0:1, :]
        dx = r * (dx - jnp.mean(dx, -1, keepdims=True) - xh * jnp.mean(dx * xh, -1, keepdims=True))
        dh1p[rs, :] = (dx + x2[rs, :]).astype(bf)

    take(v2, vxr.at[1])
    d_end(2)
    y_start(2)
    tok_start(1)

    def sums(gp):
        take(yr.at[0:7, :, YCOLS[gp][0] : YCOLS[gp][1]], ysr.at[gp])
        tot = jnp.zeros((1, 1), f32)
        for d, wd, sr, sp in GPIECES:
            if not YCOLS[gp][0] <= d < YCOLS[gp][1]:
                continue
            for cc in range(2 if sp else 1):
                srcs = [2 * j + cc for j in range(4)] if sp else range(8)
                v = sum(yr[j, 0:6, d : d + wd].astype(f32) for j in srcs)
                pg_o[:, sr + sp * cc : sr + sp * cc + wd] = v
                tot = tot + jnp.sum(jnp.sum(v * v, axis=1, keepdims=True), axis=0, keepdims=True)
        return tot

    total = sums(0) + sums(1)
    total = total + sums(2)
    V = sum(yr[j, :, 1664:1792].astype(f32) for j in range(8))
    vs_o[...] = V[0:6, 0:13]
    total = total + jnp.sum(jnp.sum(V[0:6] * V[0:6], axis=1, keepdims=True), axis=0, keepdims=True)
    n2[pln] = jnp.broadcast_to(total, (8, 128))

    def nc2(k):
        return rcopy(n2.at[pln], n2.at[pln], ss.at[10], n2r.at[0], plane_peer(k))

    def nc1(k):
        return rcopy(n1.at[s], n1.at[s], ss.at[9], n1r.at[0], seq_peer(k)[1])

    for k in range(1, 16):
        nc2(k).start()
    take(n2.at[0:15], n2r.at[0])
    n1[s] = sum(n2[j] for j in range(16))
    for k in range(1, 8):
        nc1(k).start()
    sent(rcv.at[0:7], 0)
    sent(sg.at[0:7], 1)
    sent(xr.at[0:768], 2)
    sent(xr, 3)
    sent(w.at[0:720], 4)
    sent(g.at[0:720], 5)
    sent(w.at[0:720, 0:GC], 6)
    sent(rcv.at[0:7], 7)
    sent(vsrc.at[0:720], 8)
    sent(n2.at[0:15], 10)
    for wh in range(2):
        tok_wait(wh)
    ex(0, w.at[:, WOAT : WOAT + 384], wo.at[:, mine]).wait_send()
    for p in range(3):
        ex(1 + p, att_part(p), att_part(p)).wait_send()
    ex(4, outp.at[pl.ds(away, 512)], outo).wait_send()
    for n in range(3):
        ns = slice(n * 256, n * 256 + 256)
        ex(8 + n, dh1p.at[pl.ds(away, 512), ns], dh1o.at[:, ns]).wait_send()
    take(n1.at[0:7], n1r.at[0])
    norm_o[...] = jnp.sqrt(sum(n1[j] for j in range(8)))[0:1, 0:1]
    sent(n1.at[0:7], 9)


def run_layer(par, vt, xin, dyin, sgin):
    V = pl.BlockSpec(memory_space=pltpu.VMEM)
    H = pl.BlockSpec(memory_space=pl.ANY)
    M = pltpu.VMEM
    DM = pltpu.SemaphoreType.DMA
    S = jax.ShapeDtypeStruct
    tok = (T, D)
    return pl.pallas_call(
        layer,
        out_shape=[S((4, 128, D), bf), S((4, 128, D), bf), S((6, 9344), f32), S((6, 13), f32), S((1, 1), f32)],
        in_specs=[V, V, H, H, V],
        out_specs=[H, H, V, V, V],
        scratch_shapes=[
            M((D, WC), bf), M((D, D), bf), M(tok, bf), M(tok, bf), M((8, 8, 128), f32), M((4, 8, 128), f32), M((2, 8, WC), bf), M((8, 8, WC), bf),
            M((16, D), f32), M(tok, bf), M((D, T), bf), M((T, 3 * HD), bf), M((6, T, 128), bf), M((6, T, 128), bf),
            M((T, HD), f32), M((6, 3, 128, 128), bf), M((T, 128), f32), M((4, 256, 256), bf), M((4, 256, 256), bf), M(tok, bf),
            M(tok, f32), M(tok, bf), M((D, T), bf), M((D, T), bf), M((T, FH), bf), M((T, FH), bf), M((512, D), bf),
            M(tok, bf), M((512, D), bf), M((D, 2 * FH), bf), M((576, 2 * FH), bf), M((144, 2 * FH), bf),
            M((4, 4, 48, GC), bf), M((3, 4, 48, GC), bf), M((3, 48, GC), bf), M((D, 128), bf),
            M((8, 8, WC), bf), M((8, 8, 128), f32), M((16, 8, 128), f32), M((16, D), f32), M((8, FH), f32),
            M((D, 128), f32), M((3, 192, 128), f32), M((3, 48, 128), f32),
            DM((11,)), DM((3,)), DM((1,)), DM((2,)), DM((2,)), DM((4, 10)), DM((2, 4, 2)), DM((2, 2)), DM((3,)), DM((3,)), DM((3,)), DM((2,)),
            DM((1,)), DM((1,)), DM((11,)), DM((11,)), DM((2, 8)), DM((2, 8)), DM((4,)),
        ],
        compiler_params=pltpu.CompilerParams(collective_id=0, has_side_effects=True, vmem_limit_bytes=64 * 2**20 - 2**17),
        name="layer",
    )(par, vt, xin, dyin, sgin)


def adamw(weight, grad, m, v, scale, rate, decay):
    grad = grad * scale
    m = 0.5 * m + 0.5 * grad
    v = 0.5 * v + 0.5 * grad * grad
    return grad, weight - rate * (m / (jnp.sqrt(v) + 1e-8) + decay * weight), m, v


def body(inputs, segment_ids, out_grad, params, vectors, params_m, params_v, vectors_m, vectors_v):
    out, ig, pg, vs, norm = run_layer(params, vectors.T, inputs, out_grad, segment_ids)
    scale = 1.0 / jnp.maximum(norm[0, 0], 1.0)
    p = adamw(params, pg, params_m, params_v, scale, 0.05, 0.1)
    q = adamw(vectors.T, vs, vectors_m.T, vectors_v.T, scale, 0.2, 0.0)
    return (out, ig.astype(f32), norm.reshape(1)) + p + tuple(t.T for t in q)


def solution(mesh):
    torus = Mesh(mesh.devices.reshape(4, 4, 4, 2), ("x", "z", "y", "c"))
    row, seq, every = ("x", "z"), ("y", "c"), ("x", "z", "y", "c")
    tok, mat, vec = P(row, seq, None), P(every, None), P(None, every)
    return jax.shard_map(
        body,
        mesh=torus,
        in_specs=(tok, P(row, seq), tok, mat, vec, mat, mat, vec, vec),
        out_specs=(tok, tok, P(), mat, mat, mat, mat, vec, vec, vec, vec),
        check_vma=False,
    )
```

```python
import jax
import jax.numpy as jnp
from jax import lax
from jax.experimental import pallas as pl
from jax.experimental.pallas import tpu as pltpu
from jax.sharding import Mesh
from jax.sharding import PartitionSpec as P

f32 = jnp.float32
bf = jnp.bfloat16
MESH = pl.DeviceIdType.MESH
T, D, HD, FH = 1024, 768, 384, 1536
WC = 4864
GC = 1664
PIECES = (
    (0, 128, 0, 384), (128, 128, 768, 384), (256, 128, 1536, 384), (384, 128, 3072, 0),
    (640, 128, 128, 384), (768, 128, 896, 384), (896, 128, 1664, 384),
    (1024, 128, 256, 384), (1152, 128, 1024, 384), (1280, 128, 1792, 384), (1408, 384, 2304, 384),
    (1792, 768, 3200, 1536), (2560, 768, 6272, 1536), (3328, 768, 3968, 1536), (4096, 768, 7040, 1536),
)
VAT = 512
WOAT = 1408
FAT = 384
STAGE = ((0, 640), (640, 1792), (1792, 4864))
GATHER = ((0, 256, 640), (640, 1152, 1792), (1792, 2560, 3328), (3328, 4096, 4864))
GPIECES = (
    (0, 384, 2304, 384), (384, 128, 0, 384), (512, 128, 768, 384), (640, 128, 1536, 384),
    (768, 128, 128, 384), (896, 128, 896, 384), (1024, 128, 1664, 384),
    (1152, 128, 256, 384), (1280, 128, 1024, 384), (1408, 128, 1792, 384), (1536, 128, 3072, 0),
    (1792, 768, 3200, 1536), (2560, 768, 6272, 1536), (3328, 768, 3968, 1536), (4096, 768, 7040, 1536),
)
REDUCE = ((1792, 2560, 3328), (3328, 4096, 4864))
DIRECT = (((0, 384), (384, 768)), ((768, 896), (896, 1152)), ((1152, 1408), (1408, 1664)))
YCOLS = ((1792, 4864), (0, 1152), (1152, 1792))
FAR = (0, -1, 1, 2)
BIG = 3.0e38


def dot(a, b):
    return lax.dot_general(a, b, (((1,), (0,)), ((), ())), preferred_element_type=f32)


def dot_nt(a, b):
    return lax.dot_general(a, b, (((1,), (1,)), ((), ())), preferred_element_type=f32)


def dot_tn(a, b):
    return lax.dot_general(a, b, (((0,), (0,)), ((), ())), preferred_element_type=f32)


def at(v, m=128):
    return pl.multiple_of(v, m)


def rows(i, n=256):
    return pl.ds(at(i * n), n)


def low_lanes(shape):
    return lax.broadcasted_iota(jnp.int32, shape, len(shape) - 1) < 64


def roll64(v):
    return pltpu.roll(v, 64, 1)


def slab(xx, zz):
    return at((lax.rem(xx + 8, 4) * 4 + lax.rem(zz + 8, 4)) * 48, 16)


def norm_stats(v):
    mu = jnp.mean(v, axis=-1, keepdims=True)
    cen = v - mu
    return cen, lax.rsqrt(jnp.mean(cen * cen, axis=-1, keepdims=True) + 1e-5)


def seg_ones():
    a = lax.broadcasted_iota(jnp.int32, (128, 128), 0) < 64
    return (a == low_lanes((128, 128))).astype(bf)


def feats(z, m0, ones):
    mx = jnp.where(m0, jnp.max(jnp.where(m0, z, -BIG), -1, keepdims=True), jnp.max(jnp.where(m0, -BIG, z), -1, keepdims=True))
    mn = jnp.where(m0, jnp.min(jnp.where(m0, z, BIG), -1, keepdims=True), jnp.min(jnp.where(m0, BIG, z), -1, keepdims=True))
    ep = jnp.exp(z - mx).astype(bf)
    en = jnp.exp(mn - z).astype(bf)
    fp = ep.astype(f32) / dot(ep, ones)
    fn = roll64(en.astype(f32) / dot(en, ones))
    return jnp.where(m0, fp, fn).astype(bf), jnp.where(m0, fn, fp).astype(bf)


def soft_back(fe, fo, de, do, m0, ones):
    fe = fe.astype(f32)
    fo = fo.astype(f32)
    fp = jnp.where(m0, fe, fo)
    fr = jnp.where(m0, fo, fe)
    tp = fp * jnp.where(m0, de, do)
    tr = fr * jnp.where(m0, do, de)

    def total(t):
        hi = t.astype(bf)
        return dot(hi, ones) + dot((t - hi.astype(f32)).astype(bf), ones)

    return ((tp - fp * total(tp)) - roll64(tr - fr * total(tr))).astype(bf)


def same_doc(segc, i):
    sc = segc[i * 256 : i * 256 + 256, :]
    last = segc[i * 256 + 255 : i * 256 + 256, :]
    km = (sc == last).astype(f32)
    if i == 0:
        return None, km, None
    prev = segc[i * 256 - 1 : i * 256, :]
    return (sc == prev).astype(f32), km, (last == prev).astype(f32)


def layer(
    par, vt, xin, dyin, sgin,
    out_o, ig_o, pg_o, vs_o, norm_o,
    w, wo, xr, dyr, sg, sgb, wire, rcv, vec, h1, h1t, qkv, qf, kf, invd, st, segc, mask, maskt, attf,
    x2, h2, h2t, dyt, act, du, outo, dh2o, dh1o, g, r1, r2, gq, d1, d2, gf, yr, n1, n2, vg, gb, vsrc, v1, v2,
    ss, s0r, sgr, rsr, sbr, agr, t1r, t2r, d1r, d2r, ysr, vxr, n1r, n2r, exs, exr, tks, tkr, los,
):
    x, z, y, c = (lax.axis_index(a) for a in ("x", "z", "y", "c"))
    s = y * 2 + c
    pln = x * 4 + z
    own = at(c * 384)

    def rcopy(src, dst, ss, rs, dev):
        return pltpu.make_async_remote_copy(src, dst, ss, rs, device_id=dev, device_id_type=MESH)

    def take(ref, sem):
        rcopy(ref, ref, sem, sem, other).wait_recv()

    def sent(ref, i):
        rcopy(ref, ref, ss.at[i], ss.at[i], other).wait_send()

    def seq_peer(k):
        t = lax.rem(s + k + 8, 8)
        return t, {"y": t // 2, "c": lax.rem(t, 2)}

    def axis_peer(a, k):
        return {("x", "z")[a]: lax.rem((x, z)[a] + k + 4, 4)}

    def plane_peer(k):
        t = lax.rem(pln + k, 16)
        return {"x": t // 4, "z": lax.rem(t, 4)}

    other = {"c": 1 - c}

    bar = pltpu.get_barrier_semaphore()
    for k in range(1, 8):
        pl.semaphore_signal(bar, inc=1, device_id=seq_peer(k)[1], device_id_type=MESH)
    for k in range(1, 16):
        pl.semaphore_signal(bar, inc=1, device_id=plane_peer(k), device_id_type=MESH)
    for cc in range(2):
        wire[cc, :, :] = jnp.zeros((8, WC), bf)
        for d, wd, sr, sp in PIECES:
            wire[cc, 0:6, d : d + wd] = par[:, sr + sp * cc : sr + sp * cc + wd].astype(bf)
        wire[cc, 0:6, VAT : VAT + 13] = vt[...].astype(bf)
    for j in range(4):
        sgb[j] = jnp.broadcast_to(sgin[j : j + 1, :].astype(f32), (8, 128))
    pl.semaphore_wait(bar, 22)

    def st0(gp, k):
        t, dev = seq_peer(k)
        a, b = STAGE[gp]
        return rcopy(wire.at[dev["c"], :, a:b], rcv.at[s, :, a:b], ss.at[0], s0r.at[gp], dev)

    def sgc(k):
        t, dev = seq_peer(k)
        return rcopy(sgb.at[t // 2], sg.at[s], ss.at[1], sgr.at[0], dev)

    pairs = ((xin, xr), (dyin, dyr))

    def res(wh, k):
        src, dst = pairs[wh]
        j = lax.rem(y + k, 4)
        return rcopy(src.at[j], dst.at[rows(s, 128)], ss.at[2], rsr.at[wh], {"y": j})

    def keep(wh):
        src, dst = pairs[wh]
        return pltpu.make_async_copy(src.at[y], dst.at[rows(s, 128)], los.at[wh])

    def sib(wh, k):
        ref = pairs[wh][1].at[rows(lax.rem(y - k + 4, 4) * 2 + c, 128)]
        return rcopy(ref, ref, ss.at[3], sbr.at[wh], other)

    def res_start(wh):
        keep(wh).start()
        for k in (2, 1, 3):
            res(wh, k).start()

    def res_pass(wh):
        keep(wh).wait()
        sib(wh, 0).start()
        take(pairs[wh][1].at[0:384], rsr.at[wh])
        for k in range(1, 4):
            sib(wh, k).start()

    def res_end(wh):
        take(pairs[wh][1].at[0:512], sbr.at[wh])

    def pos(p, d1, d2):
        return slab(x + d1, z + d2) if p == 0 else slab(x + d2, z + d1)

    def along(p, phase, way):
        return axis_peer((p + phase) % 2, way)

    def ag(gp, p, sem, d1, d2, phase, way):
        ref = w.at[pl.ds(pos(p, d1, d2), 48), GATHER[gp][p] : GATHER[gp][p + 1]]
        return rcopy(ref, ref, ss.at[4], agr.at[gp, sem], along(p, phase, way))

    def ag_take(gp, sem):
        take(w.at[0 : (96, 48)[sem % 2], GATHER[gp][0] : GATHER[gp][2]], agr.at[gp, sem])

    def p2send(gp, q):
        for p in range(2):
            ag(gp, p, 2 + 2 * q, FAR[q], 0, 1, 1).start()
            ag(gp, p, 2 + 2 * q, FAR[q], 0, 1, -1).start()

    def ag_d(gp, q):
        ag_take(gp, 2 + 2 * q)
        way = (1, -1, -1, 1)[q]
        for p in range(2):
            ag(gp, p, 3 + 2 * q, FAR[q], -way, 1, way).start()

    def ag_a(gp):
        for p in range(2):
            ag(gp, p, 0, 0, 0, 0, 1).start()
            ag(gp, p, 0, 0, 0, 0, -1).start()
        p2send(gp, 0)

    def ag_b(gp):
        ag_take(gp, 0)
        ag(gp, 0, 1, -1, 0, 0, 1).start()
        ag(gp, 1, 1, 1, 0, 0, -1).start()
        p2send(gp, 1)
        p2send(gp, 2)

    def ag_c(gp):
        ag_take(gp, 1)
        p2send(gp, 3)
        ag_d(gp, 0)

    def ag_e(gp):
        for q in range(4):
            ag_take(gp, 3 + 2 * q)

    rr = lax.broadcasted_iota(jnp.int32, (48, 64), 0)
    rc = lax.broadcasted_iota(jnp.int32, (48, 64), 1)
    spread = ((lax.rem(rr, 6) == lax.rem(rc, 8)) & (rr // 6 == rc // 8)).astype(bf)

    def assemble(gp):
        a, b = STAGE[gp]
        take(rcv.at[0:7, :, a:b], s0r.at[gp])
        n = (640, 1152, 768)[gp]
        for lo in range(a, b, n):
            raw = jnp.concatenate([rcv[t, :, lo : lo + n].astype(f32) for t in range(8)], axis=0).astype(bf)
            w[pl.ds(slab(x, z), 48), lo : lo + n] = dot(spread, raw).astype(bf)

    for k in range(1, 8):
        st0(0, k).start()
    for k in range(1, 8):
        st0(1, k).start()
    for k in range(1, 8):
        sgc(k).start()
    res_start(0)
    for k in range(1, 8):
        st0(2, k).start()
    sg[s] = sgb[y]
    rcv[s] = wire[c]
    assemble(0)
    ag_a(0)
    assemble(1)
    ag_a(1)
    ag_b(0)
    take(sg.at[0:7], sgr.at[0])
    for b in range(8):
        segc[b * 128 : b * 128 + 128, :] = jnp.transpose(jnp.broadcast_to(sg[b, 0:1, :], (128, 128)))
    mr = lax.broadcasted_iota(jnp.int32, (256, 256), 0)
    mc = lax.broadcasted_iota(jnp.int32, (256, 256), 1)
    for i in range(4):
        row = jnp.concatenate([sg[2 * i, 0:1, :], sg[2 * i + 1, 0:1, :]], axis=1)
        col = segc[i * 256 : i * 256 + 256, :]
        eq = jnp.concatenate([col, col], axis=1) == row
        mask[i] = jnp.where(eq & (mc <= mr), 1.0, 0.0).astype(bf)
        maskt[i] = jnp.where(eq & (mr <= mc), 1.0, 0.0).astype(bf)
    ag_c(0)
    for q in (1, 2):
        ag_d(0, q)
    res_pass(0)
    ag_b(1)
    ag_d(0, 3)
    res_end(0)
    res_start(1)

    @pl.loop(0, 4, unroll=2)
    def _(i):
        cen, r = norm_stats(xr[rows(i), :].astype(f32))
        x2[rows(i), :] = cen * r

    ag_c(1)
    assemble(2)
    ag_a(2)
    ag_e(0)

    def ex(i, src, dst):
        return rcopy(src, dst, exs.at[i], exr.at[i], other)

    mine = pl.ds(own, 384)

    vec[...] = jnp.transpose(w[:, VAT : VAT + 128].astype(f32))[0:16]

    @pl.loop(0, 4, unroll=2)
    def _(i):
        h = (x2[rows(i), :] * vec[0:1, :] + vec[1:2, :]).astype(bf)
        h1[rows(i), :] = h
        h1t[:, rows(i)] = jnp.transpose(x2[rows(i), :].astype(bf))

    ones = seg_ones()
    m0 = low_lanes((256, 128))

    def feature_maps(p):
        F = w[pl.ds(at(own + p * 128), 128), FAT : FAT + 128].astype(f32)
        R = roll64(F)
        top = lax.broadcasted_iota(jnp.int32, (128, 128), 0) < 64
        ml = low_lanes((128, 128))
        zz = jnp.zeros_like(F)
        bq = jnp.where(top & ml, F, jnp.where(top | ml, zz, R))
        bk = jnp.where(top & ml, R, jnp.where(top | ml, zz, F))
        return bq.astype(bf), bk.astype(bf)

    def pump(table, p, i):
        for (pp, ii), todo in table.items():
            if ii == i:

                @pl.when(p == pp)
                def _():
                    for t in todo:
                        t[0](*t[1:])

    def wo_start():
        ex(0, w.at[:, WOAT : WOAT + 384], wo.at[:, mine]).start()
        wo[:, mine] = w[:, WOAT : WOAT + 384]

    forward = {
        (0, 0): ((ag_d, 1, 1), (ag_d, 1, 2)),
        (0, 1): ((ag_d, 1, 3),),
        (0, 2): ((ag_b, 2), (ag_a, 3)),
        (0, 3): ((ag_e, 1), (wo_start,)),
        (1, 1): ((ag_c, 2), (res_pass, 1)),
        (1, 2): ((ag_b, 3),),
        (1, 3): ((ag_d, 2, 1), (ag_d, 2, 2)),
        (2, 1): ((ag_d, 2, 3),),
        (2, 3): ((ag_c, 3),),
    }

    def att_part(p):
        return attf.at[:, pl.ds(at(own + p * 128), 128)]

    @pl.loop(0, 3)
    def _(p):
        lanes = pl.ds(at(p * 128), 128)
        bq, bk = feature_maps(p)
        base = at(p * 384 + 256 * jnp.minimum(p, 1))
        part = pl.ds(at(own + p * 128), 128)
        bias = jnp.concatenate([vec[4:5, part], vec[5:6, part], vec[6:7, part]], axis=1)
        state = [None, None]
        for i in range(4):
            rs = slice(i * 256, i * 256 + 256)
            pr = (dot(h1[rs, :], w[:, pl.ds(base, 384)]) + bias).astype(bf)
            qkv[rs, pl.ds(at(p * 384), 384)] = pr
            qe, qo = feats(dot(pr[:, 0:128], bq), m0, ones)
            ke, ko = feats(dot(pr[:, 128:256], bk), m0, ones)
            v = pr[:, 256:384]
            qm, km, same = same_doc(segc, i)
            outs = []
            for h, (qq, kk) in enumerate(((qe, ke), (qo, ko))):
                vx = jnp.where(m0 == (h == 0), v, jnp.ones_like(v))
                qf[2 * p + h, rs, :] = qq
                kf[2 * p + h, rs, :] = kk
                o = dot((dot_nt(qq, kk) * mask[i].astype(f32)).astype(bf), vx)
                if i > 0:
                    sb = state[h].astype(bf)
                    st[2 * p + h, i - 1] = sb
                    o = o + dot(qq, sb) * qm
                if i < 3:
                    sn = dot_tn((kk.astype(f32) * km).astype(bf), vx)
                    state[h] = sn if i == 0 else sn + same * state[h]
                outs.append(o)
            num = jnp.where(m0, outs[0], outs[1])
            inv = 1.0 / roll64(jnp.where(m0, outs[1], outs[0]))
            invd[rs, lanes] = inv
            attf[rs, part] = (num * inv).astype(bf)
            if i == 3:
                ex(1 + p, att_part(p), att_part(p)).start()
            pump(forward, p, i)

    res_end(1)
    ex(0, w.at[:, WOAT : WOAT + 384], wo.at[:, pl.ds(at((1 - c) * 384), 384)]).wait_recv()
    for p in range(3):
        part = attf.at[:, pl.ds(at((1 - c) * 384 + p * 128), 128)]
        ex(1 + p, part, part).wait_recv()

    @pl.loop(0, 4, unroll=2)
    def _(i):
        v = xr[rows(i), :].astype(f32) + dot(attf[rows(i), :], wo[...]) + vec[7:8, :]
        x2[rows(i), :] = v
        cen, r = norm_stats(v)
        h = (cen * r * vec[2:3, :] + vec[3:4, :]).astype(bf)
        h2[rows(i), :] = h
        h2t[:, rows(i)] = jnp.transpose(h)
        dyt[:, rows(i)] = jnp.transpose(dyr[rows(i), :])

    k0 = 0.7978845608028654
    k1 = 0.044715

    def mlp(j):
        far = at(1792 + (j // 3) * 768 + j * 256)
        cu = pl.ds(far, 256)
        cd = pl.ds(at(far + 768), 256)
        gu = pl.ds(at(far - 1792), 256)
        gd = pl.ds(at(far - 1024), 256)
        cj = pl.ds(at(j * 256), 256)
        off = c * FH + j * 256
        bu = vec[pl.ds(8 + off // D, 1), pl.ds(at(lax.rem(off, D)), 256)]

        @pl.loop(0, 4, unroll=4)
        def _(i):
            u = dot(h2[rows(i), :], w[:, cu]) + bu
            u2 = u * u
            t = jnp.tanh(k0 * (u + k1 * u2 * u))
            act[rows(i), cj] = (0.5 * u * (1.0 + t)).astype(bf)
            da = dot(dyr[rows(i), :], w[:, cd])
            gp = 0.5 * (1.0 + t) + 0.5 * u * (1.0 - t * t) * (k0 * (1.0 + (3 * k1) * u2))
            d = (gp * da).astype(bf)
            du[rows(i), cj] = d
            gb[0:1, cj] = gb[0:1, cj] + jnp.sum(d.astype(f32), axis=0, keepdims=True)

        for m in range(3):
            ms = slice(m * 256, m * 256 + 256)
            g[ms, gd] = dot(dyt[ms, :], act[:, cj]).astype(bf)
            g[ms, gu] = dot(h2t[ms, :], du[:, cj]).astype(bf)

    def gref(gp, p, d1, d2):
        return g.at[pl.ds(pos(p, d1, d2), 48), REDUCE[gp][p] - 1792 : REDUCE[gp][p + 1] - 1792]

    def land(gp, p, slot):
        r = slice(slot % 12 * 48, slot % 12 * 48 + 48)
        return (r1 if slot < 12 else r2).at[r, REDUCE[gp][p] - 1792 : REDUCE[gp][p + 1] - 1792]

    def tree_take(n, sem):
        take(r1.at[0:n, 0:1536], sem)

    def c1(gp, p, q, kind):
        way = (1, -1, -1, 1)[q]
        e = (2, way, -way)[kind]
        return rcopy(gref(gp, p, FAR[q], e), land(gp, p, q * 3 + kind), ss.at[5], t1r.at[gp, q, (kind + 1) // 2], along(p, 1, -way if kind == 2 else way))

    def c2(gp, p, kind):
        way = (1, -1)[p]
        e = (2, way, -way)[kind]
        return rcopy(gref(gp, p, e, 0), land(gp, p, 12 + kind), ss.at[5], t2r.at[gp, (kind + 1) // 2], along(p, 0, -way if kind == 2 else way))

    def acc(dst, *srcs):
        t = dst[...].astype(f32)
        for r in srcs:
            t = t + r[...].astype(f32)
        dst[...] = t.astype(bf)

    def r1_start(gp):
        for q in (3, 1, 2, 0):
            for p in range(2):
                c1(gp, p, q, 0).start()
                c1(gp, p, q, 2).start()

    def r1_mid(gp, q):
        tree_take(48, t1r.at[gp, q, 0])
        for p in range(2):
            acc(gref(gp, p, FAR[q], (1, -1, -1, 1)[q]), land(gp, p, q * 3))
            c1(gp, p, q, 1).start()

    def r1_end(gp, q):
        tree_take(96, t1r.at[gp, q, 1])
        for p in range(2):
            acc(gref(gp, p, FAR[q], 0), land(gp, p, q * 3 + 1), land(gp, p, q * 3 + 2))

    def r2_start(gp):
        for q in (3, 1, 2):
            r1_end(gp, q)
        for p in range(2):
            c2(gp, p, 0).start()
            c2(gp, p, 2).start()

    def r2_mid(gp):
        tree_take(48, t2r.at[gp, 0])
        for p in range(2):
            acc(gref(gp, p, (1, -1)[p], 0), land(gp, p, 12))
            c2(gp, p, 1).start()

    def r2_end(gp):
        tree_take(96, t2r.at[gp, 1])
        for p in range(2):
            acc(gref(gp, p, 0, 0), land(gp, p, 13), land(gp, p, 14))

    tr = lax.broadcasted_iota(jnp.int32, (64, 48), 0)
    tc = lax.broadcasted_iota(jnp.int32, (64, 48), 1)
    split = ((lax.rem(tc, 6) == lax.rem(tr, 8)) & (tc // 6 == tr // 8)).astype(bf)

    def dcp(gp, p, phase, e):
        a, b = DIRECT[gp][p]
        first = p == 0
        if phase == 0:
            t = lax.rem((z if first else x) + e, 4)
            src = gq.at[:, t, :, a:b] if first else gq.at[t, :, :, a:b]
            return rcopy(src, d1.at[e - 1, :, :, a:b], ss.at[6], d1r.at[gp], axis_peer(1 if first else 0, e))
        t = lax.rem((x if first else z) + e, 4)
        src = gq.at[t, z, :, a:b] if first else gq.at[x, t, :, a:b]
        return rcopy(src, d2.at[e - 1, :, a:b], ss.at[6], d2r.at[gp], axis_peer(0 if first else 1, e))

    def d_start(gp):
        for e in (2, 1, 3):
            for p in range(2):
                dcp(gp, p, 0, e).start()

    def d_mid(gp):
        take(d1.at[:, :, :, DIRECT[gp][0][0] : DIRECT[gp][1][1]], d1r.at[gp])
        for p in range(2):
            a, b = DIRECT[gp][p]
            for k in range(4):
                dst = gq.at[k, z, :, a:b] if p == 0 else gq.at[x, k, :, a:b]
                acc(dst, *[d1.at[e, k, :, a:b] for e in range(3)])
            for e in (2, 1, 3):
                dcp(gp, p, 1, e).start()

    def d_end(gp):
        take(d2.at[:, :, DIRECT[gp][0][0] : DIRECT[gp][1][1]], d2r.at[gp])
        for p in range(2):
            a, b = DIRECT[gp][p]
            acc(gq.at[x, z, :, a:b], *[d2.at[e, :, a:b] for e in range(3)])

    def ycp(gp, k):
        t, dev = seq_peer(k)
        a, b = YCOLS[gp]
        return rcopy(rcv.at[t, :, a:b], yr.at[s, :, a:b], ss.at[7], ysr.at[gp], dev)

    def deal(a, b, part):
        out = dot(split, part).astype(bf)
        for t in range(8):
            rcv[t, :, a:b] = out[8 * t : 8 * t + 8]

    def y_start(gp):
        a, b = YCOLS[gp]
        if gp == 0:
            for lo in range(0, 3072, 768):
                deal(1792 + lo, 2560 + lo, g[pl.ds(slab(x, z), 48), lo : lo + 768])
        elif gp == 1:
            deal(0, 1152, gq[x, z, :, 0:1152])
        else:
            deal(1152, 1664, gq[x, z, :, 1152:1664])
            deal(1664, 1792, (vsrc[pl.ds(slab(x, z), 48), :] + (v2[0] + v2[1] + v2[2])).astype(bf))
        for k in range(1, 8):
            ycp(gp, k).start()
        yr[s, :, a:b] = rcv[s, :, a:b]

    gb[...] = jnp.zeros_like(gb)
    def mlp_first(j):
        mlp(j)

        @pl.when(j == 0)
        def _():
            ag_d(3, 2)

        @pl.when(j == 1)
        def _():
            ag_d(3, 3)

    ag_d(3, 1)
    ag_e(2)
    pl.loop(0, 3)(mlp_first)
    r1_start(0)
    ag_e(3)
    pl.loop(3, 6)(mlp)
    for q in (3, 1, 2, 0):
        r1_mid(0, q)
    r1_start(1)

    outp, dh2p, dh1p = h2, h1, du.at[:, 0:768]
    half = at(c * 512)
    away = at((1 - c) * 512)

    @pl.loop(0, 4, unroll=2)
    def _(i):
        for n in range(3):
            ns = slice(n * 256, n * 256 + 256)
            outp[rows(i), ns] = (dot_nt(act[rows(i), 0:768], w[ns, 2560:3328]) + dot_nt(act[rows(i), 768:1536], w[ns, 4096:4864])).astype(bf)

    ex(4, outp.at[pl.ds(away, 512)], outo).start()
    r2_start(0)
    for n in range(3):
        ns = slice(n * 256, n * 256 + 256)

        @pl.loop(0, 4, unroll=2)
        def _(i):
            dh2p[rows(i), ns] = (dot_nt(du[rows(i), 0:768], w[ns, 1792:2560]) + dot_nt(du[rows(i), 768:1536], w[ns, 3328:4096])).astype(bf)

        ex(5 + n, dh2p.at[:, ns], dh2o.at[:, ns]).start()
    r2_mid(0)
    r1_end(0, 0)
    for q in (3, 1):
        r1_mid(1, q)
    ex(4, outp.at[pl.ds(away, 512)], outo).wait_recv()

    @pl.loop(0, 2)
    def _(i):
        rs = pl.ds(at(half + i * 256), 256)
        outp[rs, :] = (x2[rs, :] + outp[rs, :].astype(f32) + outo[rows(i), :].astype(f32) + vec[12:13, :]).astype(bf)

    toks = ((outp, out_o), (dh1p, ig_o))

    def tok(wh, k, recv=False):
        src, dst = toks[wh]
        t, dev = seq_peer(k)
        row = (seq_peer(-k)[0] // 2) if recv else y
        return rcopy(src.at[pl.ds(at(half + lax.rem(t, 4) * 128), 128)], dst.at[row], tks.at[wh, k], tkr.at[wh, k], dev)

    def tok_keep(wh):
        src, dst = toks[wh]
        return pltpu.make_async_copy(src.at[pl.ds(at(half + lax.rem(s, 4) * 128), 128)], dst.at[y], los.at[2 + wh])

    def tok_start(wh, part=None):
        def now(t):
            return (t // 4 == c) if part is None else (t // 2 == 2 * c + part)

        for k in range(1, 8):

            @pl.when(now(seq_peer(k)[0]))
            def _():
                tok(wh, k).start()

        @pl.when(now(s))
        def _():
            tok_keep(wh).start()

    def tok_wait(wh):
        @pl.when(s // 4 == c)
        def _():
            tok_keep(wh).wait()

        for k in range(1, 8):

            @pl.when(lax.rem(seq_peer(-k)[0], 2) == s // 4)
            def _():
                tok(wh, k, True).wait_recv()

        for k in range(1, 8):

            @pl.when(seq_peer(k)[0] // 4 == c)
            def _():
                tok(wh, k).wait_send()

    tok_start(0)

    vg[...] = jnp.zeros_like(vg)
    one = (c == 0).astype(f32)
    attt = dyt

    @pl.loop(0, 4, unroll=2)
    def _(i):
        attt[:, rows(i)] = jnp.transpose(attf[rows(i), :])

    for n in range(3):
        ns = slice(n * 256, n * 256 + 256)
        ex(5 + n, dh2p.at[:, ns], dh2o.at[:, ns]).wait_recv()
        ex(5 + n, dh2p.at[:, ns], dh2o.at[:, ns]).wait_send()

    @pl.loop(0, 4, unroll=2)
    def _(i):
        cen, r = norm_stats(x2[rows(i), :])
        xh = cen * r
        dh = dh2p[rows(i), :].astype(f32) + dh2o[rows(i), :].astype(f32)
        dyv = dyr[rows(i), :].astype(f32)
        dx = dh * vec[2:3, :]
        dx = r * (dx - jnp.mean(dx, -1, keepdims=True) - xh * jnp.mean(dx * xh, -1, keepdims=True)) + dyv
        x2[rows(i), :] = dx
        do = dx.astype(bf)
        h1[rows(i), :] = do

        def sm(v):
            return jnp.sum(v, axis=0, keepdims=True) * one

        vg[2:3, :] += sm(dh * xh)
        vg[3:4, :] += sm(dh)
        vg[7:8, :] += sm(do.astype(f32))
        vg[12:13, :] += sm(dyv)
        invd[rows(i), :] = dot_nt(do, wo[mine, :]) * invd[rows(i), :]

    for q in (2, 0):
        r1_mid(1, q)
    for m in range(4):
        gq[m, :, :, 0:384] = dot(attt[m * 192 : m * 192 + 192, :], h1[:, mine]).astype(bf).reshape(4, 48, 384)
    gf[...] = jnp.zeros_like(gf)
    vsrc[...] = jnp.zeros_like(vsrc)
    lane = lax.broadcasted_iota(jnp.int32, (192, 128), 1)
    dproj = act

    backward = {
        (0, 3): ((r2_start, 1),),
        (0, 2): ((r2_end, 0),),
        (0, 1): ((r2_mid, 1),),
        (0, 0): ((r1_end, 1, 0),),
        (0, -1): ((d_start, 0),),
        (1, 3): ((r2_end, 1),),
        (1, 2): ((y_start, 0),),
        (1, 0): ((d_mid, 0),),
        (1, -1): ((d_start, 1),),
        (2, 3): ((d_end, 0),),
        (2, 2): ((d_mid, 1),),
        (2, 0): ((d_end, 1), (y_start, 1)),
    }

    @pl.loop(0, 3)
    def _(p):
        lanes = pl.ds(at(p * 128), 128)
        ql = pl.ds(at(p * 384), 128)
        kl = pl.ds(at(p * 384 + 128), 128)
        vl = pl.ds(at(p * 384 + 256), 128)
        bq, bk = feature_maps(p)
        dst = [None, None]
        fq = jnp.zeros((128, 128), f32)
        fk = jnp.zeros((128, 128), f32)
        for i in (3, 2, 1, 0):
            rs = slice(i * 256, i * 256 + 256)
            dn = invd[rs, lanes]
            dd = roll64(-(dn * attf[rs, pl.ds(at(own + p * 128), 128)].astype(f32)))
            v = qkv[rs, vl]
            qm, km, same = same_doc(segc, i)
            dq, dk, dv = [], [], []
            for h in range(2):
                mh = m0 == (h == 0)
                vx = jnp.where(mh, v, jnp.ones_like(v))
                dx = jnp.where(mh, dn, dd).astype(bf)
                qq = qf[2 * p + h, rs, :]
                kk = kf[2 * p + h, rs, :]
                a_t = (dot_nt(kk, qq) * maskt[i].astype(f32)).astype(bf)
                da = (dot_nt(dx, vx) * mask[i].astype(f32)).astype(bf)
                da_t = (dot_nt(vx, dx) * maskt[i].astype(f32)).astype(bf)
                gqf = dot(da, kk)
                gkf = dot(da_t, qq)
                gv = dot(a_t, dx)
                if i < 3:
                    ds = dst[h].astype(bf)
                    gkf = gkf + dot_nt(vx, ds) * km
                    gv = gv + dot(kk, ds) * km
                if i > 0:
                    gqf = gqf + dot_nt(dx, st[2 * p + h, i - 1]) * qm
                    new = dot_tn((qq.astype(f32) * qm).astype(bf), dx)
                    dst[h] = new if i == 3 else new + same * dst[h]
                dq.append(gqf)
                dk.append(gkf)
                dv.append(gv)
            zq = soft_back(qf[2 * p, rs, :], qf[2 * p + 1, rs, :], dq[0], dq[1], m0, ones)
            zk = soft_back(kf[2 * p, rs, :], kf[2 * p + 1, rs, :], dk[0], dk[1], m0, ones)
            fq = fq + dot_tn(qkv[rs, ql], zq)
            fk = fk + dot_tn(qkv[rs, kl], zk)
            dproj[rs, ql] = dot_nt(zq, bq).astype(bf)
            dproj[rs, kl] = dot_nt(zk, bk).astype(bf)
            dproj[rs, vl] = jnp.where(m0, dv[0], dv[1]).astype(bf)
            pump(backward, p, i)
        top = lax.broadcasted_iota(jnp.int32, (128, 128), 0) < 64
        ml = low_lanes((128, 128))
        gf[pl.ds(at(own + p * 128), 128), :] = jnp.where(
            top, jnp.where(ml, fq, roll64(fk)), jnp.where(ml, roll64(fq), fk)
        ).astype(bf)
        trio = pl.ds(at(p * 384), 384)
        sums3 = jnp.sum(dproj[:, trio].astype(f32), axis=0, keepdims=True)
        base = at(p * 384 + 256 * jnp.minimum(p, 1))
        for m in range(4):
            ms = slice(m * 192, m * 192 + 192)
            t = dot(h1t[ms, :], dproj[:, trio])
            wt = w[ms, pl.ds(base, 384)].astype(f32)
            gain = w[ms, VAT : VAT + 128].astype(f32)
            gq[m, :, :, pl.ds(at(384 + p * 384), 384)] = (t * gain[:, 0:1] + sums3 * gain[:, 1:2]).astype(bf).reshape(4, 48, 384)
            gg = jnp.sum(wt * t, axis=1, keepdims=True)
            gs = jnp.sum(wt * sums3, axis=1, keepdims=True)
            vsrc[ms, :] += jnp.where(lane == 0, gg, jnp.where(lane == 1, gs, 0.0))
        for n in range(3):
            vg[4 + n : 5 + n, pl.ds(at(own + p * 128), 128)] = sums3[:, n * 128 : n * 128 + 128]
        pump(backward, p, -1)

    for m in range(4):
        gq[m, :, :, 1536:1664] = gf[m * 192 : m * 192 + 192, :].reshape(4, 48, 128)
    d_start(2)
    for k in range(2):
        vg[pl.ds(8 + 2 * c + k, 1), :] = gb[0:1, k * 768 : k * 768 + 768]
    vsrc[...] += jnp.transpose(jnp.concatenate([vg[...], jnp.zeros((112, 768), f32)], axis=0))

    def vx_(a, e):
        t = lax.rem((x, z)[a] + e, 4)
        n = (192, 48)[a]
        src = vsrc.at[pl.ds(at(t * 192 if a == 0 else x * 192 + t * 48, 16), n)]
        return rcopy(src, (v1, v2)[a].at[e - 1], ss.at[8], vxr.at[a], axis_peer(a, e))

    for e in (2, 1, 3):
        vx_(0, e).start()

    def dh1_rows(r0):
        rs = pl.ds(at(r0), 256)
        for n in range(3):
            ns = slice(n * 256, n * 256 + 256)
            t = dot_nt(dproj[rs, 0:384], w[ns, 0:384]) + dot_nt(dproj[rs, 384:1152], w[ns, 640:1408])
            dh1p[rs, ns] = t.astype(bf)

    def dh1_ex(i):
        return ex(8 + i, dh1p.at[pl.ds(at(away + i * 256), 256)], dh1o.at[i * 256 : i * 256 + 256])

    def input_rows(i):
        dh1_ex(i).wait_recv()
        rs = pl.ds(at(half + i * 256), 256)
        cen, r = norm_stats(xr[rs, :].astype(f32))
        xh = cen * r
        dh = dh1p[rs, :].astype(f32) + dh1o[i * 256 : i * 256 + 256, :].astype(f32)
        dx = dh * vec[0:1, :]
        dx = r * (dx - jnp.mean(dx, -1, keepdims=True) - xh * jnp.mean(dx * xh, -1, keepdims=True))
        dh1p[rs, :] = (dx + x2[rs, :]).astype(bf)
        tok_start(1, i)

    dh1_rows(away)
    dh1_ex(0).start()
    dh1_rows(half)
    dh1_rows(away + 256)
    dh1_ex(1).start()
    take(v1, vxr.at[0])
    mid = pl.ds(at(x * 192, 16), 192)
    vsrc[mid, :] = vsrc[mid, :] + (v1[0] + v1[1] + v1[2])
    for e in (2, 1, 3):
        vx_(1, e).start()
    d_mid(2)
    input_rows(0)
    dh1_rows(half + 256)
    take(v2, vxr.at[1])
    d_end(2)
    y_start(2)
    input_rows(1)

    def sums(gp):
        take(yr.at[0:7, :, YCOLS[gp][0] : YCOLS[gp][1]], ysr.at[gp])
        tot = jnp.zeros((1, 1), f32)
        for d, wd, sr, sp in GPIECES:
            if not YCOLS[gp][0] <= d < YCOLS[gp][1]:
                continue
            for cc in range(2 if sp else 1):
                srcs = [2 * j + cc for j in range(4)] if sp else range(8)
                v = sum(yr[j, 0:6, d : d + wd].astype(f32) for j in srcs)
                pg_o[:, sr + sp * cc : sr + sp * cc + wd] = v
                tot = tot + jnp.sum(jnp.sum(v * v, axis=1, keepdims=True), axis=0, keepdims=True)
        return tot

    total = sums(0) + sums(1)
    total = total + sums(2)
    V = sum(yr[j, :, 1664:1792].astype(f32) for j in range(8))
    vs_o[...] = V[0:6, 0:13]
    total = total + jnp.sum(jnp.sum(V[0:6] * V[0:6], axis=1, keepdims=True), axis=0, keepdims=True)
    n2[pln] = jnp.broadcast_to(total, (8, 128))

    def nc2(k):
        return rcopy(n2.at[pln], n2.at[pln], ss.at[10], n2r.at[0], plane_peer(k))

    def nc1(k):
        return rcopy(n1.at[s], n1.at[s], ss.at[9], n1r.at[0], seq_peer(k)[1])

    for k in range(1, 16):
        nc2(k).start()
    take(n2.at[0:15], n2r.at[0])
    n1[s] = sum(n2[j] for j in range(16))
    for k in range(1, 8):
        nc1(k).start()
    sent(rcv.at[0:7], 0)
    sent(sg.at[0:7], 1)
    sent(xr.at[0:768], 2)
    sent(xr, 3)
    sent(w.at[0:720], 4)
    sent(g.at[0:720], 5)
    sent(w.at[0:720, 0:GC], 6)
    sent(rcv.at[0:7], 7)
    sent(vsrc.at[0:720], 8)
    sent(n2.at[0:15], 10)
    for wh in range(2):
        tok_wait(wh)
    ex(0, w.at[:, WOAT : WOAT + 384], wo.at[:, mine]).wait_send()
    for p in range(3):
        ex(1 + p, att_part(p), att_part(p)).wait_send()
    ex(4, outp.at[pl.ds(away, 512)], outo).wait_send()
    for i in range(2):
        dh1_ex(i).wait_send()
    take(n1.at[0:7], n1r.at[0])
    norm_o[...] = jnp.sqrt(sum(n1[j] for j in range(8)))[0:1, 0:1]
    sent(n1.at[0:7], 9)


def run_layer(par, vt, xin, dyin, sgin):
    V = pl.BlockSpec(memory_space=pltpu.VMEM)
    H = pl.BlockSpec(memory_space=pl.ANY)
    M = pltpu.VMEM
    DM = pltpu.SemaphoreType.DMA
    S = jax.ShapeDtypeStruct
    tok = (T, D)
    return pl.pallas_call(
        layer,
        out_shape=[S((4, 128, D), bf), S((4, 128, D), bf), S((6, 9344), f32), S((6, 13), f32), S((1, 1), f32)],
        in_specs=[V, V, H, H, V],
        out_specs=[H, H, V, V, V],
        scratch_shapes=[
            M((D, WC), bf), M((D, D), bf), M(tok, bf), M(tok, bf), M((8, 8, 128), f32), M((4, 8, 128), f32), M((2, 8, WC), bf), M((8, 8, WC), bf),
            M((16, D), f32), M(tok, bf), M((D, T), bf), M((T, 3 * HD), bf), M((6, T, 128), bf), M((6, T, 128), bf),
            M((T, HD), f32), M((6, 3, 128, 128), bf), M((T, 128), f32), M((4, 256, 256), bf), M((4, 256, 256), bf), M(tok, bf),
            M(tok, f32), M(tok, bf), M((D, T), bf), M((D, T), bf), M((T, FH), bf), M((T, FH), bf), M((512, D), bf),
            M(tok, bf), M((512, D), bf), M((D, 2 * FH), bf), M((576, 2 * FH), bf), M((144, 2 * FH), bf),
            M((4, 4, 48, GC), bf), M((3, 4, 48, GC), bf), M((3, 48, GC), bf), M((D, 128), bf),
            M((8, 8, WC), bf), M((8, 8, 128), f32), M((16, 8, 128), f32), M((16, D), f32), M((8, FH), f32),
            M((D, 128), f32), M((3, 192, 128), f32), M((3, 48, 128), f32),
            DM((11,)), DM((3,)), DM((1,)), DM((2,)), DM((2,)), DM((4, 10)), DM((2, 4, 2)), DM((2, 2)), DM((3,)), DM((3,)), DM((3,)), DM((2,)),
            DM((1,)), DM((1,)), DM((11,)), DM((11,)), DM((2, 8)), DM((2, 8)), DM((4,)),
        ],
        compiler_params=pltpu.CompilerParams(collective_id=0, has_side_effects=True, vmem_limit_bytes=64 * 2**20 - 2**17),
        name="layer",
    )(par, vt, xin, dyin, sgin)


def adamw(weight, grad, m, v, scale, rate, decay):
    grad = grad * scale
    m = 0.5 * m + 0.5 * grad
    v = 0.5 * v + 0.5 * grad * grad
    return grad, weight - rate * (m / (jnp.sqrt(v) + 1e-8) + decay * weight), m, v


def finish(out, ig, pg, norm, par, pm, pv, out_o, ig_o, *p_o):
    out_o[...] = out[...]
    ig_o[...] = ig[...].astype(f32)

    @pl.when(pl.program_id(0) == 0)
    def _():
        scale = 1.0 / jnp.maximum(norm[...], 1.0)
        for a in range(0, 9344, 1024):
            e = slice(a, min(a + 1024, 9344))
            for ref, val in zip(p_o, adamw(par[:, e], pg[:, e], pm[:, e], pv[:, e], scale, 0.05, 0.1)):
                ref[:, e] = val


def run_finish(out, ig, pg, norm, par, pm, pv):
    S = jax.ShapeDtypeStruct
    tok = pl.BlockSpec((2, 128, D), lambda i: (i, 0, 0))
    mat = pl.BlockSpec((6, 9344), lambda i: (0, 0))
    one = pl.BlockSpec((1, 1), lambda i: (0, 0))
    return pl.pallas_call(
        finish,
        grid=(2,),
        out_shape=[S((4, 128, D), bf), S((4, 128, D), f32)] + [S((6, 9344), f32)] * 4,
        in_specs=[tok, tok, mat, one, mat, mat, mat],
        out_specs=[tok, tok] + [mat] * 4,
        compiler_params=pltpu.CompilerParams(vmem_limit_bytes=62 * 2**20),
        name="finish",
    )(out, ig, pg, norm, par, pm, pv)


def body(inputs, segment_ids, out_grad, params, vectors, params_m, params_v, vectors_m, vectors_v):
    out, ig, pg, vs, norm = run_layer(params, vectors.T, inputs, out_grad, segment_ids)
    scale = 1.0 / jnp.maximum(norm[0, 0], 1.0)
    q = adamw(vectors.T, vs, vectors_m.T, vectors_v.T, scale, 0.2, 0.0)
    done = run_finish(out, ig, pg, norm, params, params_m, params_v)
    return (done[0], done[1], norm.reshape(1)) + tuple(done[2:]) + tuple(t.T for t in q)


def solution(mesh):
    torus = Mesh(mesh.devices.reshape(4, 4, 4, 2), ("x", "z", "y", "c"))
    row, seq, every = ("x", "z"), ("y", "c"), ("x", "z", "y", "c")
    tok, mat, vec = P(row, seq, None), P(every, None), P(None, every)
    return jax.shard_map(
        body,
        mesh=torus,
        in_specs=(tok, P(row, seq), tok, mat, vec, mat, mat, vec, vec),
        out_specs=(tok, tok, P(), mat, mat, mat, mat, vec, vec, vec, vec),
        check_vma=False,
    )
```

```python
import jax
import jax.numpy as jnp
from jax import lax
from jax.experimental import pallas as pl
from jax.experimental.pallas import tpu as pltpu
from jax.sharding import Mesh
from jax.sharding import PartitionSpec as P

f32 = jnp.float32
bf = jnp.bfloat16
MESH = pl.DeviceIdType.MESH
T, D, HD, FH = 1024, 768, 384, 1536
WC = 4864
GC = 1664
PIECES = (
    (0, 128, 0, 384), (128, 128, 768, 384), (256, 128, 1536, 384), (384, 128, 3072, 0),
    (640, 128, 128, 384), (768, 128, 896, 384), (896, 128, 1664, 384),
    (1024, 128, 256, 384), (1152, 128, 1024, 384), (1280, 128, 1792, 384), (1408, 384, 2304, 384),
    (1792, 768, 3200, 1536), (2560, 768, 6272, 1536), (3328, 768, 3968, 1536), (4096, 768, 7040, 1536),
)
VAT = 512
WOAT = 1408
FAT = 384
STAGE = ((0, 640), (640, 1792), (1792, 4864))
GATHER = ((0, 256, 640), (640, 1152, 1792), (1792, 2560, 3328), (3328, 4096, 4864))
GPIECES = (
    (0, 384, 2304, 384), (384, 128, 0, 384), (512, 128, 768, 384), (640, 128, 1536, 384),
    (768, 128, 128, 384), (896, 128, 896, 384), (1024, 128, 1664, 384),
    (1152, 128, 256, 384), (1280, 128, 1024, 384), (1408, 128, 1792, 384), (1536, 128, 3072, 0),
    (1792, 768, 3200, 1536), (2560, 768, 6272, 1536), (3328, 768, 3968, 1536), (4096, 768, 7040, 1536),
)
REDUCE = ((1792, 2560, 3328), (3328, 4096, 4864))
DIRECT = (((0, 384), (384, 768)), ((768, 896), (896, 1152)), ((1152, 1408), (1408, 1664)))
YCOLS = ((1792, 4864), (0, 1152), (1152, 1792))
FAR = (0, -1, 1, 2)
BIG = 3.0e38


def dot(a, b):
    return lax.dot_general(a, b, (((1,), (0,)), ((), ())), preferred_element_type=f32)


def dot_nt(a, b):
    return lax.dot_general(a, b, (((1,), (1,)), ((), ())), preferred_element_type=f32)


def dot_tn(a, b):
    return lax.dot_general(a, b, (((0,), (0,)), ((), ())), preferred_element_type=f32)


def at(v, m=128):
    return pl.multiple_of(v, m)


def rows(i, n=256):
    return pl.ds(at(i * n), n)


def low_lanes(shape):
    return lax.broadcasted_iota(jnp.int32, shape, len(shape) - 1) < 64


def roll64(v):
    return pltpu.roll(v, 64, 1)


def slab(xx, zz):
    return at((lax.rem(xx + 8, 4) * 4 + lax.rem(zz + 8, 4)) * 48, 16)


def norm_stats(v):
    mu = jnp.mean(v, axis=-1, keepdims=True)
    cen = v - mu
    return cen, lax.rsqrt(jnp.mean(cen * cen, axis=-1, keepdims=True) + 1e-5)


def seg_ones():
    a = lax.broadcasted_iota(jnp.int32, (128, 128), 0) < 64
    return (a == low_lanes((128, 128))).astype(bf)


def feats(z, m0, ones):
    mx = jnp.where(m0, jnp.max(jnp.where(m0, z, -BIG), -1, keepdims=True), jnp.max(jnp.where(m0, -BIG, z), -1, keepdims=True))
    mn = jnp.where(m0, jnp.min(jnp.where(m0, z, BIG), -1, keepdims=True), jnp.min(jnp.where(m0, BIG, z), -1, keepdims=True))
    ep = jnp.exp(z - mx).astype(bf)
    en = jnp.exp(mn - z).astype(bf)
    fp = ep.astype(f32) / dot(ep, ones)
    fn = roll64(en.astype(f32) / dot(en, ones))
    return jnp.where(m0, fp, fn).astype(bf), jnp.where(m0, fn, fp).astype(bf)


def soft_back(fe, fo, de, do, m0, ones):
    fe = fe.astype(f32)
    fo = fo.astype(f32)
    fp = jnp.where(m0, fe, fo)
    fr = jnp.where(m0, fo, fe)
    tp = fp * jnp.where(m0, de, do)
    tr = fr * jnp.where(m0, do, de)

    def total(t):
        hi = t.astype(bf)
        return dot(hi, ones) + dot((t - hi.astype(f32)).astype(bf), ones)

    return ((tp - fp * total(tp)) - roll64(tr - fr * total(tr))).astype(bf)


def same_doc(segc, i):
    sc = segc[i * 256 : i * 256 + 256, :]
    last = segc[i * 256 + 255 : i * 256 + 256, :]
    km = (sc == last).astype(f32)
    if i == 0:
        return None, km, None
    prev = segc[i * 256 - 1 : i * 256, :]
    return (sc == prev).astype(f32), km, (last == prev).astype(f32)


def layer(
    par, vt, xin, dyin, sgin,
    out_o, ig_o, pg_o, vs_o, norm_o,
    w, wo, xr, dyr, sg, sgb, wire, rcv, vec, h1, h1t, qkv, qf, kf, invd, st, segc, mask, maskt, attf,
    x2, h2, h2t, dyt, act, du, outo, dh2o, dh1o, g, r1, r2, gq, d1, d2, gf, yr, n1, n2, vg, gb, vsrc, v1, v2,
    ss, s0r, sgr, rsr, sbr, agr, t1r, t2r, d1r, d2r, ysr, vxr, n1r, n2r, exs, exr, tks, tkr, los,
):
    x, z, y, c = (lax.axis_index(a) for a in ("x", "z", "y", "c"))
    s = y * 2 + c
    pln = x * 4 + z
    own = at(c * 384)

    def rcopy(src, dst, ss, rs, dev):
        return pltpu.make_async_remote_copy(src, dst, ss, rs, device_id=dev, device_id_type=MESH)

    def take(ref, sem):
        rcopy(ref, ref, sem, sem, other).wait_recv()

    def sent(ref, i):
        rcopy(ref, ref, ss.at[i], ss.at[i], other).wait_send()

    def seq_peer(k):
        t = lax.rem(s + k + 8, 8)
        return t, {"y": t // 2, "c": lax.rem(t, 2)}

    def axis_peer(a, k):
        return {("x", "z")[a]: lax.rem((x, z)[a] + k + 4, 4)}

    def plane_peer(k):
        t = lax.rem(pln + k, 16)
        return {"x": t // 4, "z": lax.rem(t, 4)}

    other = {"c": 1 - c}

    bar = pltpu.get_barrier_semaphore()
    for k in range(1, 8):
        pl.semaphore_signal(bar, inc=1, device_id=seq_peer(k)[1], device_id_type=MESH)
    for k in range(1, 16):
        pl.semaphore_signal(bar, inc=1, device_id=plane_peer(k), device_id_type=MESH)
    for cc in range(2):
        wire[cc, :, :] = jnp.zeros((8, WC), bf)
        for d, wd, sr, sp in PIECES:
            wire[cc, 0:6, d : d + wd] = par[:, sr + sp * cc : sr + sp * cc + wd].astype(bf)
        wire[cc, 0:6, VAT : VAT + 13] = vt[...].astype(bf)
    for j in range(4):
        sgb[j] = jnp.broadcast_to(sgin[j : j + 1, :].astype(f32), (8, 128))
    pl.semaphore_wait(bar, 22)

    def st0(gp, k):
        t, dev = seq_peer(k)
        a, b = STAGE[gp]
        return rcopy(wire.at[dev["c"], :, a:b], rcv.at[s, :, a:b], ss.at[0], s0r.at[gp], dev)

    def sgc(k):
        t, dev = seq_peer(k)
        return rcopy(sgb.at[t // 2], sg.at[s], ss.at[1], sgr.at[0], dev)

    pairs = ((xin, xr), (dyin, dyr))

    def res(wh, k):
        src, dst = pairs[wh]
        j = lax.rem(y + k, 4)
        return rcopy(src.at[j], dst.at[rows(s, 128)], ss.at[2], rsr.at[wh], {"y": j})

    def keep(wh):
        src, dst = pairs[wh]
        return pltpu.make_async_copy(src.at[y], dst.at[rows(s, 128)], los.at[wh])

    def sib(wh, k):
        ref = pairs[wh][1].at[rows(lax.rem(y - k + 4, 4) * 2 + c, 128)]
        return rcopy(ref, ref, ss.at[3], sbr.at[wh], other)

    def res_start(wh):
        keep(wh).start()
        for k in (2, 1, 3):
            res(wh, k).start()

    def res_pass(wh):
        keep(wh).wait()
        sib(wh, 0).start()
        take(pairs[wh][1].at[0:384], rsr.at[wh])
        for k in range(1, 4):
            sib(wh, k).start()

    def res_end(wh):
        take(pairs[wh][1].at[0:512], sbr.at[wh])

    def pos(p, d1, d2):
        return slab(x + d1, z + d2) if p == 0 else slab(x + d2, z + d1)

    def along(p, phase, way):
        return axis_peer((p + phase) % 2, way)

    def ag(gp, p, sem, d1, d2, phase, way):
        ref = w.at[pl.ds(pos(p, d1, d2), 48), GATHER[gp][p] : GATHER[gp][p + 1]]
        return rcopy(ref, ref, ss.at[4], agr.at[gp, sem], along(p, phase, way))

    def ag_take(gp, sem):
        take(w.at[0 : (96, 48)[sem % 2], GATHER[gp][0] : GATHER[gp][2]], agr.at[gp, sem])

    def p2send(gp, q):
        for p in range(2):
            ag(gp, p, 2 + 2 * q, FAR[q], 0, 1, 1).start()
            ag(gp, p, 2 + 2 * q, FAR[q], 0, 1, -1).start()

    def ag_d(gp, q):
        ag_take(gp, 2 + 2 * q)
        way = (1, -1, -1, 1)[q]
        for p in range(2):
            ag(gp, p, 3 + 2 * q, FAR[q], -way, 1, way).start()

    def ag_a(gp):
        for p in range(2):
            ag(gp, p, 0, 0, 0, 0, 1).start()
            ag(gp, p, 0, 0, 0, 0, -1).start()
        p2send(gp, 0)

    def ag_b(gp):
        ag_take(gp, 0)
        ag(gp, 0, 1, -1, 0, 0, 1).start()
        ag(gp, 1, 1, 1, 0, 0, -1).start()
        p2send(gp, 1)
        p2send(gp, 2)

    def ag_c(gp):
        ag_take(gp, 1)
        p2send(gp, 3)
        ag_d(gp, 0)

    def ag_e(gp):
        for q in range(4):
            ag_take(gp, 3 + 2 * q)

    rr = lax.broadcasted_iota(jnp.int32, (48, 64), 0)
    rc = lax.broadcasted_iota(jnp.int32, (48, 64), 1)
    spread = ((lax.rem(rr, 6) == lax.rem(rc, 8)) & (rr // 6 == rc // 8)).astype(bf)

    def assemble(gp):
        a, b = STAGE[gp]
        take(rcv.at[0:7, :, a:b], s0r.at[gp])
        n = (640, 1152, 768)[gp]
        for lo in range(a, b, n):
            raw = jnp.concatenate([rcv[t, :, lo : lo + n].astype(f32) for t in range(8)], axis=0).astype(bf)
            w[pl.ds(slab(x, z), 48), lo : lo + n] = dot(spread, raw).astype(bf)

    for k in range(1, 8):
        st0(0, k).start()
    for k in range(1, 8):
        st0(1, k).start()
    for k in range(1, 8):
        sgc(k).start()
    res_start(0)
    for k in range(1, 8):
        st0(2, k).start()
    sg[s] = sgb[y]
    rcv[s] = wire[c]
    assemble(0)
    ag_a(0)
    assemble(1)
    ag_a(1)
    ag_b(0)
    take(sg.at[0:7], sgr.at[0])
    for b in range(8):
        segc[b * 128 : b * 128 + 128, :] = jnp.transpose(jnp.broadcast_to(sg[b, 0:1, :], (128, 128)))
    mr = lax.broadcasted_iota(jnp.int32, (256, 256), 0)
    mc = lax.broadcasted_iota(jnp.int32, (256, 256), 1)
    for i in range(4):
        row = jnp.concatenate([sg[2 * i, 0:1, :], sg[2 * i + 1, 0:1, :]], axis=1)
        col = segc[i * 256 : i * 256 + 256, :]
        eq = jnp.concatenate([col, col], axis=1) == row
        mask[i] = jnp.where(eq & (mc <= mr), 1.0, 0.0).astype(bf)
        maskt[i] = jnp.where(eq & (mr <= mc), 1.0, 0.0).astype(bf)
    ag_c(0)
    for q in (1, 2):
        ag_d(0, q)
    res_pass(0)
    ag_b(1)
    ag_d(0, 3)
    res_end(0)
    res_start(1)

    @pl.loop(0, 4, unroll=2)
    def _(i):
        cen, r = norm_stats(xr[rows(i), :].astype(f32))
        x2[rows(i), :] = cen * r

    ag_c(1)
    assemble(2)
    ag_a(2)
    ag_e(0)

    def ex(i, src, dst):
        return rcopy(src, dst, exs.at[i], exr.at[i], other)

    mine = pl.ds(own, 384)

    vec[...] = jnp.transpose(w[:, VAT : VAT + 128].astype(f32))[0:16]

    @pl.loop(0, 4, unroll=2)
    def _(i):
        h = (x2[rows(i), :] * vec[0:1, :] + vec[1:2, :]).astype(bf)
        h1[rows(i), :] = h
        h1t[:, rows(i)] = jnp.transpose(x2[rows(i), :].astype(bf))

    ones = seg_ones()
    m0 = low_lanes((256, 128))

    def feature_maps(p):
        F = w[pl.ds(at(own + p * 128), 128), FAT : FAT + 128].astype(f32)
        R = roll64(F)
        top = lax.broadcasted_iota(jnp.int32, (128, 128), 0) < 64
        ml = low_lanes((128, 128))
        zz = jnp.zeros_like(F)
        bq = jnp.where(top & ml, F, jnp.where(top | ml, zz, R))
        bk = jnp.where(top & ml, R, jnp.where(top | ml, zz, F))
        return bq.astype(bf), bk.astype(bf)

    def pump(table, p, i):
        for (pp, ii), todo in table.items():
            if ii == i:

                @pl.when(p == pp)
                def _():
                    for t in todo:
                        t[0](*t[1:])

    def wo_start():
        ex(0, w.at[:, WOAT : WOAT + 384], wo.at[:, mine]).start()
        wo[:, mine] = w[:, WOAT : WOAT + 384]

    forward = {
        (0, 0): ((ag_d, 1, 1), (ag_d, 1, 2)),
        (0, 1): ((ag_d, 1, 3),),
        (0, 2): ((ag_b, 2), (ag_a, 3)),
        (0, 3): ((ag_e, 1), (wo_start,)),
        (1, 1): ((ag_c, 2), (res_pass, 1)),
        (1, 3): ((ag_d, 2, 1), (ag_d, 2, 2)),
        (2, 0): ((ag_b, 3),),
        (2, 1): ((ag_d, 2, 3),),
        (2, 3): ((ag_c, 3),),
    }

    def att_part(p):
        return attf.at[:, pl.ds(at(own + p * 128), 128)]

    @pl.loop(0, 3)
    def _(p):
        lanes = pl.ds(at(p * 128), 128)
        bq, bk = feature_maps(p)
        base = at(p * 384 + 256 * jnp.minimum(p, 1))
        part = pl.ds(at(own + p * 128), 128)
        bias = jnp.concatenate([vec[4:5, part], vec[5:6, part], vec[6:7, part]], axis=1)
        state = [None, None]
        for i in range(4):
            rs = slice(i * 256, i * 256 + 256)
            pr = (dot(h1[rs, :], w[:, pl.ds(base, 384)]) + bias).astype(bf)
            qkv[rs, pl.ds(at(p * 384), 384)] = pr
            qe, qo = feats(dot(pr[:, 0:128], bq), m0, ones)
            ke, ko = feats(dot(pr[:, 128:256], bk), m0, ones)
            v = pr[:, 256:384]
            qm, km, same = same_doc(segc, i)
            outs = []
            for h, (qq, kk) in enumerate(((qe, ke), (qo, ko))):
                vx = jnp.where(m0 == (h == 0), v, jnp.ones_like(v))
                qf[2 * p + h, rs, :] = qq
                kf[2 * p + h, rs, :] = kk
                o = dot((dot_nt(qq, kk) * mask[i].astype(f32)).astype(bf), vx)
                if i > 0:
                    sb = state[h].astype(bf)
                    st[2 * p + h, i - 1] = sb
                    o = o + dot(qq, sb) * qm
                if i < 3:
                    sn = dot_tn((kk.astype(f32) * km).astype(bf), vx)
                    state[h] = sn if i == 0 else sn + same * state[h]
                outs.append(o)
            num = jnp.where(m0, outs[0], outs[1])
            inv = 1.0 / roll64(jnp.where(m0, outs[1], outs[0]))
            invd[rs, lanes] = inv
            attf[rs, part] = (num * inv).astype(bf)
            if i == 3:
                ex(1 + p, att_part(p), att_part(p)).start()
            pump(forward, p, i)

    res_end(1)
    ex(0, w.at[:, WOAT : WOAT + 384], wo.at[:, pl.ds(at((1 - c) * 384), 384)]).wait_recv()
    for p in range(3):
        part = attf.at[:, pl.ds(at((1 - c) * 384 + p * 128), 128)]
        ex(1 + p, part, part).wait_recv()

    @pl.loop(0, 4, unroll=2)
    def _(i):
        v = xr[rows(i), :].astype(f32) + dot(attf[rows(i), :], wo[...]) + vec[7:8, :]
        x2[rows(i), :] = v
        cen, r = norm_stats(v)
        h = (cen * r * vec[2:3, :] + vec[3:4, :]).astype(bf)
        h2[rows(i), :] = h
        h2t[:, rows(i)] = jnp.transpose(h)
        dyt[:, rows(i)] = jnp.transpose(dyr[rows(i), :])

    k0 = 0.7978845608028654
    k1 = 0.044715

    def mlp(j):
        far = at(1792 + (j // 3) * 768 + j * 256)
        cu = pl.ds(far, 256)
        cd = pl.ds(at(far + 768), 256)
        gu = pl.ds(at(far - 1792), 256)
        gd = pl.ds(at(far - 1024), 256)
        cj = pl.ds(at(j * 256), 256)
        off = c * FH + j * 256
        bu = vec[pl.ds(8 + off // D, 1), pl.ds(at(lax.rem(off, D)), 256)]

        @pl.loop(0, 4, unroll=4)
        def _(i):
            u = dot(h2[rows(i), :], w[:, cu]) + bu
            u2 = u * u
            t = jnp.tanh(k0 * (u + k1 * u2 * u))
            act[rows(i), cj] = (0.5 * u * (1.0 + t)).astype(bf)
            da = dot(dyr[rows(i), :], w[:, cd])
            gp = 0.5 * (1.0 + t) + 0.5 * u * (1.0 - t * t) * (k0 * (1.0 + (3 * k1) * u2))
            d = (gp * da).astype(bf)
            du[rows(i), cj] = d
            gb[0:1, cj] = gb[0:1, cj] + jnp.sum(d.astype(f32), axis=0, keepdims=True)

        for m in range(3):
            ms = slice(m * 256, m * 256 + 256)
            g[ms, gd] = dot(dyt[ms, :], act[:, cj]).astype(bf)
            g[ms, gu] = dot(h2t[ms, :], du[:, cj]).astype(bf)

    def gref(gp, p, d1, d2):
        return g.at[pl.ds(pos(p, d1, d2), 48), REDUCE[gp][p] - 1792 : REDUCE[gp][p + 1] - 1792]

    def land(gp, p, slot):
        r = slice(slot % 12 * 48, slot % 12 * 48 + 48)
        return (r1 if slot < 12 else r2).at[r, REDUCE[gp][p] - 1792 : REDUCE[gp][p + 1] - 1792]

    def tree_take(n, sem):
        take(r1.at[0:n, 0:1536], sem)

    def c1(gp, p, q, kind):
        way = (1, -1, -1, 1)[q]
        e = (2, way, -way)[kind]
        return rcopy(gref(gp, p, FAR[q], e), land(gp, p, q * 3 + kind), ss.at[5], t1r.at[gp, q, (kind + 1) // 2], along(p, 1, -way if kind == 2 else way))

    def c2(gp, p, kind):
        way = (1, -1)[p]
        e = (2, way, -way)[kind]
        return rcopy(gref(gp, p, e, 0), land(gp, p, 12 + kind), ss.at[5], t2r.at[gp, (kind + 1) // 2], along(p, 0, -way if kind == 2 else way))

    def acc(dst, *srcs):
        t = dst[...].astype(f32)
        for r in srcs:
            t = t + r[...].astype(f32)
        dst[...] = t.astype(bf)

    def r1_start(gp):
        for q in (3, 1, 2, 0):
            for p in range(2):
                c1(gp, p, q, 0).start()
                c1(gp, p, q, 2).start()

    def r1_mid(gp, q):
        tree_take(48, t1r.at[gp, q, 0])
        for p in range(2):
            acc(gref(gp, p, FAR[q], (1, -1, -1, 1)[q]), land(gp, p, q * 3))
            c1(gp, p, q, 1).start()

    def r1_end(gp, q):
        tree_take(96, t1r.at[gp, q, 1])
        for p in range(2):
            acc(gref(gp, p, FAR[q], 0), land(gp, p, q * 3 + 1), land(gp, p, q * 3 + 2))

    def r2_start(gp):
        for q in (3, 1, 2):
            r1_end(gp, q)
        for p in range(2):
            c2(gp, p, 0).start()
            c2(gp, p, 2).start()

    def r2_mid(gp):
        tree_take(48, t2r.at[gp, 0])
        for p in range(2):
            acc(gref(gp, p, (1, -1)[p], 0), land(gp, p, 12))
            c2(gp, p, 1).start()

    def r2_end(gp):
        tree_take(96, t2r.at[gp, 1])
        for p in range(2):
            acc(gref(gp, p, 0, 0), land(gp, p, 13), land(gp, p, 14))

    tr = lax.broadcasted_iota(jnp.int32, (64, 48), 0)
    tc = lax.broadcasted_iota(jnp.int32, (64, 48), 1)
    split = ((lax.rem(tc, 6) == lax.rem(tr, 8)) & (tc // 6 == tr // 8)).astype(bf)

    def dcp(gp, p, phase, e):
        a, b = DIRECT[gp][p]
        first = p == 0
        if phase == 0:
            t = lax.rem((z if first else x) + e, 4)
            src = gq.at[:, t, :, a:b] if first else gq.at[t, :, :, a:b]
            return rcopy(src, d1.at[e - 1, :, :, a:b], ss.at[6], d1r.at[gp], axis_peer(1 if first else 0, e))
        t = lax.rem((x if first else z) + e, 4)
        src = gq.at[t, z, :, a:b] if first else gq.at[x, t, :, a:b]
        return rcopy(src, d2.at[e - 1, :, a:b], ss.at[6], d2r.at[gp], axis_peer(0 if first else 1, e))

    def d_start(gp):
        for e in (2, 1, 3):
            for p in range(2):
                dcp(gp, p, 0, e).start()

    def d_mid(gp):
        take(d1.at[:, :, :, DIRECT[gp][0][0] : DIRECT[gp][1][1]], d1r.at[gp])
        for p in range(2):
            a, b = DIRECT[gp][p]
            for k in range(4):
                dst = gq.at[k, z, :, a:b] if p == 0 else gq.at[x, k, :, a:b]
                acc(dst, *[d1.at[e, k, :, a:b] for e in range(3)])
            for e in (2, 1, 3):
                dcp(gp, p, 1, e).start()

    def d_end(gp):
        take(d2.at[:, :, DIRECT[gp][0][0] : DIRECT[gp][1][1]], d2r.at[gp])
        for p in range(2):
            a, b = DIRECT[gp][p]
            acc(gq.at[x, z, :, a:b], *[d2.at[e, :, a:b] for e in range(3)])

    def ycp(gp, k):
        t, dev = seq_peer(k)
        a, b = YCOLS[gp]
        return rcopy(rcv.at[t, :, a:b], yr.at[s, :, a:b], ss.at[7], ysr.at[gp], dev)

    def deal(a, b, part):
        out = dot(split, part).astype(bf)
        for t in range(8):
            rcv[t, :, a:b] = out[8 * t : 8 * t + 8]

    def y_start(gp):
        a, b = YCOLS[gp]
        if gp == 0:
            for lo in range(0, 3072, 768):
                deal(1792 + lo, 2560 + lo, g[pl.ds(slab(x, z), 48), lo : lo + 768])
        elif gp == 1:
            deal(0, 1152, gq[x, z, :, 0:1152])
        else:
            deal(1152, 1664, gq[x, z, :, 1152:1664])
            deal(1664, 1792, (vsrc[pl.ds(slab(x, z), 48), :] + (v2[0] + v2[1] + v2[2])).astype(bf))
        for k in range(1, 8):
            ycp(gp, k).start()
        yr[s, :, a:b] = rcv[s, :, a:b]

    gb[...] = jnp.zeros_like(gb)
    for q in (1, 2, 3):
        ag_d(3, q)
    ag_e(2)
    pl.loop(0, 3)(mlp)
    r1_start(0)
    ag_e(3)
    pl.loop(3, 6)(mlp)
    for q in (3, 1, 2, 0):
        r1_mid(0, q)
    r1_start(1)

    outp, dh2p, dh1p = h2, h1, du.at[:, 0:768]
    half = at(c * 512)
    away = at((1 - c) * 512)

    @pl.loop(0, 4, unroll=2)
    def _(i):
        for n in range(3):
            ns = slice(n * 256, n * 256 + 256)
            outp[rows(i), ns] = (dot_nt(act[rows(i), 0:768], w[ns, 2560:3328]) + dot_nt(act[rows(i), 768:1536], w[ns, 4096:4864])).astype(bf)

    ex(4, outp.at[pl.ds(away, 512)], outo).start()
    r2_start(0)
    for n in range(3):
        ns = slice(n * 256, n * 256 + 256)

        @pl.loop(0, 4, unroll=2)
        def _(i):
            dh2p[rows(i), ns] = (dot_nt(du[rows(i), 0:768], w[ns, 1792:2560]) + dot_nt(du[rows(i), 768:1536], w[ns, 3328:4096])).astype(bf)

        ex(5 + n, dh2p.at[:, ns], dh2o.at[:, ns]).start()
    ex(4, outp.at[pl.ds(away, 512)], outo).wait_recv()

    @pl.loop(0, 2)
    def _(i):
        rs = pl.ds(at(half + i * 256), 256)
        outp[rs, :] = (x2[rs, :] + outp[rs, :].astype(f32) + outo[rows(i), :].astype(f32) + vec[12:13, :]).astype(bf)

    toks = ((outp, out_o), (dh1p, ig_o))

    def tok(wh, k, recv=False):
        src, dst = toks[wh]
        t, dev = seq_peer(k)
        row = (seq_peer(-k)[0] // 2) if recv else y
        return rcopy(src.at[pl.ds(at(half + lax.rem(t, 4) * 128), 128)], dst.at[row], tks.at[wh, k], tkr.at[wh, k], dev)

    def tok_keep(wh):
        src, dst = toks[wh]
        return pltpu.make_async_copy(src.at[pl.ds(at(half + lax.rem(s, 4) * 128), 128)], dst.at[y], los.at[2 + wh])

    def tok_start(wh, part=None):
        def now(t):
            return (t // 4 == c) if part is None else (t // 2 == 2 * c + part)

        for k in range(1, 8):

            @pl.when(now(seq_peer(k)[0]))
            def _():
                tok(wh, k).start()

        @pl.when(now(s))
        def _():
            tok_keep(wh).start()

    def tok_wait(wh):
        @pl.when(s // 4 == c)
        def _():
            tok_keep(wh).wait()

        for k in range(1, 8):

            @pl.when(lax.rem(seq_peer(-k)[0], 2) == s // 4)
            def _():
                tok(wh, k, True).wait_recv()

        for k in range(1, 8):

            @pl.when(seq_peer(k)[0] // 4 == c)
            def _():
                tok(wh, k).wait_send()

    tok_start(0)

    vg[...] = jnp.zeros_like(vg)
    one = (c == 0).astype(f32)
    attt = dyt

    @pl.loop(0, 4, unroll=2)
    def _(i):
        attt[:, rows(i)] = jnp.transpose(attf[rows(i), :])

    for n in range(3):
        ns = slice(n * 256, n * 256 + 256)
        ex(5 + n, dh2p.at[:, ns], dh2o.at[:, ns]).wait_recv()
        ex(5 + n, dh2p.at[:, ns], dh2o.at[:, ns]).wait_send()

    @pl.loop(0, 4, unroll=2)
    def _(i):
        cen, r = norm_stats(x2[rows(i), :])
        xh = cen * r
        dh = dh2p[rows(i), :].astype(f32) + dh2o[rows(i), :].astype(f32)
        dyv = dyr[rows(i), :].astype(f32)
        dx = dh * vec[2:3, :]
        dx = r * (dx - jnp.mean(dx, -1, keepdims=True) - xh * jnp.mean(dx * xh, -1, keepdims=True)) + dyv
        x2[rows(i), :] = dx
        do = dx.astype(bf)
        h1[rows(i), :] = do

        def sm(v):
            return jnp.sum(v, axis=0, keepdims=True) * one

        vg[2:3, :] += sm(dh * xh)
        vg[3:4, :] += sm(dh)
        vg[7:8, :] += sm(do.astype(f32))
        vg[12:13, :] += sm(dyv)
        invd[rows(i), :] = dot_nt(do, wo[mine, :]) * invd[rows(i), :]

    r2_mid(0)
    r1_end(0, 0)
    for q in (3, 1, 2, 0):
        r1_mid(1, q)
    for m in range(4):
        gq[m, :, :, 0:384] = dot(attt[m * 192 : m * 192 + 192, :], h1[:, mine]).astype(bf).reshape(4, 48, 384)
    gf[...] = jnp.zeros_like(gf)
    vsrc[...] = jnp.zeros_like(vsrc)
    lane = lax.broadcasted_iota(jnp.int32, (192, 128), 1)
    dproj = act

    backward = {
        (0, 3): ((r2_end, 0),),
        (0, 2): ((r2_start, 1),),
        (0, 0): ((r2_mid, 1), (r1_end, 1, 0)),
        (0, -1): ((d_start, 0),),
        (1, 3): ((r2_end, 1),),
        (1, 2): ((y_start, 0),),
        (1, -1): ((d_start, 1),),
        (2, 3): ((d_mid, 0),),
        (2, 1): ((d_end, 0),),
    }

    @pl.loop(0, 3)
    def _(p):
        lanes = pl.ds(at(p * 128), 128)
        ql = pl.ds(at(p * 384), 128)
        kl = pl.ds(at(p * 384 + 128), 128)
        vl = pl.ds(at(p * 384 + 256), 128)
        bq, bk = feature_maps(p)
        dst = [None, None]
        fq = jnp.zeros((128, 128), f32)
        fk = jnp.zeros((128, 128), f32)
        for i in (3, 2, 1, 0):
            rs = slice(i * 256, i * 256 + 256)
            dn = invd[rs, lanes]
            dd = roll64(-(dn * attf[rs, pl.ds(at(own + p * 128), 128)].astype(f32)))
            v = qkv[rs, vl]
            qm, km, same = same_doc(segc, i)
            dq, dk, dv = [], [], []
            for h in range(2):
                mh = m0 == (h == 0)
                vx = jnp.where(mh, v, jnp.ones_like(v))
                dx = jnp.where(mh, dn, dd).astype(bf)
                qq = qf[2 * p + h, rs, :]
                kk = kf[2 * p + h, rs, :]
                a_t = (dot_nt(kk, qq) * maskt[i].astype(f32)).astype(bf)
                da = (dot_nt(dx, vx) * mask[i].astype(f32)).astype(bf)
                da_t = (dot_nt(vx, dx) * maskt[i].astype(f32)).astype(bf)
                gqf = dot(da, kk)
                gkf = dot(da_t, qq)
                gv = dot(a_t, dx)
                if i < 3:
                    ds = dst[h].astype(bf)
                    gkf = gkf + dot_nt(vx, ds) * km
                    gv = gv + dot(kk, ds) * km
                if i > 0:
                    gqf = gqf + dot_nt(dx, st[2 * p + h, i - 1]) * qm
                    new = dot_tn((qq.astype(f32) * qm).astype(bf), dx)
                    dst[h] = new if i == 3 else new + same * dst[h]
                dq.append(gqf)
                dk.append(gkf)
                dv.append(gv)
            zq = soft_back(qf[2 * p, rs, :], qf[2 * p + 1, rs, :], dq[0], dq[1], m0, ones)
            zk = soft_back(kf[2 * p, rs, :], kf[2 * p + 1, rs, :], dk[0], dk[1], m0, ones)
            fq = fq + dot_tn(qkv[rs, ql], zq)
            fk = fk + dot_tn(qkv[rs, kl], zk)
            dproj[rs, ql] = dot_nt(zq, bq).astype(bf)
            dproj[rs, kl] = dot_nt(zk, bk).astype(bf)
            dproj[rs, vl] = jnp.where(m0, dv[0], dv[1]).astype(bf)
            pump(backward, p, i)
        top = lax.broadcasted_iota(jnp.int32, (128, 128), 0) < 64
        ml = low_lanes((128, 128))
        gf[pl.ds(at(own + p * 128), 128), :] = jnp.where(
            top, jnp.where(ml, fq, roll64(fk)), jnp.where(ml, roll64(fq), fk)
        ).astype(bf)
        trio = pl.ds(at(p * 384), 384)
        sums3 = jnp.sum(dproj[:, trio].astype(f32), axis=0, keepdims=True)
        base = at(p * 384 + 256 * jnp.minimum(p, 1))
        for m in range(4):
            ms = slice(m * 192, m * 192 + 192)
            t = dot(h1t[ms, :], dproj[:, trio])
            wt = w[ms, pl.ds(base, 384)].astype(f32)
            gain = w[ms, VAT : VAT + 128].astype(f32)
            gq[m, :, :, pl.ds(at(384 + p * 384), 384)] = (t * gain[:, 0:1] + sums3 * gain[:, 1:2]).astype(bf).reshape(4, 48, 384)
            gg = jnp.sum(wt * t, axis=1, keepdims=True)
            gs = jnp.sum(wt * sums3, axis=1, keepdims=True)
            vsrc[ms, :] += jnp.where(lane == 0, gg, jnp.where(lane == 1, gs, 0.0))
        for n in range(3):
            vg[4 + n : 5 + n, pl.ds(at(own + p * 128), 128)] = sums3[:, n * 128 : n * 128 + 128]
        pump(backward, p, -1)

    for m in range(4):
        gq[m, :, :, 1536:1664] = gf[m * 192 : m * 192 + 192, :].reshape(4, 48, 128)
    d_mid(1)
    d_start(2)
    for k in range(2):
        vg[pl.ds(8 + 2 * c + k, 1), :] = gb[0:1, k * 768 : k * 768 + 768]
    vsrc[...] += jnp.transpose(jnp.concatenate([vg[...], jnp.zeros((112, 768), f32)], axis=0))

    def vx_(a, e):
        t = lax.rem((x, z)[a] + e, 4)
        n = (192, 48)[a]
        src = vsrc.at[pl.ds(at(t * 192 if a == 0 else x * 192 + t * 48, 16), n)]
        return rcopy(src, (v1, v2)[a].at[e - 1], ss.at[8], vxr.at[a], axis_peer(a, e))

    for e in (2, 1, 3):
        vx_(0, e).start()

    def dh1_rows(r0):
        rs = pl.ds(at(r0), 256)
        for n in range(3):
            ns = slice(n * 256, n * 256 + 256)
            t = dot_nt(dproj[rs, 0:384], w[ns, 0:384]) + dot_nt(dproj[rs, 384:1152], w[ns, 640:1408])
            dh1p[rs, ns] = t.astype(bf)

    def dh1_ex(i):
        return ex(8 + i, dh1p.at[pl.ds(at(away + i * 256), 256)], dh1o.at[i * 256 : i * 256 + 256])

    def input_rows(i):
        dh1_ex(i).wait_recv()
        rs = pl.ds(at(half + i * 256), 256)
        cen, r = norm_stats(xr[rs, :].astype(f32))
        xh = cen * r
        dh = dh1p[rs, :].astype(f32) + dh1o[i * 256 : i * 256 + 256, :].astype(f32)
        dx = dh * vec[0:1, :]
        dx = r * (dx - jnp.mean(dx, -1, keepdims=True) - xh * jnp.mean(dx * xh, -1, keepdims=True))
        dh1p[rs, :] = (dx + x2[rs, :]).astype(bf)
        tok_start(1, i)

    dh1_rows(away)
    dh1_ex(0).start()
    dh1_rows(half)
    dh1_rows(away + 256)
    dh1_ex(1).start()
    take(v1, vxr.at[0])
    mid = pl.ds(at(x * 192, 16), 192)
    vsrc[mid, :] = vsrc[mid, :] + (v1[0] + v1[1] + v1[2])
    for e in (2, 1, 3):
        vx_(1, e).start()
    d_end(1)
    y_start(1)
    d_mid(2)
    input_rows(0)
    dh1_rows(half + 256)
    take(v2, vxr.at[1])
    d_end(2)
    y_start(2)
    input_rows(1)

    def sums(gp):
        take(yr.at[0:7, :, YCOLS[gp][0] : YCOLS[gp][1]], ysr.at[gp])
        tot = jnp.zeros((1, 1), f32)
        for d, wd, sr, sp in GPIECES:
            if not YCOLS[gp][0] <= d < YCOLS[gp][1]:
                continue
            for cc in range(2 if sp else 1):
                srcs = [2 * j + cc for j in range(4)] if sp else range(8)
                v = sum(yr[j, 0:6, d : d + wd].astype(f32) for j in srcs)
                pg_o[:, sr + sp * cc : sr + sp * cc + wd] = v
                tot = tot + jnp.sum(jnp.sum(v * v, axis=1, keepdims=True), axis=0, keepdims=True)
        return tot

    total = sums(0) + sums(1)
    total = total + sums(2)
    V = sum(yr[j, :, 1664:1792].astype(f32) for j in range(8))
    vs_o[...] = V[0:6, 0:13]
    total = total + jnp.sum(jnp.sum(V[0:6] * V[0:6], axis=1, keepdims=True), axis=0, keepdims=True)
    n2[pln] = jnp.broadcast_to(total, (8, 128))

    def nc2(k):
        return rcopy(n2.at[pln], n2.at[pln], ss.at[10], n2r.at[0], plane_peer(k))

    def nc1(k):
        return rcopy(n1.at[s], n1.at[s], ss.at[9], n1r.at[0], seq_peer(k)[1])

    for k in range(1, 16):
        nc2(k).start()
    take(n2.at[0:15], n2r.at[0])
    n1[s] = sum(n2[j] for j in range(16))
    for k in range(1, 8):
        nc1(k).start()
    sent(rcv.at[0:7], 0)
    sent(sg.at[0:7], 1)
    sent(xr.at[0:768], 2)
    sent(xr, 3)
    sent(w.at[0:720], 4)
    sent(g.at[0:720], 5)
    sent(w.at[0:720, 0:GC], 6)
    sent(rcv.at[0:7], 7)
    sent(vsrc.at[0:720], 8)
    sent(n2.at[0:15], 10)
    for wh in range(2):
        tok_wait(wh)
    ex(0, w.at[:, WOAT : WOAT + 384], wo.at[:, mine]).wait_send()
    for p in range(3):
        ex(1 + p, att_part(p), att_part(p)).wait_send()
    ex(4, outp.at[pl.ds(away, 512)], outo).wait_send()
    for i in range(2):
        dh1_ex(i).wait_send()
    take(n1.at[0:7], n1r.at[0])
    norm_o[...] = jnp.sqrt(sum(n1[j] for j in range(8)))[0:1, 0:1]
    sent(n1.at[0:7], 9)


def run_layer(par, vt, xin, dyin, sgin):
    V = pl.BlockSpec(memory_space=pltpu.VMEM)
    H = pl.BlockSpec(memory_space=pl.ANY)
    M = pltpu.VMEM
    DM = pltpu.SemaphoreType.DMA
    S = jax.ShapeDtypeStruct
    tok = (T, D)
    return pl.pallas_call(
        layer,
        out_shape=[S((4, 128, D), bf), S((4, 128, D), bf), S((6, 9344), f32), S((6, 13), f32), S((1, 1), f32)],
        in_specs=[V, V, H, H, V],
        out_specs=[H, H, V, V, V],
        scratch_shapes=[
            M((D, WC), bf), M((D, D), bf), M(tok, bf), M(tok, bf), M((8, 8, 128), f32), M((4, 8, 128), f32), M((2, 8, WC), bf), M((8, 8, WC), bf),
            M((16, D), f32), M(tok, bf), M((D, T), bf), M((T, 3 * HD), bf), M((6, T, 128), bf), M((6, T, 128), bf),
            M((T, HD), f32), M((6, 3, 128, 128), bf), M((T, 128), f32), M((4, 256, 256), bf), M((4, 256, 256), bf), M(tok, bf),
            M(tok, f32), M(tok, bf), M((D, T), bf), M((D, T), bf), M((T, FH), bf), M((T, FH), bf), M((512, D), bf),
            M(tok, bf), M((512, D), bf), M((D, 2 * FH), bf), M((576, 2 * FH), bf), M((144, 2 * FH), bf),
            M((4, 4, 48, GC), bf), M((3, 4, 48, GC), bf), M((3, 48, GC), bf), M((D, 128), bf),
            M((8, 8, WC), bf), M((8, 8, 128), f32), M((16, 8, 128), f32), M((16, D), f32), M((8, FH), f32),
            M((D, 128), f32), M((3, 192, 128), f32), M((3, 48, 128), f32),
            DM((11,)), DM((3,)), DM((1,)), DM((2,)), DM((2,)), DM((4, 10)), DM((2, 4, 2)), DM((2, 2)), DM((3,)), DM((3,)), DM((3,)), DM((2,)),
            DM((1,)), DM((1,)), DM((11,)), DM((11,)), DM((2, 8)), DM((2, 8)), DM((4,)),
        ],
        compiler_params=pltpu.CompilerParams(collective_id=0, has_side_effects=True, vmem_limit_bytes=64 * 2**20 - 2**17),
        name="layer",
    )(par, vt, xin, dyin, sgin)


def adamw(weight, grad, m, v, scale, rate, decay):
    grad = grad * scale
    m = 0.5 * m + 0.5 * grad
    v = 0.5 * v + 0.5 * grad * grad
    return grad, weight - rate * (m / (jnp.sqrt(v) + 1e-8) + decay * weight), m, v


def finish(out, ig, pg, norm, par, pm, pv, out_o, ig_o, *p_o):
    out_o[...] = out[...]
    ig_o[...] = ig[...].astype(f32)

    @pl.when(pl.program_id(0) == 0)
    def _():
        scale = 1.0 / jnp.maximum(norm[...], 1.0)
        for a in range(0, 9344, 1024):
            e = slice(a, min(a + 1024, 9344))
            for ref, val in zip(p_o, adamw(par[:, e], pg[:, e], pm[:, e], pv[:, e], scale, 0.05, 0.1)):
                ref[:, e] = val


def run_finish(out, ig, pg, norm, par, pm, pv):
    S = jax.ShapeDtypeStruct
    tok = pl.BlockSpec((2, 128, D), lambda i: (i, 0, 0))
    mat = pl.BlockSpec((6, 9344), lambda i: (0, 0))
    one = pl.BlockSpec((1, 1), lambda i: (0, 0))
    return pl.pallas_call(
        finish,
        grid=(2,),
        out_shape=[S((4, 128, D), bf), S((4, 128, D), f32)] + [S((6, 9344), f32)] * 4,
        in_specs=[tok, tok, mat, one, mat, mat, mat],
        out_specs=[tok, tok] + [mat] * 4,
        compiler_params=pltpu.CompilerParams(vmem_limit_bytes=62 * 2**20),
        name="finish",
    )(out, ig, pg, norm, par, pm, pv)


def body(inputs, segment_ids, out_grad, params, vectors, params_m, params_v, vectors_m, vectors_v):
    out, ig, pg, vs, norm = run_layer(params, vectors.T, inputs, out_grad, segment_ids)
    scale = 1.0 / jnp.maximum(norm[0, 0], 1.0)
    q = adamw(vectors.T, vs, vectors_m.T, vectors_v.T, scale, 0.2, 0.0)
    done = run_finish(out, ig, pg, norm, params, params_m, params_v)
    return (done[0], done[1], norm.reshape(1)) + tuple(done[2:]) + tuple(t.T for t in q)


def solution(mesh):
    torus = Mesh(mesh.devices.reshape(4, 4, 4, 2), ("x", "z", "y", "c"))
    row, seq, every = ("x", "z"), ("y", "c"), ("x", "z", "y", "c")
    tok, mat, vec = P(row, seq, None), P(every, None), P(None, every)
    return jax.shard_map(
        body,
        mesh=torus,
        in_specs=(tok, P(row, seq), tok, mat, vec, mat, mat, vec, vec),
        out_specs=(tok, tok, P(), mat, mat, mat, mat, vec, vec, vec, vec),
        check_vma=False,
    )
```

```python
import jax
import jax.numpy as jnp
from jax import lax
from jax.experimental import pallas as pl
from jax.experimental.pallas import tpu as pltpu
from jax.sharding import Mesh
from jax.sharding import PartitionSpec as P

f32 = jnp.float32
bf = jnp.bfloat16
MESH = pl.DeviceIdType.MESH
T, D, HD, FH = 1024, 768, 384, 1536
WC = 4864
GC = 1664
PIECES = (
    (0, 128, 0, 384), (128, 128, 768, 384), (256, 128, 1536, 384), (384, 128, 3072, 0),
    (640, 128, 128, 384), (768, 128, 896, 384), (896, 128, 1664, 384),
    (1024, 128, 256, 384), (1152, 128, 1024, 384), (1280, 128, 1792, 384), (1408, 384, 2304, 384),
    (1792, 768, 3200, 1536), (2560, 768, 6272, 1536), (3328, 768, 3968, 1536), (4096, 768, 7040, 1536),
)
VAT = 512
WOAT = 1408
FAT = 384
STAGE = ((0, 640), (640, 1792), (1792, 4864))
GATHER = ((0, 256, 640), (640, 1152, 1792), (1792, 2560, 3328), (3328, 4096, 4864))
GPIECES = (
    (0, 384, 2304, 384), (384, 128, 0, 384), (512, 128, 768, 384), (640, 128, 1536, 384),
    (768, 128, 128, 384), (896, 128, 896, 384), (1024, 128, 1664, 384),
    (1152, 128, 256, 384), (1280, 128, 1024, 384), (1408, 128, 1792, 384), (1536, 128, 3072, 0),
    (1792, 768, 3200, 1536), (2560, 768, 6272, 1536), (3328, 768, 3968, 1536), (4096, 768, 7040, 1536),
)
REDUCE = ((1792, 2560, 3328), (3328, 4096, 4864))
DIRECT = (((0, 384), (384, 768)), ((768, 896), (896, 1152)), ((1152, 1408), (1408, 1664)))
YCOLS = ((1792, 4864), (0, 1152), (1152, 1792))
FAR = (0, -1, 1, 2)
BIG = 3.0e38


def dot(a, b):
    return lax.dot_general(a, b, (((1,), (0,)), ((), ())), preferred_element_type=f32)


def dot_nt(a, b):
    return lax.dot_general(a, b, (((1,), (1,)), ((), ())), preferred_element_type=f32)


def dot_tn(a, b):
    return lax.dot_general(a, b, (((0,), (0,)), ((), ())), preferred_element_type=f32)


def at(v, m=128):
    return pl.multiple_of(v, m)


def rows(i, n=256):
    return pl.ds(at(i * n), n)


def low_lanes(shape):
    return lax.broadcasted_iota(jnp.int32, shape, len(shape) - 1) < 64


def roll64(v):
    return pltpu.roll(v, 64, 1)


def slab(xx, zz):
    return at((lax.rem(xx + 8, 4) * 4 + lax.rem(zz + 8, 4)) * 48, 16)


def norm_stats(v):
    mu = jnp.mean(v, axis=-1, keepdims=True)
    cen = v - mu
    return cen, lax.rsqrt(jnp.mean(cen * cen, axis=-1, keepdims=True) + 1e-5)


def seg_ones():
    a = lax.broadcasted_iota(jnp.int32, (128, 128), 0) < 64
    return (a == low_lanes((128, 128))).astype(bf)


def feats(z, m0, ones):
    mx = jnp.where(m0, jnp.max(jnp.where(m0, z, -BIG), -1, keepdims=True), jnp.max(jnp.where(m0, -BIG, z), -1, keepdims=True))
    mn = jnp.where(m0, jnp.min(jnp.where(m0, z, BIG), -1, keepdims=True), jnp.min(jnp.where(m0, BIG, z), -1, keepdims=True))
    ep = jnp.exp(z - mx).astype(bf)
    en = jnp.exp(mn - z).astype(bf)
    fp = ep.astype(f32) / dot(ep, ones)
    fn = roll64(en.astype(f32) / dot(en, ones))
    return jnp.where(m0, fp, fn).astype(bf), jnp.where(m0, fn, fp).astype(bf)


def soft_back(fe, fo, de, do, m0, ones):
    fe = fe.astype(f32)
    fo = fo.astype(f32)
    fp = jnp.where(m0, fe, fo)
    fr = jnp.where(m0, fo, fe)
    tp = fp * jnp.where(m0, de, do)
    tr = fr * jnp.where(m0, do, de)

    def total(t):
        hi = t.astype(bf)
        return dot(hi, ones) + dot((t - hi.astype(f32)).astype(bf), ones)

    return ((tp - fp * total(tp)) - roll64(tr - fr * total(tr))).astype(bf)


def same_doc(segc, i):
    sc = segc[i * 256 : i * 256 + 256, :]
    last = segc[i * 256 + 255 : i * 256 + 256, :]
    km = (sc == last).astype(f32)
    if i == 0:
        return None, km, None
    prev = segc[i * 256 - 1 : i * 256, :]
    return (sc == prev).astype(f32), km, (last == prev).astype(f32)


def layer(
    par, vt, xin, dyin, sgin,
    out_o, ig_o, pg_o, vs_o, norm_o,
    w, wo, xr, dyr, sg, sgb, wire, rcv, vec, h1, h1t, qkv, qf, kf, invd, st, segc, mask, maskt, attf,
    x2, h2, h2t, dyt, act, du, outo, dh2o, dh1o, g, r1, r2, gq, d1, d2, gf, yr, n1, n2, vg, gb, vsrc, v1, v2,
    ss, s0r, sgr, rsr, sbr, agr, t1r, t2r, d1r, d2r, ysr, vxr, n1r, n2r, exs, exr, tks, tkr, los,
):
    x, z, y, c = (lax.axis_index(a) for a in ("x", "z", "y", "c"))
    s = y * 2 + c
    pln = x * 4 + z
    own = at(c * 384)

    def rcopy(src, dst, ss, rs, dev):
        return pltpu.make_async_remote_copy(src, dst, ss, rs, device_id=dev, device_id_type=MESH)

    def take(ref, sem):
        rcopy(ref, ref, sem, sem, other).wait_recv()

    def sent(ref, i):
        rcopy(ref, ref, ss.at[i], ss.at[i], other).wait_send()

    def seq_peer(k):
        t = lax.rem(s + k + 8, 8)
        return t, {"y": t // 2, "c": lax.rem(t, 2)}

    def axis_peer(a, k):
        return {("x", "z")[a]: lax.rem((x, z)[a] + k + 4, 4)}

    def plane_peer(k):
        t = lax.rem(pln + k, 16)
        return {"x": t // 4, "z": lax.rem(t, 4)}

    other = {"c": 1 - c}

    bar = pltpu.get_barrier_semaphore()
    for k in range(1, 8):
        pl.semaphore_signal(bar, inc=1, device_id=seq_peer(k)[1], device_id_type=MESH)
    for k in range(1, 16):
        pl.semaphore_signal(bar, inc=1, device_id=plane_peer(k), device_id_type=MESH)
    for cc in range(2):
        wire[cc, :, :] = jnp.zeros((8, WC), bf)
        for d, wd, sr, sp in PIECES:
            wire[cc, 0:6, d : d + wd] = par[:, sr + sp * cc : sr + sp * cc + wd].astype(bf)
        wire[cc, 0:6, VAT : VAT + 13] = vt[...].astype(bf)
    for j in range(4):
        sgb[j] = jnp.broadcast_to(sgin[j : j + 1, :].astype(f32), (8, 128))
    pl.semaphore_wait(bar, 22)

    def st0(gp, k):
        t, dev = seq_peer(k)
        a, b = STAGE[gp]
        return rcopy(wire.at[dev["c"], :, a:b], rcv.at[s, :, a:b], ss.at[0], s0r.at[gp], dev)

    def sgc(k):
        t, dev = seq_peer(k)
        return rcopy(sgb.at[t // 2], sg.at[s], ss.at[1], sgr.at[0], dev)

    pairs = ((xin, xr), (dyin, dyr))

    def res(wh, k):
        src, dst = pairs[wh]
        j = lax.rem(y + k, 4)
        return rcopy(src.at[j], dst.at[rows(s, 128)], ss.at[2], rsr.at[wh], {"y": j})

    def keep(wh):
        src, dst = pairs[wh]
        return pltpu.make_async_copy(src.at[y], dst.at[rows(s, 128)], los.at[wh])

    def sib(wh, k):
        ref = pairs[wh][1].at[rows(lax.rem(y - k + 4, 4) * 2 + c, 128)]
        return rcopy(ref, ref, ss.at[3], sbr.at[wh], other)

    def res_start(wh):
        keep(wh).start()
        for k in (2, 1, 3):
            res(wh, k).start()

    def res_pass(wh):
        keep(wh).wait()
        sib(wh, 0).start()
        take(pairs[wh][1].at[0:384], rsr.at[wh])
        for k in range(1, 4):
            sib(wh, k).start()

    def res_end(wh):
        take(pairs[wh][1].at[0:512], sbr.at[wh])

    def pos(p, d1, d2):
        return slab(x + d1, z + d2) if p == 0 else slab(x + d2, z + d1)

    def along(p, phase, way):
        return axis_peer((p + phase) % 2, way)

    def ag(gp, p, sem, d1, d2, phase, way):
        ref = w.at[pl.ds(pos(p, d1, d2), 48), GATHER[gp][p] : GATHER[gp][p + 1]]
        return rcopy(ref, ref, ss.at[4], agr.at[gp, sem], along(p, phase, way))

    def ag_take(gp, sem):
        take(w.at[0 : (96, 48)[sem % 2], GATHER[gp][0] : GATHER[gp][2]], agr.at[gp, sem])

    def p2send(gp, q):
        for p in range(2):
            ag(gp, p, 2 + 2 * q, FAR[q], 0, 1, 1).start()
            ag(gp, p, 2 + 2 * q, FAR[q], 0, 1, -1).start()

    def ag_d(gp, q):
        ag_take(gp, 2 + 2 * q)
        way = (1, -1, -1, 1)[q]
        for p in range(2):
            ag(gp, p, 3 + 2 * q, FAR[q], -way, 1, way).start()

    def ag_a(gp):
        for p in range(2):
            ag(gp, p, 0, 0, 0, 0, 1).start()
            ag(gp, p, 0, 0, 0, 0, -1).start()
        p2send(gp, 0)

    def ag_b(gp):
        ag_take(gp, 0)
        ag(gp, 0, 1, -1, 0, 0, 1).start()
        ag(gp, 1, 1, 1, 0, 0, -1).start()
        p2send(gp, 1)
        p2send(gp, 2)

    def ag_c(gp):
        ag_take(gp, 1)
        p2send(gp, 3)
        ag_d(gp, 0)

    def ag_e(gp):
        for q in range(4):
            ag_take(gp, 3 + 2 * q)

    rr = lax.broadcasted_iota(jnp.int32, (48, 64), 0)
    rc = lax.broadcasted_iota(jnp.int32, (48, 64), 1)
    spread = ((lax.rem(rr, 6) == lax.rem(rc, 8)) & (rr // 6 == rc // 8)).astype(bf)

    def assemble(gp):
        a, b = STAGE[gp]
        take(rcv.at[0:7, :, a:b], s0r.at[gp])
        n = (640, 1152, 768)[gp]
        for lo in range(a, b, n):
            raw = jnp.concatenate([rcv[t, :, lo : lo + n].astype(f32) for t in range(8)], axis=0).astype(bf)
            w[pl.ds(slab(x, z), 48), lo : lo + n] = dot(spread, raw).astype(bf)

    for k in range(1, 8):
        st0(0, k).start()
    for k in range(1, 8):
        st0(1, k).start()
    for k in range(1, 8):
        sgc(k).start()
    res_start(0)
    for k in range(1, 8):
        st0(2, k).start()
    sg[s] = sgb[y]
    rcv[s] = wire[c]
    assemble(0)
    ag_a(0)
    assemble(1)
    ag_a(1)
    ag_b(0)
    take(sg.at[0:7], sgr.at[0])
    for b in range(8):
        segc[b * 128 : b * 128 + 128, :] = jnp.transpose(jnp.broadcast_to(sg[b, 0:1, :], (128, 128)))
    mr = lax.broadcasted_iota(jnp.int32, (256, 256), 0)
    mc = lax.broadcasted_iota(jnp.int32, (256, 256), 1)
    for i in range(4):
        row = jnp.concatenate([sg[2 * i, 0:1, :], sg[2 * i + 1, 0:1, :]], axis=1)
        col = segc[i * 256 : i * 256 + 256, :]
        eq = jnp.concatenate([col, col], axis=1) == row
        mask[i] = jnp.where(eq & (mc <= mr), 1.0, 0.0).astype(bf)
        maskt[i] = jnp.where(eq & (mr <= mc), 1.0, 0.0).astype(bf)
    ag_c(0)
    for q in (1, 2):
        ag_d(0, q)
    res_pass(0)
    ag_b(1)
    ag_d(0, 3)
    res_end(0)
    res_start(1)

    @pl.loop(0, 4, unroll=2)
    def _(i):
        cen, r = norm_stats(xr[rows(i), :].astype(f32))
        x2[rows(i), :] = cen * r

    ag_c(1)
    assemble(2)
    ag_a(2)
    ag_e(0)

    def ex(i, src, dst):
        return rcopy(src, dst, exs.at[i], exr.at[i], other)

    mine = pl.ds(own, 384)

    vec[...] = jnp.transpose(w[:, VAT : VAT + 128].astype(f32))[0:16]

    @pl.loop(0, 4, unroll=2)
    def _(i):
        h = (x2[rows(i), :] * vec[0:1, :] + vec[1:2, :]).astype(bf)
        h1[rows(i), :] = h
        h1t[:, rows(i)] = jnp.transpose(x2[rows(i), :].astype(bf))

    ones = seg_ones()
    m0 = low_lanes((256, 128))

    def feature_maps(p):
        F = w[pl.ds(at(own + p * 128), 128), FAT : FAT + 128].astype(f32)
        R = roll64(F)
        top = lax.broadcasted_iota(jnp.int32, (128, 128), 0) < 64
        ml = low_lanes((128, 128))
        zz = jnp.zeros_like(F)
        bq = jnp.where(top & ml, F, jnp.where(top | ml, zz, R))
        bk = jnp.where(top & ml, R, jnp.where(top | ml, zz, F))
        return bq.astype(bf), bk.astype(bf)

    def pump(table, p, i):
        for (pp, ii), todo in table.items():
            if ii == i:

                @pl.when(p == pp)
                def _():
                    for t in todo:
                        t[0](*t[1:])

    def wo_start():
        ex(0, w.at[:, WOAT : WOAT + 384], wo.at[:, mine]).start()
        wo[:, mine] = w[:, WOAT : WOAT + 384]

    forward = {
        (0, 0): ((ag_d, 1, 1), (ag_d, 1, 2)),
        (0, 1): ((ag_d, 1, 3), (ag_b, 2)),
        (0, 2): ((ag_a, 3),),
        (0, 3): ((ag_e, 1), (wo_start,)),
        (1, 0): ((ag_c, 2),),
        (1, 1): ((res_pass, 1),),
        (1, 2): ((ag_d, 2, 1), (ag_d, 2, 2)),
        (1, 3): ((ag_b, 3),),
        (2, 0): ((ag_d, 2, 3),),
        (2, 2): ((ag_c, 3),),
    }

    def att_part(p):
        return attf.at[:, pl.ds(at(own + p * 128), 128)]

    @pl.loop(0, 3)
    def _(p):
        lanes = pl.ds(at(p * 128), 128)
        bq, bk = feature_maps(p)
        base = at(p * 384 + 256 * jnp.minimum(p, 1))
        part = pl.ds(at(own + p * 128), 128)
        bias = jnp.concatenate([vec[4:5, part], vec[5:6, part], vec[6:7, part]], axis=1)
        state = [None, None]
        for i in range(4):
            rs = slice(i * 256, i * 256 + 256)
            pr = (dot(h1[rs, :], w[:, pl.ds(base, 384)]) + bias).astype(bf)
            qkv[rs, pl.ds(at(p * 384), 384)] = pr
            qe, qo = feats(dot(pr[:, 0:128], bq), m0, ones)
            ke, ko = feats(dot(pr[:, 128:256], bk), m0, ones)
            v = pr[:, 256:384]
            qm, km, same = same_doc(segc, i)
            outs = []
            for h, (qq, kk) in enumerate(((qe, ke), (qo, ko))):
                vx = jnp.where(m0 == (h == 0), v, jnp.ones_like(v))
                qf[2 * p + h, rs, :] = qq
                kf[2 * p + h, rs, :] = kk
                o = dot((dot_nt(qq, kk) * mask[i].astype(f32)).astype(bf), vx)
                if i > 0:
                    sb = state[h].astype(bf)
                    st[2 * p + h, i - 1] = sb
                    o = o + dot(qq, sb) * qm
                if i < 3:
                    sn = dot_tn((kk.astype(f32) * km).astype(bf), vx)
                    state[h] = sn if i == 0 else sn + same * state[h]
                outs.append(o)
            num = jnp.where(m0, outs[0], outs[1])
            inv = 1.0 / roll64(jnp.where(m0, outs[1], outs[0]))
            invd[rs, lanes] = inv
            attf[rs, part] = (num * inv).astype(bf)
            if i == 3:
                ex(1 + p, att_part(p), att_part(p)).start()
            pump(forward, p, i)

    res_end(1)
    ex(0, w.at[:, WOAT : WOAT + 384], wo.at[:, pl.ds(at((1 - c) * 384), 384)]).wait_recv()
    for p in range(3):
        part = attf.at[:, pl.ds(at((1 - c) * 384 + p * 128), 128)]
        ex(1 + p, part, part).wait_recv()

    @pl.loop(0, 4, unroll=2)
    def _(i):
        v = xr[rows(i), :].astype(f32) + dot(attf[rows(i), :], wo[...]) + vec[7:8, :]
        x2[rows(i), :] = v
        cen, r = norm_stats(v)
        h = (cen * r * vec[2:3, :] + vec[3:4, :]).astype(bf)
        h2[rows(i), :] = h
        h2t[:, rows(i)] = jnp.transpose(h)
        dyt[:, rows(i)] = jnp.transpose(dyr[rows(i), :])

    k0 = 0.7978845608028654
    k1 = 0.044715

    def mlp(j):
        far = at(1792 + (j // 3) * 768 + j * 256)
        cu = pl.ds(far, 256)
        cd = pl.ds(at(far + 768), 256)
        gu = pl.ds(at(far - 1792), 256)
        gd = pl.ds(at(far - 1024), 256)
        cj = pl.ds(at(j * 256), 256)
        off = c * FH + j * 256
        bu = vec[pl.ds(8 + off // D, 1), pl.ds(at(lax.rem(off, D)), 256)]

        @pl.loop(0, 4, unroll=4)
        def _(i):
            u = dot(h2[rows(i), :], w[:, cu]) + bu
            u2 = u * u
            t = jnp.tanh(k0 * (u + k1 * u2 * u))
            act[rows(i), cj] = (0.5 * u * (1.0 + t)).astype(bf)
            da = dot(dyr[rows(i), :], w[:, cd])
            gp = 0.5 * (1.0 + t) + 0.5 * u * (1.0 - t * t) * (k0 * (1.0 + (3 * k1) * u2))
            d = (gp * da).astype(bf)
            du[rows(i), cj] = d
            gb[0:1, cj] = gb[0:1, cj] + jnp.sum(d.astype(f32), axis=0, keepdims=True)

        for m in range(3):
            ms = slice(m * 256, m * 256 + 256)
            g[ms, gd] = dot(dyt[ms, :], act[:, cj]).astype(bf)
            g[ms, gu] = dot(h2t[ms, :], du[:, cj]).astype(bf)

    def gref(gp, p, d1, d2):
        return g.at[pl.ds(pos(p, d1, d2), 48), REDUCE[gp][p] - 1792 : REDUCE[gp][p + 1] - 1792]

    def land(gp, p, slot):
        r = slice(slot % 12 * 48, slot % 12 * 48 + 48)
        return (r1 if slot < 12 else r2).at[r, REDUCE[gp][p] - 1792 : REDUCE[gp][p + 1] - 1792]

    def tree_take(n, sem):
        take(r1.at[0:n, 0:1536], sem)

    def c1(gp, p, q, kind):
        way = (1, -1, -1, 1)[q]
        e = (2, way, -way)[kind]
        return rcopy(gref(gp, p, FAR[q], e), land(gp, p, q * 3 + kind), ss.at[5], t1r.at[gp, q, (kind + 1) // 2], along(p, 1, -way if kind == 2 else way))

    def c2(gp, p, kind):
        way = (1, -1)[p]
        e = (2, way, -way)[kind]
        return rcopy(gref(gp, p, e, 0), land(gp, p, 12 + kind), ss.at[5], t2r.at[gp, (kind + 1) // 2], along(p, 0, -way if kind == 2 else way))

    def acc(dst, *srcs):
        if len(srcs) == 1:
            dst[...] = dst[...] + srcs[0][...]
            return
        t = dst[...].astype(f32)
        for r in srcs:
            t = t + r[...].astype(f32)
        dst[...] = t.astype(bf)

    def r1_start(gp):
        for q in (3, 1, 2, 0):
            for p in range(2):
                c1(gp, p, q, 0).start()
                c1(gp, p, q, 2).start()

    def r1_mid(gp, q):
        tree_take(48, t1r.at[gp, q, 0])
        for p in range(2):
            acc(gref(gp, p, FAR[q], (1, -1, -1, 1)[q]), land(gp, p, q * 3))
            c1(gp, p, q, 1).start()

    def r1_end(gp, q):
        tree_take(96, t1r.at[gp, q, 1])
        for p in range(2):
            acc(gref(gp, p, FAR[q], 0), land(gp, p, q * 3 + 1), land(gp, p, q * 3 + 2))

    def r2_start(gp):
        for q in (3, 1, 2):
            r1_end(gp, q)
        for p in range(2):
            c2(gp, p, 0).start()
            c2(gp, p, 2).start()

    def r2_mid(gp):
        tree_take(48, t2r.at[gp, 0])
        for p in range(2):
            acc(gref(gp, p, (1, -1)[p], 0), land(gp, p, 12))
            c2(gp, p, 1).start()

    def r2_end(gp):
        tree_take(96, t2r.at[gp, 1])
        for p in range(2):
            acc(gref(gp, p, 0, 0), land(gp, p, 13), land(gp, p, 14))

    tr = lax.broadcasted_iota(jnp.int32, (64, 48), 0)
    tc = lax.broadcasted_iota(jnp.int32, (64, 48), 1)
    split = ((lax.rem(tc, 6) == lax.rem(tr, 8)) & (tc // 6 == tr // 8)).astype(bf)

    def dcp(gp, p, phase, e):
        a, b = DIRECT[gp][p]
        first = p == 0
        if phase == 0:
            t = lax.rem((z if first else x) + e, 4)
            src = gq.at[:, t, :, a:b] if first else gq.at[t, :, :, a:b]
            return rcopy(src, d1.at[e - 1, :, :, a:b], ss.at[6], d1r.at[gp], axis_peer(1 if first else 0, e))
        t = lax.rem((x if first else z) + e, 4)
        src = gq.at[t, z, :, a:b] if first else gq.at[x, t, :, a:b]
        return rcopy(src, d2.at[e - 1, :, a:b], ss.at[6], d2r.at[gp], axis_peer(0 if first else 1, e))

    def d_start(gp):
        for e in (2, 1, 3):
            for p in range(2):
                dcp(gp, p, 0, e).start()

    def d_mid(gp):
        take(d1.at[:, :, :, DIRECT[gp][0][0] : DIRECT[gp][1][1]], d1r.at[gp])
        for p in range(2):
            a, b = DIRECT[gp][p]
            for k in range(4):
                dst = gq.at[k, z, :, a:b] if p == 0 else gq.at[x, k, :, a:b]
                acc(dst, *[d1.at[e, k, :, a:b] for e in range(3)])
            for e in (2, 1, 3):
                dcp(gp, p, 1, e).start()

    def d_end(gp):
        take(d2.at[:, :, DIRECT[gp][0][0] : DIRECT[gp][1][1]], d2r.at[gp])
        for p in range(2):
            a, b = DIRECT[gp][p]
            acc(gq.at[x, z, :, a:b], *[d2.at[e, :, a:b] for e in range(3)])

    def ycp(gp, k):
        t, dev = seq_peer(k)
        a, b = YCOLS[gp]
        return rcopy(rcv.at[t, :, a:b], yr.at[s, :, a:b], ss.at[7], ysr.at[gp], dev)

    def deal(a, b, part):
        out = dot(split, part).astype(bf)
        for t in range(8):
            rcv[t, :, a:b] = out[8 * t : 8 * t + 8]

    def y_start(gp):
        a, b = YCOLS[gp]
        if gp == 0:
            for lo in range(0, 3072, 768):
                deal(1792 + lo, 2560 + lo, g[pl.ds(slab(x, z), 48), lo : lo + 768])
        elif gp == 1:
            deal(0, 1152, gq[x, z, :, 0:1152])
        else:
            deal(1152, 1664, gq[x, z, :, 1152:1664])
            deal(1664, 1792, (vsrc[pl.ds(slab(x, z), 48), :] + (v2[0] + v2[1] + v2[2])).astype(bf))
        for k in range(1, 8):
            ycp(gp, k).start()
        yr[s, :, a:b] = rcv[s, :, a:b]

    gb[...] = jnp.zeros_like(gb)
    for q in (1, 2, 3):
        ag_d(3, q)
    ag_e(2)
    pl.loop(0, 3)(mlp)
    r1_start(0)
    ag_e(3)
    pl.loop(3, 6)(mlp)
    for q in (3, 1, 2, 0):
        r1_mid(0, q)
    r1_start(1)

    outp, dh2p, dh1p = h2, h1, du.at[:, 0:768]
    half = at(c * 512)
    away = at((1 - c) * 512)

    @pl.loop(0, 4, unroll=2)
    def _(i):
        for n in range(3):
            ns = slice(n * 256, n * 256 + 256)
            outp[rows(i), ns] = (dot_nt(act[rows(i), 0:768], w[ns, 2560:3328]) + dot_nt(act[rows(i), 768:1536], w[ns, 4096:4864])).astype(bf)

    ex(4, outp.at[pl.ds(away, 512)], outo).start()
    r2_start(0)
    for n in range(3):
        ns = slice(n * 256, n * 256 + 256)

        @pl.loop(0, 4, unroll=2)
        def _(i):
            dh2p[rows(i), ns] = (dot_nt(du[rows(i), 0:768], w[ns, 1792:2560]) + dot_nt(du[rows(i), 768:1536], w[ns, 3328:4096])).astype(bf)

        ex(5 + n, dh2p.at[:, ns], dh2o.at[:, ns]).start()
    ex(4, outp.at[pl.ds(away, 512)], outo).wait_recv()

    @pl.loop(0, 2)
    def _(i):
        rs = pl.ds(at(half + i * 256), 256)
        outp[rs, :] = (x2[rs, :] + outp[rs, :].astype(f32) + outo[rows(i), :].astype(f32) + vec[12:13, :]).astype(bf)

    toks = ((outp, out_o), (dh1p, ig_o))

    def tok(wh, k, recv=False):
        src, dst = toks[wh]
        t, dev = seq_peer(k)
        row = (seq_peer(-k)[0] // 2) if recv else y
        return rcopy(src.at[pl.ds(at(half + lax.rem(t, 4) * 128), 128)], dst.at[row], tks.at[wh, k], tkr.at[wh, k], dev)

    def tok_keep(wh):
        src, dst = toks[wh]
        return pltpu.make_async_copy(src.at[pl.ds(at(half + lax.rem(s, 4) * 128), 128)], dst.at[y], los.at[2 + wh])

    def tok_start(wh, part=None):
        def now(t):
            return (t // 4 == c) if part is None else (t // 2 == 2 * c + part)

        for k in range(1, 8):

            @pl.when(now(seq_peer(k)[0]))
            def _():
                tok(wh, k).start()

        @pl.when(now(s))
        def _():
            tok_keep(wh).start()

    def tok_wait(wh):
        @pl.when(s // 4 == c)
        def _():
            tok_keep(wh).wait()

        for k in range(1, 8):

            @pl.when(lax.rem(seq_peer(-k)[0], 2) == s // 4)
            def _():
                tok(wh, k, True).wait_recv()

        for k in range(1, 8):

            @pl.when(seq_peer(k)[0] // 4 == c)
            def _():
                tok(wh, k).wait_send()

    tok_start(0)

    vg[...] = jnp.zeros_like(vg)
    one = (c == 0).astype(f32)
    attt = dyt

    @pl.loop(0, 4, unroll=2)
    def _(i):
        attt[:, rows(i)] = jnp.transpose(attf[rows(i), :])

    for n in range(3):
        ns = slice(n * 256, n * 256 + 256)
        ex(5 + n, dh2p.at[:, ns], dh2o.at[:, ns]).wait_recv()
        ex(5 + n, dh2p.at[:, ns], dh2o.at[:, ns]).wait_send()

    @pl.loop(0, 4, unroll=2)
    def _(i):
        cen, r = norm_stats(x2[rows(i), :])
        xh = cen * r
        dh = dh2p[rows(i), :].astype(f32) + dh2o[rows(i), :].astype(f32)
        dyv = dyr[rows(i), :].astype(f32)
        dx = dh * vec[2:3, :]
        dx = r * (dx - jnp.mean(dx, -1, keepdims=True) - xh * jnp.mean(dx * xh, -1, keepdims=True)) + dyv
        x2[rows(i), :] = dx
        do = dx.astype(bf)
        h1[rows(i), :] = do

        def sm(v):
            return jnp.sum(v, axis=0, keepdims=True) * one

        vg[2:3, :] += sm(dh * xh)
        vg[3:4, :] += sm(dh)
        vg[7:8, :] += sm(do.astype(f32))
        vg[12:13, :] += sm(dyv)
        invd[rows(i), :] = dot_nt(do, wo[mine, :]) * invd[rows(i), :]

    r2_mid(0)
    r1_end(0, 0)
    for q in (3, 1, 2, 0):
        r1_mid(1, q)
    for m in range(4):
        gq[m, :, :, 0:384] = dot(attt[m * 192 : m * 192 + 192, :], h1[:, mine]).astype(bf).reshape(4, 48, 384)
    gf[...] = jnp.zeros_like(gf)
    vsrc[...] = jnp.zeros_like(vsrc)
    lane = lax.broadcasted_iota(jnp.int32, (192, 128), 1)
    dproj = act

    backward = {
        (0, 3): ((r2_end, 0),),
        (0, 2): ((r2_start, 1),),
        (0, 0): ((r2_mid, 1), (r1_end, 1, 0)),
        (0, -1): ((d_start, 0),),
        (1, 3): ((r2_end, 1),),
        (1, 2): ((y_start, 0),),
        (1, -1): ((d_start, 1),),
        (2, 3): ((d_mid, 0),),
        (2, 1): ((d_end, 0),),
    }

    @pl.loop(0, 3)
    def _(p):
        lanes = pl.ds(at(p * 128), 128)
        ql = pl.ds(at(p * 384), 128)
        kl = pl.ds(at(p * 384 + 128), 128)
        vl = pl.ds(at(p * 384 + 256), 128)
        bq, bk = feature_maps(p)
        dst = [None, None]
        fq = jnp.zeros((128, 128), f32)
        fk = jnp.zeros((128, 128), f32)
        for i in (3, 2, 1, 0):
            rs = slice(i * 256, i * 256 + 256)
            dn = invd[rs, lanes]
            dd = roll64(-(dn * attf[rs, pl.ds(at(own + p * 128), 128)].astype(f32)))
            v = qkv[rs, vl]
            qm, km, same = same_doc(segc, i)
            dq, dk, dv = [], [], []
            for h in range(2):
                mh = m0 == (h == 0)
                vx = jnp.where(mh, v, jnp.ones_like(v))
                dx = jnp.where(mh, dn, dd).astype(bf)
                qq = qf[2 * p + h, rs, :]
                kk = kf[2 * p + h, rs, :]
                a_t = (dot_nt(kk, qq) * maskt[i].astype(f32)).astype(bf)
                da = (dot_nt(dx, vx) * mask[i].astype(f32)).astype(bf)
                da_t = (dot_nt(vx, dx) * maskt[i].astype(f32)).astype(bf)
                gqf = dot(da, kk)
                gkf = dot(da_t, qq)
                gv = dot(a_t, dx)
                if i < 3:
                    ds = dst[h].astype(bf)
                    gkf = gkf + dot_nt(vx, ds) * km
                    gv = gv + dot(kk, ds) * km
                if i > 0:
                    gqf = gqf + dot_nt(dx, st[2 * p + h, i - 1]) * qm
                    new = dot_tn((qq.astype(f32) * qm).astype(bf), dx)
                    dst[h] = new if i == 3 else new + same * dst[h]
                dq.append(gqf)
                dk.append(gkf)
                dv.append(gv)
            zq = soft_back(qf[2 * p, rs, :], qf[2 * p + 1, rs, :], dq[0], dq[1], m0, ones)
            zk = soft_back(kf[2 * p, rs, :], kf[2 * p + 1, rs, :], dk[0], dk[1], m0, ones)
            fq = fq + dot_tn(qkv[rs, ql], zq)
            fk = fk + dot_tn(qkv[rs, kl], zk)
            dproj[rs, ql] = dot_nt(zq, bq).astype(bf)
            dproj[rs, kl] = dot_nt(zk, bk).astype(bf)
            dproj[rs, vl] = jnp.where(m0, dv[0], dv[1]).astype(bf)
            pump(backward, p, i)
        top = lax.broadcasted_iota(jnp.int32, (128, 128), 0) < 64
        ml = low_lanes((128, 128))
        gf[pl.ds(at(own + p * 128), 128), :] = jnp.where(
            top, jnp.where(ml, fq, roll64(fk)), jnp.where(ml, roll64(fq), fk)
        ).astype(bf)
        trio = pl.ds(at(p * 384), 384)
        sums3 = jnp.sum(dproj[:, trio].astype(f32), axis=0, keepdims=True)
        base = at(p * 384 + 256 * jnp.minimum(p, 1))
        for m in range(4):
            ms = slice(m * 192, m * 192 + 192)
            t = dot(h1t[ms, :], dproj[:, trio])
            wt = w[ms, pl.ds(base, 384)].astype(f32)
            gain = w[ms, VAT : VAT + 128].astype(f32)
            gq[m, :, :, pl.ds(at(384 + p * 384), 384)] = (t * gain[:, 0:1] + sums3 * gain[:, 1:2]).astype(bf).reshape(4, 48, 384)
            gg = jnp.sum(wt * t, axis=1, keepdims=True)
            gs = jnp.sum(wt * sums3, axis=1, keepdims=True)
            vsrc[ms, :] += jnp.where(lane == 0, gg, jnp.where(lane == 1, gs, 0.0))
        for n in range(3):
            vg[4 + n : 5 + n, pl.ds(at(own + p * 128), 128)] = sums3[:, n * 128 : n * 128 + 128]
        pump(backward, p, -1)

    for m in range(4):
        gq[m, :, :, 1536:1664] = gf[m * 192 : m * 192 + 192, :].reshape(4, 48, 128)
    d_mid(1)
    d_start(2)
    for k in range(2):
        vg[pl.ds(8 + 2 * c + k, 1), :] = gb[0:1, k * 768 : k * 768 + 768]
    vsrc[...] += jnp.transpose(jnp.concatenate([vg[...], jnp.zeros((112, 768), f32)], axis=0))

    def vx_(a, e):
        t = lax.rem((x, z)[a] + e, 4)
        n = (192, 48)[a]
        src = vsrc.at[pl.ds(at(t * 192 if a == 0 else x * 192 + t * 48, 16), n)]
        return rcopy(src, (v1, v2)[a].at[e - 1], ss.at[8], vxr.at[a], axis_peer(a, e))

    for e in (2, 1, 3):
        vx_(0, e).start()

    def dh1_rows(r0):
        rs = pl.ds(at(r0), 256)
        for n in range(3):
            ns = slice(n * 256, n * 256 + 256)
            t = dot_nt(dproj[rs, 0:384], w[ns, 0:384]) + dot_nt(dproj[rs, 384:1152], w[ns, 640:1408])
            dh1p[rs, ns] = t.astype(bf)

    def dh1_ex(i):
        return ex(8 + i, dh1p.at[pl.ds(at(away + i * 256), 256)], dh1o.at[i * 256 : i * 256 + 256])

    def input_rows(i):
        dh1_ex(i).wait_recv()
        rs = pl.ds(at(half + i * 256), 256)
        cen, r = norm_stats(xr[rs, :].astype(f32))
        xh = cen * r
        dh = dh1p[rs, :].astype(f32) + dh1o[i * 256 : i * 256 + 256, :].astype(f32)
        dx = dh * vec[0:1, :]
        dx = r * (dx - jnp.mean(dx, -1, keepdims=True) - xh * jnp.mean(dx * xh, -1, keepdims=True))
        dh1p[rs, :] = (dx + x2[rs, :]).astype(bf)
        tok_start(1, i)

    dh1_rows(away)
    dh1_ex(0).start()
    dh1_rows(half)
    dh1_rows(away + 256)
    dh1_ex(1).start()
    take(v1, vxr.at[0])
    mid = pl.ds(at(x * 192, 16), 192)
    vsrc[mid, :] = vsrc[mid, :] + (v1[0] + v1[1] + v1[2])
    for e in (2, 1, 3):
        vx_(1, e).start()
    d_end(1)
    y_start(1)
    d_mid(2)
    input_rows(0)
    dh1_rows(half + 256)
    take(v2, vxr.at[1])
    d_end(2)
    y_start(2)
    input_rows(1)

    def sums(gp):
        take(yr.at[0:7, :, YCOLS[gp][0] : YCOLS[gp][1]], ysr.at[gp])
        tot = jnp.zeros((1, 1), f32)
        for d, wd, sr, sp in GPIECES:
            if not YCOLS[gp][0] <= d < YCOLS[gp][1]:
                continue
            for cc in range(2 if sp else 1):
                srcs = [2 * j + cc for j in range(4)] if sp else range(8)
                v = sum(yr[j, 0:6, d : d + wd].astype(f32) for j in srcs)
                pg_o[:, sr + sp * cc : sr + sp * cc + wd] = v
                tot = tot + jnp.sum(jnp.sum(v * v, axis=1, keepdims=True), axis=0, keepdims=True)
        return tot

    total = sums(0) + sums(1)
    total = total + sums(2)
    V = sum(yr[j, :, 1664:1792].astype(f32) for j in range(8))
    vs_o[...] = V[0:6, 0:13]
    total = total + jnp.sum(jnp.sum(V[0:6] * V[0:6], axis=1, keepdims=True), axis=0, keepdims=True)
    n2[pln] = jnp.broadcast_to(total, (8, 128))

    def nc2(k):
        return rcopy(n2.at[pln], n2.at[pln], ss.at[10], n2r.at[0], plane_peer(k))

    def nc1(k):
        return rcopy(n1.at[s], n1.at[s], ss.at[9], n1r.at[0], seq_peer(k)[1])

    for k in range(1, 16):
        nc2(k).start()
    take(n2.at[0:15], n2r.at[0])
    n1[s] = sum(n2[j] for j in range(16))
    for k in range(1, 8):
        nc1(k).start()
    sent(rcv.at[0:7], 0)
    sent(sg.at[0:7], 1)
    sent(xr.at[0:768], 2)
    sent(xr, 3)
    sent(w.at[0:720], 4)
    sent(g.at[0:720], 5)
    sent(w.at[0:720, 0:GC], 6)
    sent(rcv.at[0:7], 7)
    sent(vsrc.at[0:720], 8)
    sent(n2.at[0:15], 10)
    for wh in range(2):
        tok_wait(wh)
    ex(0, w.at[:, WOAT : WOAT + 384], wo.at[:, mine]).wait_send()
    for p in range(3):
        ex(1 + p, att_part(p), att_part(p)).wait_send()
    ex(4, outp.at[pl.ds(away, 512)], outo).wait_send()
    for i in range(2):
        dh1_ex(i).wait_send()
    take(n1.at[0:7], n1r.at[0])
    norm_o[...] = jnp.sqrt(sum(n1[j] for j in range(8)))[0:1, 0:1]
    sent(n1.at[0:7], 9)


def run_layer(par, vt, xin, dyin, sgin):
    V = pl.BlockSpec(memory_space=pltpu.VMEM)
    H = pl.BlockSpec(memory_space=pl.ANY)
    M = pltpu.VMEM
    DM = pltpu.SemaphoreType.DMA
    S = jax.ShapeDtypeStruct
    tok = (T, D)
    return pl.pallas_call(
        layer,
        out_shape=[S((4, 128, D), bf), S((4, 128, D), bf), S((6, 9344), f32), S((6, 13), f32), S((1, 1), f32)],
        in_specs=[V, V, H, H, V],
        out_specs=[H, H, V, V, V],
        scratch_shapes=[
            M((D, WC), bf), M((D, D), bf), M(tok, bf), M(tok, bf), M((8, 8, 128), f32), M((4, 8, 128), f32), M((2, 8, WC), bf), M((8, 8, WC), bf),
            M((16, D), f32), M(tok, bf), M((D, T), bf), M((T, 3 * HD), bf), M((6, T, 128), bf), M((6, T, 128), bf),
            M((T, HD), f32), M((6, 3, 128, 128), bf), M((T, 128), f32), M((4, 256, 256), bf), M((4, 256, 256), bf), M(tok, bf),
            M(tok, f32), M(tok, bf), M((D, T), bf), M((D, T), bf), M((T, FH), bf), M((T, FH), bf), M((512, D), bf),
            M(tok, bf), M((512, D), bf), M((D, 2 * FH), bf), M((576, 2 * FH), bf), M((144, 2 * FH), bf),
            M((4, 4, 48, GC), bf), M((3, 4, 48, GC), bf), M((3, 48, GC), bf), M((D, 128), bf),
            M((8, 8, WC), bf), M((8, 8, 128), f32), M((16, 8, 128), f32), M((16, D), f32), M((8, FH), f32),
            M((D, 128), f32), M((3, 192, 128), f32), M((3, 48, 128), f32),
            DM((11,)), DM((3,)), DM((1,)), DM((2,)), DM((2,)), DM((4, 10)), DM((2, 4, 2)), DM((2, 2)), DM((3,)), DM((3,)), DM((3,)), DM((2,)),
            DM((1,)), DM((1,)), DM((11,)), DM((11,)), DM((2, 8)), DM((2, 8)), DM((4,)),
        ],
        compiler_params=pltpu.CompilerParams(collective_id=0, has_side_effects=True, vmem_limit_bytes=64 * 2**20 - 2**17),
        name="layer",
    )(par, vt, xin, dyin, sgin)


def adamw(weight, grad, m, v, scale, rate, decay):
    grad = grad * scale
    m = 0.5 * m + 0.5 * grad
    v = 0.5 * v + 0.5 * grad * grad
    return grad, weight - rate * (m / (jnp.sqrt(v) + 1e-8) + decay * weight), m, v


def finish(out, ig, pg, norm, par, pm, pv, out_o, ig_o, *p_o):
    out_o[...] = out[...]
    ig_o[...] = ig[...].astype(f32)

    @pl.when(pl.program_id(0) == 0)
    def _():
        scale = 1.0 / jnp.maximum(norm[...], 1.0)
        for a in range(0, 9344, 1024):
            e = slice(a, min(a + 1024, 9344))
            for ref, val in zip(p_o, adamw(par[:, e], pg[:, e], pm[:, e], pv[:, e], scale, 0.05, 0.1)):
                ref[:, e] = val


def run_finish(out, ig, pg, norm, par, pm, pv):
    S = jax.ShapeDtypeStruct
    tok = pl.BlockSpec((2, 128, D), lambda i: (i, 0, 0))
    mat = pl.BlockSpec((6, 9344), lambda i: (0, 0))
    one = pl.BlockSpec((1, 1), lambda i: (0, 0))
    return pl.pallas_call(
        finish,
        grid=(2,),
        out_shape=[S((4, 128, D), bf), S((4, 128, D), f32)] + [S((6, 9344), f32)] * 4,
        in_specs=[tok, tok, mat, one, mat, mat, mat],
        out_specs=[tok, tok] + [mat] * 4,
        compiler_params=pltpu.CompilerParams(vmem_limit_bytes=62 * 2**20),
        name="finish",
    )(out, ig, pg, norm, par, pm, pv)


def body(inputs, segment_ids, out_grad, params, vectors, params_m, params_v, vectors_m, vectors_v):
    out, ig, pg, vs, norm = run_layer(params, vectors.T, inputs, out_grad, segment_ids)
    scale = 1.0 / jnp.maximum(norm[0, 0], 1.0)
    q = adamw(vectors.T, vs, vectors_m.T, vectors_v.T, scale, 0.2, 0.0)
    done = run_finish(out, ig, pg, norm, params, params_m, params_v)
    return (done[0], done[1], norm.reshape(1)) + tuple(done[2:]) + tuple(t.T for t in q)


def solution(mesh):
    torus = Mesh(mesh.devices.reshape(4, 4, 4, 2), ("x", "z", "y", "c"))
    row, seq, every = ("x", "z"), ("y", "c"), ("x", "z", "y", "c")
    tok, mat, vec = P(row, seq, None), P(every, None), P(None, every)
    return jax.shard_map(
        body,
        mesh=torus,
        in_specs=(tok, P(row, seq), tok, mat, vec, mat, mat, vec, vec),
        out_specs=(tok, tok, P(), mat, mat, mat, mat, vec, vec, vec, vec),
        check_vma=False,
    )
```
